256 devices in a mesh: batch: 16 (over z, core), proto: 16 (over x, y).
Axes of the slice: x: 4, y: 4, z: 8, core: 2. Of those that a mesh axis runs over, the one named last changes fastest.
Arguments:
- slow_embed: bfloat16 [16384, 256], P('batch'), may hold values from -1 to 1
- fast_embed: bfloat16 [16384, 256], P('batch'), may hold values from -1 to 1
- prototypes: float32 [32768, 256], P('proto'), may hold values from -1 to 1
Outputs:
- proto_grad: float32 [32768, 256], P('proto')
- slow_grad: float32 [16384, 256], P('batch')
- fast_grad: float32 [16384, 256], P('batch')
The draws below stay inside these ranges and needn't reach their ends.
All inputs are finite; a program needn't handle non-finite values.
Results may differ from the reference program's by a relative error of at most 0.0005.
The reference program's roundings to bfloat16 on the way count: a program that leaves them out, or rounds other values in their place, can miss the bound.
Values sent between devices are 32-bit elements; how exact they have to be, the bound alone decides.
A program may use at most 128 MiB of HBM per device.

```python
import jax
import jax.numpy as jnp
from jax import lax

D = 256
PROTO_DEV = 2048
ITERS = 3
CLIPS = 16384
PROTOS = 32768


def row_scales(scale_key, count):
    position = jnp.arange(count, dtype=jnp.float32)[:, None] / count
    jitter = jax.random.uniform(scale_key, (count, 1), jnp.float32, 0.0, jnp.log(4.0))
    return jnp.exp(jnp.log(3.0) * position + jitter)


def view_draw(key, salt):
    common_key = jax.random.fold_in(key, 21)
    own_key = jax.random.fold_in(key, salt)
    first_key, second_key = jax.random.split(own_key, 2)
    scaling = row_scales(second_key, CLIPS)
    shared_part = jnp.clip(jax.random.normal(common_key, (CLIPS, D), jnp.float32), -5.0, 5.0)
    own_part = jnp.clip(jax.random.normal(first_key, (CLIPS, D), jnp.float32), -5.0, 5.0)
    mixed = 0.7 * shared_part + 0.7 * own_part
    return jnp.clip(0.01 * mixed * scaling, -1.0, 1.0).astype(jnp.bfloat16)


def draw_slow_embed(key, part):
    return view_draw(key, 31)


def draw_fast_embed(key, part):
    return view_draw(key, 41)


def draw_prototypes(key, part):
    own_key = jax.random.fold_in(key, 51)
    first_key, second_key = jax.random.split(own_key, 2)
    scaling = row_scales(second_key, PROTOS)
    mixed = jnp.clip(jax.random.normal(first_key, (PROTOS, D), jnp.float32), -5.0, 5.0)
    return jnp.clip(0.01 * mixed * scaling, -1.0, 1.0).astype(jnp.float32)


def setup_inputs(seed: int = 0) -> dict:
    splits = jax.random.split(jax.random.key(seed), 4)
    return {
        "slow_embed": draw_slow_embed(jax.random.fold_in(splits[3], 71), 0),
        "fast_embed": draw_fast_embed(jax.random.fold_in(splits[3], 71), 0),
        "prototypes": draw_prototypes(jax.random.fold_in(splits[3], 71), 0),
    }


CODE_EPS = 0.05
TEMPER = 0.1
NORM_EPS = 1e-06
HIGH = lax.Precision.HIGHEST

def normalize(raw_rows):
    lengths = jnp.sqrt(lax.optimization_barrier(jnp.sum(raw_rows * raw_rows, axis=-1, keepdims=True)) + 1e-12)
    return (raw_rows / lengths, lengths)

def project_back(grad_unit, unit_vec, lengths):
    along = lax.optimization_barrier(jnp.sum(unit_vec * grad_unit, axis=-1, keepdims=True))
    return (grad_unit - unit_vec * along) / lengths

def reference(slow_embed, fast_embed, prototypes):
    raw_views = jnp.stack([slow_embed, fast_embed]).astype(jnp.float32)
    unit_vec, lengths = normalize(raw_views)
    unit_b = lax.optimization_barrier(unit_vec.astype(jnp.bfloat16)).astype(jnp.float32)
    proto_unit, proto_len = normalize(prototypes.astype(jnp.float32))
    proto_b = lax.optimization_barrier(proto_unit.astype(jnp.bfloat16)).astype(jnp.float32)
    blocks = proto_b.reshape(PROTOS // PROTO_DEV, PROTO_DEV, D)

    def score_of(block):
        return jnp.einsum('vbd,kd->vbk', unit_b, block, precision=HIGH)

    def sweep_all(clip_scale, with_denom):

        def advance(running, block):
            clip_total, denominator = running
            score_blk = score_of(block)
            code_table = jnp.exp(score_blk / CODE_EPS)
            col_total = lax.optimization_barrier(jnp.sum(code_table * clip_scale[:, :, None], axis=1))
            proto_scale = 1.0 / (PROTOS * col_total)
            clip_total = clip_total + lax.optimization_barrier(jnp.sum(code_table * proto_scale[:, None, :], axis=2))
            if with_denom:
                denominator = denominator + lax.optimization_barrier(jnp.sum(jnp.exp(score_blk / TEMPER), axis=2))
            return ((clip_total, denominator), proto_scale)
        initial = (jnp.zeros((2, CLIPS), jnp.float32), jnp.zeros((2, CLIPS), jnp.float32))
        (clip_total, denominator), scales = lax.scan(advance, initial, blocks)
        return (clip_total, denominator, scales)
    clip_scale = jnp.ones((2, CLIPS), jnp.float32)
    denominator = jnp.zeros((2, CLIPS), jnp.float32)
    for iteration in range(ITERS):
        clip_total, denom_now, scales = sweep_all(clip_scale, iteration == 0)
        if iteration == 0:
            denominator = denom_now
        clip_scale = 1.0 / (CLIPS * clip_total)

    def grad_step(accum_grad, inputs):
        block, proto_scale = inputs
        score_blk = score_of(block)
        codes = jnp.exp(score_blk / CODE_EPS) * proto_scale[:, None, :] / clip_total[:, :, None]
        probs = jnp.exp(score_blk / TEMPER) / denominator[:, :, None]
        score_grad = jnp.stack([probs[0] - codes[1], probs[1] - codes[0]]) / TEMPER
        grad_b = lax.optimization_barrier(score_grad.astype(jnp.bfloat16)).astype(jnp.float32)
        accum_grad = accum_grad + jnp.einsum('vbk,kd->vbd', grad_b, block, precision=HIGH)
        proto_blk = jnp.einsum('vbk,vbd->kd', grad_b, unit_b, precision=HIGH)
        return (accum_grad, proto_blk)
    grad_unit, proto_blocks = lax.scan(grad_step, jnp.zeros((2, CLIPS, D), jnp.float32), (blocks, scales))
    grad_proto_unit = proto_blocks.reshape(PROTOS, D)
    grad_embed = project_back(grad_unit, unit_vec, lengths)
    grad_proto = project_back(grad_proto_unit, proto_unit, proto_len)
    proto_grad = grad_proto / jnp.sqrt(jnp.mean(grad_proto * grad_proto) + NORM_EPS)
    embed_factor = 1.0 / jnp.sqrt(jnp.mean(grad_embed * grad_embed) + NORM_EPS)
    return (proto_grad, grad_embed[0] * embed_factor, grad_embed[1] * embed_factor)
```

```python
import functools

import jax
import jax.numpy as jnp
from jax import lax
from jax.experimental import pallas as pl
from jax.experimental.pallas import tpu as pltpu
from jax.sharding import PartitionSpec as P

ITERS = 3
NORM_EPS = 1e-06
MESH = pl.DeviceIdType.MESH
F32 = jnp.float32
BF16 = jnp.bfloat16


def normalized(rows):
    total = jnp.sum(rows * rows, axis=-1, keepdims=True) + 1e-12
    inverse = 1.0 / jnp.sqrt(total)
    return rows * inverse, inverse


def fold8(block):
    rows, lanes = block.shape
    return jnp.sum(block.reshape(rows // 8, 8, lanes), axis=0)


def kernel(
    dims,
    slow_ref, fast_ref, proto_ref,
    dw_ref, dx_ref, sum_ref,
    table, grads, unit_b, unit_t, proto_b, partial, clip_b, soft_b, code_b,
    du, dct, dc_pair, dc_half, du_recv, dc_recv,
    col_z, col_pair, row_recv, den_recv, sq_p, sq_z, sq_pair, own_dx, own_dw,
    send_sem, pair_send, col_sem, colp_sem, row_sem, den_sem, den_send,
    du_sem, dcp_sem, dc_sem, sqp_sem, sqz_sem, sqr_sem, agx_sem, agw_sem, agwp_sem,
    du_send, dc_send, agx_send, agw_send, agwp_send, local_sem,
):
    clips, protos, width, n_z, n_p = dims
    batch_me = lax.axis_index("batch")
    me_p = lax.axis_index("proto")
    me_z = batch_me // 2
    core = batch_me % 2
    clips_all = clips * 2 * n_z
    protos_all = protos * n_p
    rows = 2 * clips
    lane_chunks = protos // 128
    row_blocks = rows // 128
    view_blocks = clips // 128
    embeds = (slow_ref, fast_ref)

    def p_id(d):
        return {"proto": (me_p + d) % n_p}

    def z_id(d):
        return {"batch": ((me_z + d) % n_z) * 2 + core}

    partner = {"batch": me_z * 2 + 1 - core}

    def remote(src, dst, send, recv, device):
        return pltpu.make_async_remote_copy(
            src_ref=src, dst_ref=dst, send_sem=send, recv_sem=recv,
            device_id=device, device_id_type=MESH,
        )

    barrier = pltpu.get_barrier_semaphore()
    for d in range(1, n_p):
        pl.semaphore_signal(barrier, inc=1, device_id=p_id(d), device_id_type=MESH)
    for d in range(1, n_z):
        pl.semaphore_signal(barrier, inc=1, device_id=z_id(d), device_id_type=MESH)
    pl.semaphore_signal(barrier, inc=1, device_id=partner, device_id_type=MESH)

    def proto_norm(i, carry):
        at = pl.ds(pl.multiple_of(i * 128, 128), 128)
        unit, _ = normalized(proto_ref[at, :])
        proto_b[at, :] = unit.astype(BF16)
        return carry

    lax.fori_loop(0, protos // 128, proto_norm, 0)

    def chunk(c):
        return slice(c * 128, (c + 1) * 128)

    step_w = 512
    for v in range(2):
        def first(i, cols):
            at = pl.ds(pl.multiple_of(i * 128, 128), 128)
            glob = pl.ds(pl.multiple_of(v * clips + i * 128, 128), 128)
            unit, _ = normalized(embeds[v][at, :].astype(F32))
            ub = unit.astype(BF16)
            unit_b[glob, :] = ub
            den = jnp.zeros((128, 128), F32)
            cols = list(cols)
            for k in range(protos // step_w):
                score = lax.dot_general(
                    ub, proto_b[k * step_w:(k + 1) * step_w, :],
                    (((1,), (1,)), ((), ())), preferred_element_type=F32)
                soft = jnp.exp(score * 10.0)
                table[glob, k * step_w:(k + 1) * step_w] = soft
                for j in range(step_w // 128):
                    t = soft[:, chunk(j)]
                    den = den + t
                    c = k * (step_w // 128) + j
                    cols[c] = cols[c] + fold8(t * t)
            partial[glob, :] = den
            return tuple(cols)

        cols = lax.fori_loop(
            0, view_blocks, first,
            tuple(jnp.zeros((8, 128), F32) for _ in range(lane_chunks)))
        for c in range(lane_chunks):
            col_z[0, me_z, v * lane_chunks + c:v * lane_chunks + c + 1, :] = jnp.sum(
                cols[c], axis=0, keepdims=True)

    pl.semaphore_wait(barrier, n_p - 1 + n_z - 1 + 1)

    ones = jnp.ones((8, 128), F32)

    def dense_rows(store):
        for v in range(2):
            total = lax.dot_general(
                ones, partial[v * clips:(v + 1) * clips, :], (((1,), (1,)), ((), ())),
                precision=lax.Precision.HIGHEST, preferred_element_type=F32)
            for i in range(view_blocks):
                store(v * view_blocks + i, total[0:1, chunk(i)])

    def spread(values, target):
        for i in range(row_blocks):
            target[chunk(i), :] = jnp.broadcast_to(values[i:i + 1, :], (128, 128)).T

    def start_all(ref, me, count, ids, send, recv):
        copies = []
        for d in range(1, count):
            copy = remote(ref.at[me], ref.at[me], send.at[d], recv.at[d], ids(d))
            copy.start()
            copies.append(copy)
        return copies

    def total_of(ref, count):
        acc = ref[0]
        for i in range(1, count):
            acc = acc + ref[i]
        return acc

    def col_total(it):
        buf = col_z.at[it]
        for copy in start_all(buf, me_z, n_z, z_id, send_sem, col_sem.at[it]):
            copy.wait()
        pair = col_pair.at[it]
        pair[core] = total_of(buf, n_z)
        copy = remote(pair.at[core], pair.at[core], pair_send, colp_sem.at[it], partner)
        copy.start()
        copy.wait()
        return pair[0] + pair[1]

    def row_total(it):
        buf = row_recv.at[it]

        def put(i, value):
            buf[me_p, i:i + 1, :] = value

        dense_rows(put)
        for copy in start_all(buf, me_p, n_p, p_id, send_sem, row_sem.at[it]):
            copy.wait()
        return total_of(buf, n_p)

    def put_den(i, value):
        den_recv[me_p, i:i + 1, :] = value

    dense_rows(put_den)
    den_copies = start_all(den_recv, me_p, n_p, p_id, den_send, den_sem)

    scale = None
    for it in range(ITERS):
        if it > 0:
            for v in range(2):
                def cols_pass(i, cols):
                    at = pl.ds(pl.multiple_of(v * clips + i * 64, 64), 64)
                    s = clip_b[at, :]
                    out = []
                    for c in range(lane_chunks):
                        t = table[at, chunk(c)]
                        out.append(cols[c] + fold8(t * t * s))
                    return tuple(out)

                cols = lax.fori_loop(
                    0, clips // 64, cols_pass,
                    tuple(jnp.zeros((8, 128), F32) for _ in range(lane_chunks)))
                for c in range(lane_chunks):
                    col_z[it, me_z, v * lane_chunks + c:v * lane_chunks + c + 1, :] = jnp.sum(
                        cols[c], axis=0, keepdims=True)
        scale = 1.0 / (protos_all * col_total(it))
        for v in range(2):
            def rows_pass(i, carry):
                at = pl.ds(pl.multiple_of(v * clips + i * 64, 64), 64)
                acc = jnp.zeros((64, 128), F32)
                for c in range(lane_chunks):
                    t = table[at, chunk(c)]
                    r = scale[v * lane_chunks + c:v * lane_chunks + c + 1, :]
                    acc = acc + t * t * r
                partial[at, :] = acc
                return carry

            lax.fori_loop(0, clips // 64, rows_pass, 0)
        row_sum = row_total(it)
        if it < ITERS - 1:
            spread(1.0 / (clips_all * row_sum), clip_b)
    for copy in den_copies:
        copy.wait()
    spread(10.0 / total_of(den_recv, n_p), soft_b)
    spread(10.0 / row_sum, code_b)

    for v in range(2):
        w = 1 - v

        def grad_pass(i, carry):
            mine = pl.ds(pl.multiple_of(v * clips + i * 64, 64), 64)
            other = pl.ds(pl.multiple_of(w * clips + i * 64, 64), 64)
            soft_scale = soft_b[mine, :]
            code_scale = code_b[other, :]
            for c in range(lane_chunks):
                r = scale[w * lane_chunks + c:w * lane_chunks + c + 1, :]
                t = table[other, chunk(c)]
                g = table[mine, chunk(c)] * soft_scale - t * t * r * code_scale
                grads[mine, chunk(c)] = g.astype(BF16)
            return carry

        lax.fori_loop(0, clips // 64, grad_pass, 0)

    def transpose_unit(i, carry):
        at = pl.ds(pl.multiple_of(i * 128, 128), 128)
        unit_t[:, at] = unit_b[at, :].astype(F32).T.astype(BF16)
        return carry

    lax.fori_loop(0, row_blocks, transpose_unit, 0)

    def dc_dot(i, carry):
        at = pl.ds(pl.multiple_of(i * 256, 256), 256)
        out = jnp.dot(unit_t[...], grads[:, at], preferred_element_type=F32)
        dct[2 * i] = out[:, :128]
        dct[2 * i + 1] = out[:, 128:]
        return carry

    lax.fori_loop(0, protos // 256, dc_dot, 0)
    half = pl.ds((1 - core) * n_z, n_z)
    pair_copy = remote(dct.at[half], dc_pair, pair_send, dcp_sem, partner)
    pair_copy.start()

    def du_dot(i, carry):
        at = pl.ds(pl.multiple_of(i * 256, 256), 256)
        out = jnp.dot(grads[at, :], proto_b[...], preferred_element_type=F32)
        du[2 * i] = out[:128, :]
        du[2 * i + 1] = out[128:, :]
        return carry

    lax.fori_loop(0, rows // 256, du_dot, 0)
    du_copies = []
    for d in range(1, n_p):
        copy = remote(du.at[(me_p + d) % n_p], du_recv.at[me_p], du_send.at[d], du_sem.at[d], p_id(d))
        copy.start()
        du_copies.append(copy)

    pair_copy.wait()
    for i in range(n_z):
        dc_half[i] = dct[core * n_z + i] + dc_pair[i]
    dc_copies = []
    for d in range(1, n_z):
        copy = remote(dc_half.at[(me_z + d) % n_z], dc_recv.at[me_z], dc_send.at[d], dc_sem.at[d], z_id(d))
        copy.start()
        dc_copies.append(copy)

    def project(grad, raw):
        unit, inverse = normalized(raw)
        along = jnp.sum(unit * grad, axis=-1, keepdims=True)
        return (grad - unit * along) * inverse

    def lanes_square(block):
        sq = block * block
        return jnp.sum(sq[:, :128] + sq[:, 128:], axis=0, keepdims=True)

    du_recv[me_p] = du[me_p]
    for copy in du_copies:
        copy.wait()
    total = total_of(du_recv, n_p)
    at = pl.ds(pl.multiple_of((me_p % view_blocks) * 128, 128), 128)
    is_slow = me_p < view_blocks
    raw = jnp.where(is_slow, slow_ref[at, :].astype(F32), fast_ref[at, :].astype(F32))
    dx_own = project(total, raw)
    own_dx[...] = dx_own
    agx = []
    spot = dx_ref.at[pl.ds(pl.multiple_of(me_p * 128, 128), 128), :]
    for d in range(1, n_p):
        copy = remote(own_dx, spot, agx_send.at[d], agx_sem.at[d], p_id(d))
        copy.start()
        agx.append(copy)
    local_x = pltpu.make_async_copy(own_dx, spot, local_sem.at[0])
    local_x.start()

    dc_recv[me_z] = dc_half[me_z]
    for copy in dc_copies:
        copy.wait()
    total = total_of(dc_recv, n_z).T
    at = pl.ds(pl.multiple_of((core * n_z + me_z) * 128, 128), 128)
    dw_own = project(total, proto_ref[at, :])
    own_dw[...] = dw_own
    agw = []
    spot_w = dw_ref.at[at, :]
    for d in range(1, n_z):
        copy = remote(own_dw, spot_w, agw_send.at[d], agw_sem.at[d], z_id(d))
        copy.start()
        agw.append(copy)
    local_w = pltpu.make_async_copy(own_dw, spot_w, local_sem.at[1])
    local_w.start()

    sq_p[me_p, 0:1, :] = lanes_square(dw_own)
    sq_p[me_p, 1:2, :] = lanes_square(dx_own)
    sq_p[me_p, 2:8, :] = jnp.zeros((6, 128), F32)
    for copy in start_all(sq_p, me_p, n_p, p_id, send_sem, sqp_sem):
        copy.wait()
    sq_z[me_z] = total_of(sq_p, n_p)
    for copy in start_all(sq_z, me_z, n_z, z_id, send_sem, sqz_sem):
        copy.wait()
    sq_pair[core] = total_of(sq_z, n_z)
    copy = remote(sq_pair.at[core], sq_pair.at[core], pair_send, sqr_sem, partner)
    copy.start()
    copy.wait()
    sum_ref[...] = sq_pair[0] + sq_pair[1]

    for copy in agw:
        copy.wait()
    local_w.wait()
    half_rows = pl.ds(pl.multiple_of(core * n_z * 128, 128), n_z * 128)
    copy = remote(dw_ref.at[half_rows, :], dw_ref.at[half_rows, :], agwp_send, agwp_sem, partner)
    copy.start()
    copy.wait()
    local_x.wait()
    for copy in agx:
        copy.wait()


def body(slow_embed, fast_embed, prototypes):
    clips, width = slow_embed.shape
    protos = prototypes.shape[0]
    n_b = lax.axis_size("batch")
    n_p = lax.axis_size("proto")
    n_z = n_b // 2
    rows = 2 * clips
    DMA = pltpu.SemaphoreType.DMA
    vmem = pltpu.VMEM
    lane_chunks = protos // 128
    row_blocks = rows // 128
    scratch = [
        vmem((rows, protos), F32),
        vmem((rows, protos), BF16),
        vmem((rows, width), BF16),
        vmem((width, rows), BF16),
        vmem((protos, width), BF16),
        vmem((rows, 128), F32),
        vmem((rows, 128), F32),
        vmem((rows, 128), F32),
        vmem((rows, 128), F32),
        vmem((n_p, rows // n_p, width), F32),
        vmem((lane_chunks, width, 128), F32),
        vmem((n_z, width, 128), F32),
        vmem((n_z, width, 128), F32),
        vmem((n_p, rows // n_p, width), F32),
        vmem((n_z, width, 128), F32),
        vmem((ITERS, n_z, 2 * lane_chunks, 128), F32),
        vmem((ITERS, 2, 2 * lane_chunks, 128), F32),
        vmem((ITERS, n_p, row_blocks, 128), F32),
        vmem((n_p, row_blocks, 128), F32),
        vmem((n_p, 8, 128), F32),
        vmem((n_z, 8, 128), F32),
        vmem((2, 8, 128), F32),
        vmem((rows // n_p, width), F32),
        vmem((128, width), F32),
        DMA((16,)), DMA(()), DMA((ITERS, n_z)), DMA((ITERS,)), DMA((ITERS, n_p)),
        DMA((n_p,)), DMA((n_p,)),
        DMA((n_p,)), DMA(()), DMA((n_z,)), DMA((n_p,)), DMA((n_z,)), DMA(()),
        DMA((n_p,)), DMA((n_z,)), DMA(()),
        DMA((n_p,)), DMA((n_z,)), DMA((n_p,)), DMA((n_z,)), DMA(()), DMA((2,)),
    ]
    whole = pl.BlockSpec(memory_space=pltpu.VMEM)
    anywhere = pl.BlockSpec(memory_space=pl.ANY)
    dw, dx, sums = pl.pallas_call(
        functools.partial(kernel, (clips, protos, width, n_z, n_p)),
        out_shape=(
            jax.ShapeDtypeStruct((protos, width), F32),
            jax.ShapeDtypeStruct((rows, width), F32),
            jax.ShapeDtypeStruct((8, 128), F32),
        ),
        in_specs=[whole] * 3,
        out_specs=(anywhere, anywhere, whole),
        scratch_shapes=scratch,
        compiler_params=pltpu.CompilerParams(
            collective_id=0, has_side_effects=True, vmem_limit_bytes=60 * 2**20),
        name="swav",
    )(slow_embed, fast_embed, prototypes)
    totals = jnp.sum(sums, axis=1)
    proto_entries = float(protos * n_p * width)
    embed_entries = float(2 * clips * n_b * width)
    proto_factor = lax.rsqrt(totals[0] / proto_entries + NORM_EPS)
    embed_factor = lax.rsqrt(totals[1] / embed_entries + NORM_EPS)
    return (dw * proto_factor, dx[:clips] * embed_factor, dx[clips:] * embed_factor)


def solution(mesh):
    placed = (P("batch", None), P("batch", None), P("proto", None))
    return jax.shard_map(
        body,
        mesh=mesh,
        in_specs=placed,
        out_specs=(P("proto", None), P("batch", None), P("batch", None)),
        check_vma=False,
    )
```

```python
import functools

import jax
import jax.numpy as jnp
from jax import lax
from jax.experimental import pallas as pl
from jax.experimental.pallas import tpu as pltpu
from jax.sharding import PartitionSpec as P

ITERS = 3
COPIES = 128
NORM_EPS = 1e-06
MESH = pl.DeviceIdType.MESH
F32 = jnp.float32
BF16 = jnp.bfloat16


def normalized(rows):
    total = jnp.sum(rows * rows, axis=-1, keepdims=True) + 1e-12
    inverse = 1.0 / jnp.sqrt(total)
    return rows * inverse, inverse


def fold8(block):
    rows, lanes = block.shape
    return jnp.sum(block.reshape(rows // 8, 8, lanes), axis=0)


def kernel(
    dims,
    slow_ref, fast_ref, proto_ref,
    dw_ref, dx_ref, wf_ref, xf_ref,
    table, grads, unit_b, unit_t, proto_b, partial, clip_b, soft_b, code_b,
    du, dct, dc_pair, dc_half, rs_buf, rs_small, z_buf, agx, agw,
    col_z, col_pair, row_recv, den_recv, sq_p, sq_z, sq_pair,
    send_sem, pair_send, col_sem, colp_sem, row_sem, den_sem, den_send,
    sqp_sem, sqz_sem, out_sem, in_sem, local_sem,
):
    clips, protos, width, n_z, n_p = dims
    batch_me = lax.axis_index("batch")
    me_p = lax.axis_index("proto")
    me_z = batch_me // 2
    core = batch_me % 2
    clips_all = clips * 2 * n_z
    protos_all = protos * n_p
    rows = 2 * clips
    lane_chunks = protos // 128
    row_blocks = rows // 128
    view_blocks = clips // 128
    embeds = (slow_ref, fast_ref)

    def p_id(d):
        return {"proto": (me_p + d) % n_p}

    def z_id(d):
        return {"batch": ((me_z + d) % n_z) * 2 + core}

    partner = {"batch": me_z * 2 + 1 - core}

    def remote(src, dst, send, recv, device):
        return pltpu.make_async_remote_copy(
            src_ref=src, dst_ref=dst, send_sem=send, recv_sem=recv,
            device_id=device, device_id_type=MESH,
        )

    barrier = pltpu.get_barrier_semaphore()
    for d in range(1, n_p):
        pl.semaphore_signal(barrier, inc=1, device_id=p_id(d), device_id_type=MESH)
    for d in range(1, n_z):
        pl.semaphore_signal(barrier, inc=1, device_id=z_id(d), device_id_type=MESH)
    pl.semaphore_signal(barrier, inc=1, device_id=partner, device_id_type=MESH)

    def proto_norm(i, carry):
        at = pl.ds(pl.multiple_of(i * 128, 128), 128)
        unit, _ = normalized(proto_ref[at, :])
        proto_b[at, :] = unit.astype(BF16)
        return carry

    lax.fori_loop(0, protos // 128, proto_norm, 0)

    def chunk(c):
        return slice(c * 128, (c + 1) * 128)

    step_w = 512
    for v in range(2):
        def first(i, cols):
            at = pl.ds(pl.multiple_of(i * 128, 128), 128)
            glob = pl.ds(pl.multiple_of(v * clips + i * 128, 128), 128)
            unit, _ = normalized(embeds[v][at, :].astype(F32))
            ub = unit.astype(BF16)
            unit_b[glob, :] = ub
            den = jnp.zeros((128, 128), F32)
            cols = list(cols)
            for k in range(protos // step_w):
                score = lax.dot_general(
                    ub, proto_b[k * step_w:(k + 1) * step_w, :],
                    (((1,), (1,)), ((), ())), preferred_element_type=F32)
                soft = jnp.exp(score * 10.0)
                table[glob, k * step_w:(k + 1) * step_w] = soft
                for j in range(step_w // 128):
                    t = soft[:, chunk(j)]
                    den = den + t
                    c = k * (step_w // 128) + j
                    cols[c] = cols[c] + fold8(t * t)
            partial[glob, :] = den
            return tuple(cols)

        cols = lax.fori_loop(
            0, view_blocks, first,
            tuple(jnp.zeros((8, 128), F32) for _ in range(lane_chunks)))
        for c in range(lane_chunks):
            col_z[0, me_z, v * lane_chunks + c:v * lane_chunks + c + 1, :] = jnp.sum(
                cols[c], axis=0, keepdims=True)

    pl.semaphore_wait(barrier, n_p - 1 + n_z - 1 + 1)

    ones = jnp.ones((8, 128), F32)

    def dense_rows(store):
        for v in range(2):
            total = lax.dot_general(
                ones, partial[v * clips:(v + 1) * clips, :], (((1,), (1,)), ((), ())),
                precision=lax.Precision.HIGHEST, preferred_element_type=F32)
            for i in range(view_blocks):
                store(v * view_blocks + i, total[0:1, chunk(i)])

    def spread(values, target):
        for i in range(row_blocks):
            target[chunk(i), :] = jnp.broadcast_to(values[i:i + 1, :], (128, 128)).T

    def start_all(ref, me, count, ids, send, recv):
        copies = []
        for d in range(1, count):
            copy = remote(ref.at[me], ref.at[me], send.at[d], recv.at[d], ids(d))
            copy.start()
            copies.append(copy)
        return copies

    def total_of(ref, count):
        acc = ref[0]
        for i in range(1, count):
            acc = acc + ref[i]
        return acc

    def col_total(it):
        buf = col_z.at[it]
        for copy in start_all(buf, me_z, n_z, z_id, send_sem, col_sem.at[it]):
            copy.wait()
        pair = col_pair.at[it]
        pair[core] = total_of(buf, n_z)
        copy = remote(pair.at[core], pair.at[core], pair_send, colp_sem.at[it], partner)
        copy.start()
        copy.wait()
        return pair[0] + pair[1]

    def row_total(it):
        buf = row_recv.at[it]

        def put(i, value):
            buf[me_p, i:i + 1, :] = value

        dense_rows(put)
        for copy in start_all(buf, me_p, n_p, p_id, send_sem, row_sem.at[it]):
            copy.wait()
        return total_of(buf, n_p)

    def put_den(i, value):
        den_recv[me_p, i:i + 1, :] = value

    dense_rows(put_den)
    den_copies = start_all(den_recv, me_p, n_p, p_id, den_send, den_sem)

    scale = None
    for it in range(ITERS):
        if it > 0:
            for v in range(2):
                def cols_pass(i, cols):
                    at = pl.ds(pl.multiple_of(v * clips + i * 64, 64), 64)
                    s = clip_b[at, :]
                    out = []
                    for c in range(lane_chunks):
                        t = table[at, chunk(c)]
                        out.append(cols[c] + fold8(t * t * s))
                    return tuple(out)

                cols = lax.fori_loop(
                    0, clips // 64, cols_pass,
                    tuple(jnp.zeros((8, 128), F32) for _ in range(lane_chunks)))
                for c in range(lane_chunks):
                    col_z[it, me_z, v * lane_chunks + c:v * lane_chunks + c + 1, :] = jnp.sum(
                        cols[c], axis=0, keepdims=True)
        scale = 1.0 / (protos_all * col_total(it))
        for v in range(2):
            def rows_pass(i, carry):
                at = pl.ds(pl.multiple_of(v * clips + i * 64, 64), 64)
                acc = jnp.zeros((64, 128), F32)
                for c in range(lane_chunks):
                    t = table[at, chunk(c)]
                    r = scale[v * lane_chunks + c:v * lane_chunks + c + 1, :]
                    acc = acc + t * t * r
                partial[at, :] = acc
                return carry

            lax.fori_loop(0, clips // 64, rows_pass, 0)
        row_sum = row_total(it)
        if it < ITERS - 1:
            spread(1.0 / (clips_all * row_sum), clip_b)
    for copy in den_copies:
        copy.wait()
    spread(10.0 / total_of(den_recv, n_p), soft_b)
    spread(10.0 / row_sum, code_b)

    for v in range(2):
        w = 1 - v

        def grad_pass(i, carry):
            mine = pl.ds(pl.multiple_of(v * clips + i * 64, 64), 64)
            other = pl.ds(pl.multiple_of(w * clips + i * 64, 64), 64)
            soft_scale = soft_b[mine, :]
            code_scale = code_b[other, :]
            for c in range(lane_chunks):
                r = scale[w * lane_chunks + c:w * lane_chunks + c + 1, :]
                t = table[other, chunk(c)]
                g = table[mine, chunk(c)] * soft_scale - t * t * r * code_scale
                grads[mine, chunk(c)] = g.astype(BF16)
            return carry

        lax.fori_loop(0, clips // 64, grad_pass, 0)

    def transpose_unit(i, carry):
        at = pl.ds(pl.multiple_of(i * 128, 128), 128)
        unit_t[:, at] = unit_b[at, :].astype(F32).T.astype(BF16)
        return carry

    lax.fori_loop(0, row_blocks, transpose_unit, 0)

    pending = []
    counter = [0]

    def send(src, dst, device):
        n = counter[0]
        counter[0] += 1
        copy = remote(src, dst, out_sem.at[n], in_sem.at[n], device)
        copy.start()
        pending.append(copy)
        return copy

    def add_to(ref, value):
        ref[...] = ref[...] + value

    x, y = me_p // 4, me_p % 4
    x_next = {"proto": (x + 1) % 4 * 4 + y}
    x_prev = {"proto": (x + 3) % 4 * 4 + y}
    y_next = {"proto": x * 4 + (y + 1) % 4}
    y_prev = {"proto": x * 4 + (y + 3) % 4}
    z_next, z_prev = z_id(1), z_id(n_z - 1)

    class Scatter4:
        def __init__(self, view, me, ahead, behind, buf):
            self.view, self.me, self.ahead, self.behind, self.buf = view, me, ahead, behind, buf
            self.c = {}

        def send(self, slot, dest, part):
            device = self.ahead if slot < 3 else self.behind
            self.c[slot] = send(self.view(dest, part), self.buf.at[slot], device)

        def start(self):
            m = self.me
            self.send(0, (m + 2) % 4, 0)
            self.send(3, (m + 2) % 4, 1)
            self.send(1, (m + 1) % 4, 1)
            self.send(4, (m + 3) % 4, 0)

        def mid(self):
            m = self.me
            self.c[0].wait_recv()
            add_to(self.view((m + 1) % 4, 0), self.buf[0])
            self.send(2, (m + 1) % 4, 0)
            self.c[3].wait_recv()
            add_to(self.view((m + 3) % 4, 1), self.buf[3])
            self.send(5, (m + 3) % 4, 1)

        def finish(self):
            for slot in (1, 4, 2, 5):
                self.c[slot].wait_recv()
            add_to(self.view(self.me, 0), self.buf[2] + self.buf[4])
            add_to(self.view(self.me, 1), self.buf[1] + self.buf[5])

    class Gather4:
        def __init__(self, view, me, ahead, behind):
            self.view, self.me, self.ahead, self.behind = view, me, ahead, behind
            self.c = {}

        def send(self, slot, owner, part):
            spot = self.view(owner, part)
            self.c[slot] = send(spot, spot, self.ahead if slot < 3 else self.behind)

        def start(self):
            self.send(0, self.me, 0)
            self.send(3, self.me, 1)
            self.send(1, self.me, 1)
            self.send(4, self.me, 0)

        def mid(self):
            self.c[0].wait_recv()
            self.send(2, (self.me + 3) % 4, 0)
            self.c[3].wait_recv()
            self.send(5, (self.me + 1) % 4, 1)

        def finish(self):
            for slot in (1, 4, 2, 5):
                self.c[slot].wait_recv()

    def quarter(half, part):
        return pl.ds(half * 64 + part * 32, 32)

    def along_x(ref, half):
        return lambda at, part: ref.at[at, :, quarter(half, part), :]

    def along_y(ref, half):
        return lambda at, part: ref.at[:, at, quarter(half, part), :]

    def in_x(ref, half):
        return lambda at, part: ref.at[at, y, quarter(half, part), :]

    def in_y(ref, half):
        return lambda at, part: ref.at[x, at, quarter(half, part), :]

    hops = (4, 3, 3, 2, 2, 1, 1)

    class ScatterZ:
        def __init__(self):
            self.c = {}

        def view(self, dest, part):
            return dc_half.at[dest, pl.ds(part * 128, 128), :]

        def step(self, i):
            part = i % 2
            for way in (0, 1):
                dest = (me_z + (hops[i] if way == 0 else n_z - hops[i])) % n_z
                spot = self.view(dest, part ^ way)
                if i >= 2:
                    self.c[way, i - 2].wait_recv()
                    add_to(spot, z_buf[way, i - 2])
                self.c[way, i] = send(spot, z_buf.at[way, i], z_prev if way else z_next)

        def finish(self):
            for way in (0, 1):
                for i in (5, 6):
                    self.c[way, i].wait_recv()
                    add_to(self.view(me_z, i % 2 ^ way), z_buf[way, i])

    class GatherZ:
        def __init__(self):
            self.c = {}
            self.p = []

        def view(self, owner, part):
            return agw.at[core * n_z + owner, pl.ds(part * 64, 64), :]

        def came(self, way, i):
            far = i // 2 + 1
            owner = (me_z + (far if way else n_z - far)) % n_z
            return self.view(owner, i % 2 ^ way)

        def relay(self, way, i):
            self.c[way, i].wait_recv()
            spot = self.came(way, i)
            self.p.append(send(spot, spot, partner))
            return spot

        def step(self, i):
            for way in (0, 1):
                if i >= 2:
                    self.c[way, i - 2].wait_recv()
                    spot = self.came(way, i - 2)
                else:
                    spot = self.view(me_z, i % 2 ^ way)
                self.c[way, i] = send(spot, spot, z_prev if way else z_next)
                if i >= 2 or way == 0:
                    self.p.append(send(spot, spot, partner))

        def finish(self):
            for way in (0, 1):
                for i in (5, 6):
                    self.relay(way, i)

    def dc_dot(first_chunk):
        def step(i, carry):
            c = first_chunk + 2 * i
            at = pl.ds(pl.multiple_of(c * 128, 256), 256)
            out = jnp.dot(unit_t[...], grads[:, at], preferred_element_type=F32)
            dct[c] = out[:, :128]
            dct[c + 1] = out[:, 128:]
            return carry

        lax.fori_loop(0, n_z // 2, step, 0)

    theirs = (1 - core) * n_z
    dc_dot(theirs)
    pair_copy = send(dct.at[pl.ds(theirs, n_z)], dc_pair, partner)

    def du_dot(i, carry):
        at = pl.ds(pl.multiple_of(i * 512, 512), 512)
        out = jnp.dot(grads[at, :], proto_b[...], preferred_element_type=F32)
        du[i] = out.reshape(4, 128, width)
        return carry

    lax.fori_loop(0, rows // 512, du_dot, 0)
    a1 = Scatter4(along_x(du, 0), x, x_next, x_prev, rs_buf.at[0])
    b1 = Scatter4(along_y(du, 1), y, y_next, y_prev, rs_buf.at[1])
    a2 = Scatter4(in_y(du, 0), y, y_next, y_prev, rs_small.at[0])
    b2 = Scatter4(in_x(du, 1), x, x_next, x_prev, rs_small.at[1])
    zs, zg = ScatterZ(), GatherZ()
    a1.start()
    b1.start()

    dc_dot(core * n_z)
    pair_copy.wait_recv()
    for i in range(n_z):
        dc_half[i] = dct[core * n_z + i] + dc_pair[i]
    zs.step(0)
    zs.step(1)
    a1.mid()
    b1.mid()
    zs.step(2)
    zs.step(3)
    zs.step(4)
    a1.finish()
    a2.start()
    b1.finish()
    b2.start()
    zs.step(5)
    zs.step(6)
    a2.mid()
    b2.mid()

    def project(grad, raw):
        unit, inverse = normalized(raw)
        along = jnp.sum(unit * grad, axis=-1, keepdims=True)
        return (grad - unit * along) * inverse

    def lanes_square(block):
        sq = block * block
        return jnp.sum(sq[:, :128] + sq[:, 128:], axis=0, keepdims=True)

    zs.finish()
    mine = core * n_z + me_z
    dw_own = project(dc_half[me_z].T, proto_ref[pl.ds(pl.multiple_of(mine * 128, 128), 128), :])
    agw[mine] = dw_own
    zg.step(0)
    zg.step(1)
    sq_p[me_p, 0:1, :] = lanes_square(dw_own)

    a2.finish()
    b2.finish()
    at = pl.ds(pl.multiple_of((me_p % view_blocks) * 128, 128), 128)
    is_slow = me_p < view_blocks
    raw = jnp.where(is_slow, slow_ref[at, :].astype(F32), fast_ref[at, :].astype(F32))
    dx_own = project(du[x, y], raw)
    agx[x, y] = dx_own
    ga1 = Gather4(in_y(agx, 0), y, y_next, y_prev)
    gb1 = Gather4(in_x(agx, 1), x, x_next, x_prev)
    ga2 = Gather4(along_x(agx, 0), x, x_next, x_prev)
    gb2 = Gather4(along_y(agx, 1), y, y_next, y_prev)
    ga1.start()
    gb1.start()
    sq_p[me_p, 1:2, :] = lanes_square(dx_own)
    sq_p[me_p, 2:8, :] = jnp.zeros((6, 128), F32)
    sq_copies = start_all(sq_p, me_p, n_p, p_id, send_sem, sqp_sem)
    zg.step(2)
    zg.step(3)
    ga1.mid()
    gb1.mid()
    zg.step(4)
    ga1.finish()
    ga2.start()
    gb1.finish()
    gb2.start()
    for copy in sq_copies:
        copy.wait()
    sq_z[me_z] = total_of(sq_p, n_p)
    sq_copies = start_all(sq_z, me_z, n_z, z_id, send_sem, sqz_sem)
    zg.step(5)
    zg.step(6)
    ga2.mid()
    gb2.mid()
    for copy in sq_copies:
        copy.wait()
    sq_pair[core] = total_of(sq_z, n_z)
    pair_copy = send(sq_pair.at[core], sq_pair.at[core], partner)
    zg.finish()
    for copy in zg.p:
        copy.wait_recv()
    local_w = pltpu.make_async_copy(agw, dw_ref, local_sem.at[0])
    local_w.start()
    pair_copy.wait_recv()
    square = jnp.sum(sq_pair[0] + sq_pair[1], axis=1, keepdims=True)
    entries = float(protos_all * width), float(2 * clips_all * width)
    for i, out in enumerate((wf_ref, xf_ref)):
        out[...] = jnp.broadcast_to(
            lax.rsqrt(square[i:i + 1, :] / entries[i] + NORM_EPS), (8, width))
    ga2.finish()
    gb2.finish()
    local_x = pltpu.make_async_copy(agx, dx_ref, local_sem.at[1])
    local_x.start()
    for copy in pending:
        copy.wait_send()
    local_w.wait()
    local_x.wait()


def body(slow_embed, fast_embed, prototypes):
    clips, width = slow_embed.shape
    protos = prototypes.shape[0]
    n_b = lax.axis_size("batch")
    n_p = lax.axis_size("proto")
    n_z = n_b // 2
    rows = 2 * clips
    DMA = pltpu.SemaphoreType.DMA
    vmem = pltpu.VMEM
    lane_chunks = protos // 128
    row_blocks = rows // 128
    scratch = [
        vmem((rows, protos), F32),
        vmem((rows, protos), BF16),
        vmem((rows, width), BF16),
        vmem((width, rows), BF16),
        vmem((protos, width), BF16),
        vmem((rows, 128), F32),
        vmem((rows, 128), F32),
        vmem((rows, 128), F32),
        vmem((rows, 128), F32),
        vmem((4, 4, 128, width), F32),
        vmem((lane_chunks, width, 128), F32),
        vmem((n_z, width, 128), F32),
        vmem((n_z, width, 128), F32),
        vmem((2, 6, 4, 32, width), F32),
        vmem((2, 6, 32, width), F32),
        vmem((2, 7, 128, 128), F32),
        vmem((4, 4, 128, width), F32),
        vmem((lane_chunks, 128, width), F32),
        vmem((ITERS, n_z, 2 * lane_chunks, 128), F32),
        vmem((ITERS, 2, 2 * lane_chunks, 128), F32),
        vmem((ITERS, n_p, row_blocks, 128), F32),
        vmem((n_p, row_blocks, 128), F32),
        vmem((n_p, 8, 128), F32),
        vmem((n_z, 8, 128), F32),
        vmem((2, 8, 128), F32),
        DMA((16,)), DMA(()), DMA((ITERS, n_z)), DMA((ITERS,)), DMA((ITERS, n_p)),
        DMA((n_p,)), DMA((n_p,)),
        DMA((n_p,)), DMA((n_z,)), DMA((COPIES,)), DMA((COPIES,)), DMA((2,)),
    ]
    whole = pl.BlockSpec(memory_space=pltpu.VMEM)
    anywhere = pl.BlockSpec(memory_space=pl.ANY)
    dw, dx, dw_factor, dx_factor = pl.pallas_call(
        functools.partial(kernel, (clips, protos, width, n_z, n_p)),
        out_shape=(
            jax.ShapeDtypeStruct((lane_chunks, 128, width), F32),
            jax.ShapeDtypeStruct((4, 4, 128, width), F32),
            jax.ShapeDtypeStruct((8, width), F32),
            jax.ShapeDtypeStruct((8, width), F32),
        ),
        in_specs=[whole] * 3,
        out_specs=(anywhere, anywhere, whole, whole),
        scratch_shapes=scratch,
        compiler_params=pltpu.CompilerParams(
            collective_id=0, has_side_effects=True, vmem_limit_bytes=60 * 2**20),
        name="swav",
    )(slow_embed, fast_embed, prototypes)
    dw = (dw.reshape(protos // 8, 8, width) * dw_factor).reshape(protos, width)
    dx = dx.reshape(rows // 8, 8, width)
    half = clips // 8
    slow = (dx[:half] * dx_factor).reshape(clips, width)
    fast = (dx[half:] * dx_factor).reshape(clips, width)
    return (dw, slow, fast)


def solution(mesh):
    placed = (P("batch", None), P("batch", None), P("proto", None))
    return jax.shard_map(
        body,
        mesh=mesh,
        in_specs=placed,
        out_specs=(P("proto", None), P("batch", None), P("batch", None)),
        check_vma=False,
    )
```

```python
import functools

import jax
import jax.numpy as jnp
from jax import lax
from jax.experimental import pallas as pl
from jax.experimental.pallas import tpu as pltpu
from jax.sharding import PartitionSpec as P

ITERS = 3
COPIES = 128
NORM_EPS = 1e-06
MESH = pl.DeviceIdType.MESH
F32 = jnp.float32
BF16 = jnp.bfloat16


def normalized(rows):
    total = jnp.sum(rows * rows, axis=-1, keepdims=True) + 1e-12
    inverse = 1.0 / jnp.sqrt(total)
    return rows * inverse, inverse


def fold8(block):
    rows, lanes = block.shape
    return jnp.sum(block.reshape(rows // 8, 8, lanes), axis=0)


def kernel(
    dims,
    slow_ref, fast_ref, proto_ref,
    dw_ref, dx_ref, wf_ref, xf_ref,
    table, grads, unit_b, unit_t, proto_b, scale, clip_b, soft_b, code_b,
    du, dct, dc_pair, dc_half, rs_buf, rs_small, z_buf, agx, agw,
    col_z, col_pair, row_recv, den_recv, sq_p, sq_z, sq_pair,
    send_sem, col_send, col_sem, colp_send, colp_sem, row_send, row_sem, den_sem, den_send,
    sqp_sem, sqz_sem, out_sem, in_sem, local_sem,
):
    clips, protos, width, n_z, n_p = dims
    batch_me = lax.axis_index("batch")
    me_p = lax.axis_index("proto")
    me_z = batch_me // 2
    core = batch_me % 2
    clips_all = clips * 2 * n_z
    protos_all = protos * n_p
    rows = 2 * clips
    lane_chunks = protos // 128
    row_blocks = rows // 128
    view_blocks = clips // 128
    embeds = (slow_ref, fast_ref)

    def p_id(d):
        return {"proto": (me_p + d) % n_p}

    def z_id(d):
        return {"batch": ((me_z + d) % n_z) * 2 + core}

    partner = {"batch": me_z * 2 + 1 - core}

    def remote(src, dst, send, recv, device):
        return pltpu.make_async_remote_copy(
            src_ref=src, dst_ref=dst, send_sem=send, recv_sem=recv,
            device_id=device, device_id_type=MESH,
        )

    barrier = pltpu.get_barrier_semaphore()
    for d in range(1, n_p):
        pl.semaphore_signal(barrier, inc=1, device_id=p_id(d), device_id_type=MESH)
    for d in range(1, n_z):
        pl.semaphore_signal(barrier, inc=1, device_id=z_id(d), device_id_type=MESH)
    pl.semaphore_signal(barrier, inc=1, device_id=partner, device_id_type=MESH)

    def proto_norm(i, carry):
        at = pl.ds(pl.multiple_of(i * 128, 128), 128)
        unit, _ = normalized(proto_ref[at, :])
        proto_b[at, :] = unit.astype(BF16)
        return carry

    lax.fori_loop(0, protos // 128, proto_norm, 0)

    def chunk(c):
        return slice(c * 128, (c + 1) * 128)

    def total_of(ref, count):
        acc = ref[0]
        for i in range(1, count):
            acc = acc + ref[i]
        return acc

    def start_all(ref, me, count, ids, send, recv):
        copies = []
        for d in range(1, count):
            copy = remote(ref.at[me], ref.at[me], send.at[d], recv.at[d], ids(d))
            copy.start()
            copies.append(copy)
        return copies

    zero = jnp.zeros((8, 128), F32)

    def put_cols(it, v, cols):
        for c in range(lane_chunks):
            col_z[it, v, me_z, c:c + 1, :] = jnp.sum(cols[c], axis=0, keepdims=True)
        return start_all(col_z.at[it, v], me_z, n_z, z_id, col_send.at[it, v], col_sem.at[it, v])

    def lane_sums(block):
        return jnp.sum(block.T, axis=0, keepdims=True)

    def spread(values, v, target):
        for i in range(view_blocks):
            at = slice(v * clips + i * 128, v * clips + (i + 1) * 128)
            target[at, :] = jnp.broadcast_to(values[i:i + 1, :], (128, 128)).T

    step_m, step_w = 256, 512

    def first_pass(v):
        def step(i, cols):
            at = pl.ds(pl.multiple_of(i * step_m, step_m), step_m)
            glob = pl.ds(pl.multiple_of(v * clips + i * step_m, step_m), step_m)
            unit, _ = normalized(embeds[v][at, :].astype(F32))
            ub = unit.astype(BF16)
            unit_b[glob, :] = ub
            den = jnp.zeros((step_m, 128), F32)
            cols = list(cols)
            for k in range(protos // step_w):
                score = lax.dot_general(
                    ub, proto_b[k * step_w:(k + 1) * step_w, :],
                    (((1,), (1,)), ((), ())), preferred_element_type=F32)
                soft = jnp.exp(score * 10.0)
                code = soft * soft
                table[glob, k * step_w:(k + 1) * step_w] = code
                for j in range(step_w // 128):
                    den = den + soft[:, chunk(j)]
                    c = k * (step_w // 128) + j
                    cols[c] = cols[c] + fold8(code[:, chunk(j)])
            for j in range(step_m // 128):
                den_recv[me_p, pl.ds(v * view_blocks + i * (step_m // 128) + j, 1), :] = lane_sums(den[chunk(j), :])
            return tuple(cols)

        return lax.fori_loop(0, clips // step_m, step, (zero,) * lane_chunks)

    def cols_pass(v):
        def step(i, cols):
            at = pl.ds(pl.multiple_of(v * clips + i * 64, 64), 64)
            s = clip_b[at, :]
            return tuple(cols[c] + fold8(table[at, chunk(c)] * s) for c in range(lane_chunks))

        return lax.fori_loop(0, clips // 64, step, (zero,) * lane_chunks)

    def rows_pass(it, v):
        def step(i, carry):
            for j in range(2):
                block = 2 * i + j
                at = pl.ds(pl.multiple_of(v * clips + block * 128, 128), 128)
                acc = jnp.zeros((128, 128), F32)
                for c in range(lane_chunks):
                    acc = acc + table[at, chunk(c)] * scale[v, c:c + 1, :]
                row_recv[it, v, me_p, pl.ds(block, 1), :] = lane_sums(acc)
            return carry

        lax.fori_loop(0, view_blocks // 2, step, 0)
        return start_all(row_recv.at[it, v], me_p, n_p, p_id, row_send.at[it, v], row_sem.at[it, v])

    def wait_all(copies):
        for copy in copies:
            copy.wait_recv()
        sends.extend(copies)

    def pair_start(it, v, copies):
        wait_all(copies)
        pair = col_pair.at[it, v]
        pair[core] = total_of(col_z.at[it, v], n_z)
        copy = remote(pair.at[core], pair.at[core], colp_send.at[it, v], colp_sem.at[it, v], partner)
        copy.start()
        return copy

    sends = []
    z_copies = [None, None]
    row_copies = [None, None]
    z_cols = first_pass(0)
    pl.semaphore_wait(barrier, n_p - 1 + n_z - 1 + 1)
    z_copies[0] = put_cols(0, 0, z_cols)
    z_copies[1] = put_cols(0, 1, first_pass(1))
    den_copies = start_all(den_recv, me_p, n_p, p_id, den_send, den_sem)

    def transpose_unit(i, carry):
        at = pl.ds(pl.multiple_of(i * 128, 128), 128)
        unit_t[:, at] = unit_b[at, :].astype(F32).T.astype(BF16)
        return carry

    lax.fori_loop(0, row_blocks, transpose_unit, 0)

    def grad_pass(v):
        w = 1 - v

        def step(i, carry):
            mine = pl.ds(pl.multiple_of(v * clips + i * 64, 64), 64)
            other = pl.ds(pl.multiple_of(w * clips + i * 64, 64), 64)
            soft_scale = soft_b[mine, :]
            code_scale = code_b[other, :]
            for c in range(lane_chunks):
                e = table[mine, chunk(c)]
                code = table[other, chunk(c)] * scale[w, c:c + 1, :] * code_scale
                grads[mine, chunk(c)] = (e * lax.rsqrt(e) * soft_scale - code).astype(BF16)
            return carry

        lax.fori_loop(0, clips // 64, step, 0)

    def du_dot(first_step):
        def step(i, carry):
            at = pl.ds(pl.multiple_of(i * 512, 512), 512)
            out = jnp.dot(grads[at, :], proto_b[...], preferred_element_type=F32)
            du[i] = out.reshape(4, 128, width)
            return carry

        lax.fori_loop(first_step, first_step + 2, step, 0)

    for it in range(ITERS):
        pairs = [pair_start(it, v, z_copies[v]) for v in range(2)]
        for v in range(2):
            wait_all([pairs[v]])
            scale[v] = 1.0 / (protos_all * (col_pair[it, v, 0] + col_pair[it, v, 1]))
            row_copies[v] = rows_pass(it, v)
        if it == 0:
            wait_all(den_copies)
            soft = 10.0 / total_of(den_recv, n_p)
            for v in range(2):
                spread(soft[v * view_blocks:(v + 1) * view_blocks], v, soft_b)
        for v in range(2):
            wait_all(row_copies[v])
            row_sum = total_of(row_recv.at[it, v], n_p)
            if it < ITERS - 1:
                spread(1.0 / (clips_all * row_sum), v, clip_b)
                z_copies[v] = put_cols(it + 1, v, cols_pass(v))
            else:
                spread(10.0 / row_sum, v, code_b)
                grad_pass(1 - v)
                if v == 0:
                    du_dot(2)

    pending = []
    counter = [0]

    def send(src, dst, device):
        n = counter[0]
        counter[0] += 1
        copy = remote(src, dst, out_sem.at[n], in_sem.at[n], device)
        copy.start()
        pending.append(copy)
        return copy

    def add_to(ref, value):
        ref[...] = ref[...] + value

    x, y = me_p // 4, me_p % 4
    x_next = {"proto": (x + 1) % 4 * 4 + y}
    x_prev = {"proto": (x + 3) % 4 * 4 + y}
    y_next = {"proto": x * 4 + (y + 1) % 4}
    y_prev = {"proto": x * 4 + (y + 3) % 4}
    z_next, z_prev = z_id(1), z_id(n_z - 1)

    class Scatter4:
        def __init__(self, view, me, ahead, behind, buf):
            self.view, self.me, self.ahead, self.behind, self.buf = view, me, ahead, behind, buf
            self.c = {}

        def send(self, slot, dest, part):
            device = self.ahead if slot < 3 else self.behind
            self.c[slot] = send(self.view(dest, part), self.buf.at[slot], device)

        def start(self):
            m = self.me
            self.send(0, (m + 2) % 4, 0)
            self.send(3, (m + 2) % 4, 1)
            self.send(1, (m + 1) % 4, 1)
            self.send(4, (m + 3) % 4, 0)

        def mid(self):
            m = self.me
            self.c[0].wait_recv()
            add_to(self.view((m + 1) % 4, 0), self.buf[0])
            self.send(2, (m + 1) % 4, 0)
            self.c[3].wait_recv()
            add_to(self.view((m + 3) % 4, 1), self.buf[3])
            self.send(5, (m + 3) % 4, 1)

        def finish(self):
            for slot in (1, 4, 2, 5):
                self.c[slot].wait_recv()
            add_to(self.view(self.me, 0), self.buf[2] + self.buf[4])
            add_to(self.view(self.me, 1), self.buf[1] + self.buf[5])

    class Gather4:
        def __init__(self, view, me, ahead, behind):
            self.view, self.me, self.ahead, self.behind = view, me, ahead, behind
            self.c = {}

        def send(self, slot, owner, part):
            spot = self.view(owner, part)
            self.c[slot] = send(spot, spot, self.ahead if slot < 3 else self.behind)

        def start(self):
            self.send(0, self.me, 0)
            self.send(3, self.me, 1)
            self.send(1, self.me, 1)
            self.send(4, self.me, 0)

        def mid(self):
            self.c[0].wait_recv()
            self.send(2, (self.me + 3) % 4, 0)
            self.c[3].wait_recv()
            self.send(5, (self.me + 1) % 4, 1)

        def finish(self):
            for slot in (1, 4, 2, 5):
                self.c[slot].wait_recv()

    def quarter(half, part):
        return pl.ds(half * 64 + part * 32, 32)

    def along_x(ref, half):
        return lambda at, part: ref.at[at, :, quarter(half, part), :]

    def along_y(ref, half):
        return lambda at, part: ref.at[:, at, quarter(half, part), :]

    def in_x(ref, half):
        return lambda at, part: ref.at[at, y, quarter(half, part), :]

    def in_y(ref, half):
        return lambda at, part: ref.at[x, at, quarter(half, part), :]

    hops = (4, 3, 3, 2, 2, 1, 1)

    class ScatterZ:
        def __init__(self):
            self.c = {}

        def view(self, dest, part):
            return dc_half.at[dest, pl.ds(part * 128, 128), :]

        def step(self, i):
            part = i % 2
            for way in (0, 1):
                dest = (me_z + (hops[i] if way == 0 else n_z - hops[i])) % n_z
                spot = self.view(dest, part ^ way)
                if i >= 2:
                    self.c[way, i - 2].wait_recv()
                    add_to(spot, z_buf[way, i - 2])
                self.c[way, i] = send(spot, z_buf.at[way, i], z_prev if way else z_next)

        def finish(self):
            for way in (0, 1):
                for i in (5, 6):
                    self.c[way, i].wait_recv()
                    add_to(self.view(me_z, i % 2 ^ way), z_buf[way, i])

    class GatherZ:
        def __init__(self):
            self.c = {}
            self.p = []

        def view(self, owner, part):
            return agw.at[core * n_z + owner, pl.ds(part * 64, 64), :]

        def came(self, way, i):
            far = i // 2 + 1
            owner = (me_z + (far if way else n_z - far)) % n_z
            return self.view(owner, i % 2 ^ way)

        def relay(self, way, i):
            self.c[way, i].wait_recv()
            spot = self.came(way, i)
            self.p.append(send(spot, spot, partner))
            return spot

        def step(self, i):
            for way in (0, 1):
                if i >= 2:
                    self.c[way, i - 2].wait_recv()
                    spot = self.came(way, i - 2)
                else:
                    spot = self.view(me_z, i % 2 ^ way)
                self.c[way, i] = send(spot, spot, z_prev if way else z_next)
                if i >= 2 or way == 0:
                    self.p.append(send(spot, spot, partner))

        def finish(self):
            for way in (0, 1):
                for i in (5, 6):
                    self.relay(way, i)

    def dc_dot(first_chunk):
        def step(i, carry):
            c = first_chunk + 2 * i
            at = pl.ds(pl.multiple_of(c * 128, 256), 256)
            out = jnp.dot(unit_t[...], grads[:, at], preferred_element_type=F32)
            dct[c] = out[:, :128]
            dct[c + 1] = out[:, 128:]
            return carry

        lax.fori_loop(0, n_z // 2, step, 0)

    theirs = (1 - core) * n_z
    dc_dot(theirs)
    pair_copy = send(dct.at[pl.ds(theirs, n_z)], dc_pair, partner)

    du_dot(0)
    a1 = Scatter4(along_x(du, 0), x, x_next, x_prev, rs_buf.at[0])
    b1 = Scatter4(along_y(du, 1), y, y_next, y_prev, rs_buf.at[1])
    a2 = Scatter4(in_y(du, 0), y, y_next, y_prev, rs_small.at[0])
    b2 = Scatter4(in_x(du, 1), x, x_next, x_prev, rs_small.at[1])
    zs, zg = ScatterZ(), GatherZ()
    a1.start()
    b1.start()

    dc_dot(core * n_z)
    pair_copy.wait_recv()
    for i in range(n_z):
        dc_half[i] = dct[core * n_z + i] + dc_pair[i]
    zs.step(0)
    zs.step(1)
    a1.mid()
    b1.mid()
    zs.step(2)
    zs.step(3)
    zs.step(4)
    a1.finish()
    a2.start()
    b1.finish()
    b2.start()
    zs.step(5)
    zs.step(6)
    a2.mid()
    b2.mid()

    def project(grad, raw):
        unit, inverse = normalized(raw)
        along = jnp.sum(unit * grad, axis=-1, keepdims=True)
        return (grad - unit * along) * inverse

    def lanes_square(block):
        sq = block * block
        return jnp.sum(sq[:, :128] + sq[:, 128:], axis=0, keepdims=True)

    zs.finish()
    mine = core * n_z + me_z
    dw_own = project(dc_half[me_z].T, proto_ref[pl.ds(pl.multiple_of(mine * 128, 128), 128), :])
    agw[mine] = dw_own
    zg.step(0)
    zg.step(1)
    sq_p[me_p, 0:1, :] = lanes_square(dw_own)

    a2.finish()
    b2.finish()
    at = pl.ds(pl.multiple_of((me_p % view_blocks) * 128, 128), 128)
    is_slow = me_p < view_blocks
    raw = jnp.where(is_slow, slow_ref[at, :].astype(F32), fast_ref[at, :].astype(F32))
    dx_own = project(du[x, y], raw)
    agx[x, y] = dx_own
    ga1 = Gather4(in_y(agx, 0), y, y_next, y_prev)
    gb1 = Gather4(in_x(agx, 1), x, x_next, x_prev)
    ga2 = Gather4(along_x(agx, 0), x, x_next, x_prev)
    gb2 = Gather4(along_y(agx, 1), y, y_next, y_prev)
    ga1.start()
    gb1.start()
    sq_p[me_p, 1:2, :] = lanes_square(dx_own)
    sq_p[me_p, 2:8, :] = jnp.zeros((6, 128), F32)
    sq_copies = start_all(sq_p, me_p, n_p, p_id, send_sem, sqp_sem)
    zg.step(2)
    zg.step(3)
    ga1.mid()
    gb1.mid()
    zg.step(4)
    ga1.finish()
    ga2.start()
    gb1.finish()
    gb2.start()
    for copy in sq_copies:
        copy.wait()
    sq_z[me_z] = total_of(sq_p, n_p)
    sq_copies = start_all(sq_z, me_z, n_z, z_id, send_sem, sqz_sem)
    zg.step(5)
    zg.step(6)
    ga2.mid()
    gb2.mid()
    for copy in sq_copies:
        copy.wait()
    sq_pair[core] = total_of(sq_z, n_z)
    pair_copy = send(sq_pair.at[core], sq_pair.at[core], partner)
    zg.finish()
    for copy in zg.p:
        copy.wait_recv()
    local_w = pltpu.make_async_copy(agw, dw_ref, local_sem.at[0])
    local_w.start()
    pair_copy.wait_recv()
    square = jnp.sum(sq_pair[0] + sq_pair[1], axis=1, keepdims=True)
    entries = float(protos_all * width), float(2 * clips_all * width)
    for i, out in enumerate((wf_ref, xf_ref)):
        out[...] = jnp.broadcast_to(
            lax.rsqrt(square[i:i + 1, :] / entries[i] + NORM_EPS), (8, width))
    ga2.finish()
    gb2.finish()
    local_x = pltpu.make_async_copy(agx, dx_ref, local_sem.at[1])
    local_x.start()
    for copy in pending + sends:
        copy.wait_send()
    local_w.wait()
    local_x.wait()


def body(slow_embed, fast_embed, prototypes):
    clips, width = slow_embed.shape
    protos = prototypes.shape[0]
    n_b = lax.axis_size("batch")
    n_p = lax.axis_size("proto")
    n_z = n_b // 2
    rows = 2 * clips
    DMA = pltpu.SemaphoreType.DMA
    vmem = pltpu.VMEM
    lane_chunks = protos // 128
    row_blocks = rows // 128
    scratch = [
        vmem((rows, protos), F32),
        vmem((rows, protos), BF16),
        vmem((rows, width), BF16),
        vmem((width, rows), BF16),
        vmem((protos, width), BF16),
        vmem((2, lane_chunks, 128), F32),
        vmem((rows, 128), F32),
        vmem((rows, 128), F32),
        vmem((rows, 128), F32),
        vmem((4, 4, 128, width), F32),
        vmem((lane_chunks, width, 128), F32),
        vmem((n_z, width, 128), F32),
        vmem((n_z, width, 128), F32),
        vmem((2, 6, 4, 32, width), F32),
        vmem((2, 6, 32, width), F32),
        vmem((2, 7, 128, 128), F32),
        vmem((4, 4, 128, width), F32),
        vmem((lane_chunks, 128, width), F32),
        vmem((ITERS, 2, n_z, lane_chunks, 128), F32),
        vmem((ITERS, 2, 2, lane_chunks, 128), F32),
        vmem((ITERS, 2, n_p, row_blocks // 2, 128), F32),
        vmem((n_p, row_blocks, 128), F32),
        vmem((n_p, 8, 128), F32),
        vmem((n_z, 8, 128), F32),
        vmem((2, 8, 128), F32),
        DMA((16,)), DMA((ITERS, 2, n_z)), DMA((ITERS, 2, n_z)), DMA((ITERS, 2)), DMA((ITERS, 2)),
        DMA((ITERS, 2, n_p)), DMA((ITERS, 2, n_p)),
        DMA((n_p,)), DMA((n_p,)),
        DMA((n_p,)), DMA((n_z,)), DMA((COPIES,)), DMA((COPIES,)), DMA((2,)),
    ]
    whole = pl.BlockSpec(memory_space=pltpu.VMEM)
    anywhere = pl.BlockSpec(memory_space=pl.ANY)
    dw, dx, dw_factor, dx_factor = pl.pallas_call(
        functools.partial(kernel, (clips, protos, width, n_z, n_p)),
        out_shape=(
            jax.ShapeDtypeStruct((lane_chunks, 128, width), F32),
            jax.ShapeDtypeStruct((4, 4, 128, width), F32),
            jax.ShapeDtypeStruct((8, width), F32),
            jax.ShapeDtypeStruct((8, width), F32),
        ),
        in_specs=[whole] * 3,
        out_specs=(anywhere, anywhere, whole, whole),
        scratch_shapes=scratch,
        compiler_params=pltpu.CompilerParams(
            collective_id=0, has_side_effects=True, vmem_limit_bytes=60 * 2**20),
        name="swav",
    )(slow_embed, fast_embed, prototypes)
    dw = (dw.reshape(protos // 8, 8, width) * dw_factor).reshape(protos, width)
    dx = dx.reshape(rows // 8, 8, width)
    half = clips // 8
    slow = (dx[:half] * dx_factor).reshape(clips, width)
    fast = (dx[half:] * dx_factor).reshape(clips, width)
    return (dw, slow, fast)


def solution(mesh):
    placed = (P("batch", None), P("batch", None), P("proto", None))
    return jax.shard_map(
        body,
        mesh=mesh,
        in_specs=placed,
        out_specs=(P("proto", None), P("batch", None), P("batch", None)),
        check_vma=False,
    )
```

```python
import functools

import jax
import jax.numpy as jnp
from jax import lax
from jax.experimental import pallas as pl
from jax.experimental.pallas import tpu as pltpu
from jax.sharding import PartitionSpec as P

ITERS = 3
COPIES = 192
NORM_EPS = 1e-06
MESH = pl.DeviceIdType.MESH
F32 = jnp.float32
BF16 = jnp.bfloat16


def normalized(rows):
    total = jnp.sum(rows * rows, axis=-1, keepdims=True) + 1e-12
    inverse = 1.0 / jnp.sqrt(total)
    return rows * inverse, inverse


def fold8(block):
    rows, lanes = block.shape
    return jnp.sum(block.reshape(rows // 8, 8, lanes), axis=0)


def kernel(
    dims,
    slow_ref, fast_ref, proto_ref,
    agw, slow_out, fast_out, wf_ref, xf_ref,
    table, grads, unit_b, unit_t, proto_b, scale, clip_b, soft_b, code_b,
    du, dct, dc_pair, dc_half, rs_buf, rs_small, z_buf,
    col_z, col_pair, row_recv, den_recv, sq_p, sq_z,
    send_sem, col_send, col_sem, colp_send, colp_sem, row_send, row_sem, den_sem, den_send,
    sqp_sem, sqz_sem, sqz_send, pair_out, pair_in, out_sem, in_sem,
):
    clips, protos, width, n_z, n_p = dims
    batch_me = lax.axis_index("batch")
    me_p = lax.axis_index("proto")
    me_z = batch_me // 2
    core = batch_me % 2
    clips_all = clips * 2 * n_z
    protos_all = protos * n_p
    rows = 2 * clips
    lane_chunks = protos // 128
    row_blocks = rows // 128
    view_blocks = clips // 128
    embeds = (slow_ref, fast_ref)

    def p_id(d):
        return {"proto": (me_p + d) % n_p}

    def z_id(d):
        return {"batch": ((me_z + d) % n_z) * 2 + core}

    def b_id(d):
        return {"batch": (batch_me + d) % (2 * n_z)}

    partner = {"batch": me_z * 2 + 1 - core}

    def remote(src, dst, send, recv, device):
        return pltpu.make_async_remote_copy(
            src_ref=src, dst_ref=dst, send_sem=send, recv_sem=recv,
            device_id=device, device_id_type=MESH,
        )

    barrier = pltpu.get_barrier_semaphore()
    for d in range(1, n_p):
        pl.semaphore_signal(barrier, inc=1, device_id=p_id(d), device_id_type=MESH)
    for d in range(1, 2 * n_z):
        pl.semaphore_signal(barrier, inc=1, device_id=b_id(d), device_id_type=MESH)

    def proto_norm(i, carry):
        at = pl.ds(pl.multiple_of(i * 128, 128), 128)
        unit, _ = normalized(proto_ref[at, :])
        proto_b[at, :] = unit.astype(BF16)
        return carry

    lax.fori_loop(0, protos // 128, proto_norm, 0)

    def chunk(c):
        return slice(c * 128, (c + 1) * 128)

    def total_of(ref, count):
        acc = ref[0]
        for i in range(1, count):
            acc = acc + ref[i]
        return acc

    def start_all(ref, me, count, ids, send, recv):
        copies = []
        for d in range(1, count):
            copy = remote(ref.at[me], ref.at[me], send.at[d], recv.at[d], ids(d))
            copy.start()
            copies.append(copy)
        return copies

    zero = jnp.zeros((8, 128), F32)

    def put_cols(it, v, cols):
        for c in range(lane_chunks):
            col_z[it, v, me_z, c:c + 1, :] = jnp.sum(cols[c], axis=0, keepdims=True)
        return start_all(col_z.at[it, v], me_z, n_z, z_id, col_send.at[it, v], col_sem.at[it, v])

    def lane_sums(block):
        return jnp.sum(block.T, axis=0, keepdims=True)

    def spread(values, v, target):
        for i in range(view_blocks):
            at = slice(v * clips + i * 128, v * clips + (i + 1) * 128)
            target[at, :] = jnp.broadcast_to(values[i:i + 1, :], (128, 128)).T

    pending = []
    counter = [0]

    def send(src, dst, device):
        n = counter[0]
        counter[0] += 1
        copy = remote(src, dst, out_sem.at[n], in_sem.at[n], device)
        copy.start()
        pending.append(copy)
        return copy

    def add_to(ref, value):
        ref[...] = ref[...] + value

    x, y = me_p // 4, me_p % 4
    x_next = {"proto": (x + 1) % 4 * 4 + y}
    x_prev = {"proto": (x + 3) % 4 * 4 + y}
    y_next = {"proto": x * 4 + (y + 1) % 4}
    y_prev = {"proto": x * 4 + (y + 3) % 4}
    z_next, z_prev = z_id(1), z_id(n_z - 1)

    class Scatter4:
        def __init__(self, view, me, ahead, behind, buf):
            self.view, self.me, self.ahead, self.behind, self.buf = view, me, ahead, behind, buf
            self.c = {}

        def send(self, slot, dest, part):
            device = self.ahead if slot < 3 else self.behind
            self.c[slot] = send(self.view(dest, part), self.buf.at[slot], device)

        def start(self):
            m = self.me
            self.send(0, (m + 2) % 4, 0)
            self.send(3, (m + 2) % 4, 1)
            self.send(1, (m + 1) % 4, 1)
            self.send(4, (m + 3) % 4, 0)

        def mid(self):
            m = self.me
            self.c[0].wait_recv()
            add_to(self.view((m + 1) % 4, 0), self.buf[0])
            self.send(2, (m + 1) % 4, 0)
            self.c[3].wait_recv()
            add_to(self.view((m + 3) % 4, 1), self.buf[3])
            self.send(5, (m + 3) % 4, 1)

        def finish(self):
            for slot in (1, 4, 2, 5):
                self.c[slot].wait_recv()
            add_to(self.view(self.me, 0), self.buf[2] + self.buf[4])
            add_to(self.view(self.me, 1), self.buf[1] + self.buf[5])

    class Gather4:
        def __init__(self, view, me, ahead, behind):
            self.view, self.me, self.ahead, self.behind = view, me, ahead, behind
            self.c = {}

        def send(self, slot, owner, part):
            spot = self.view(owner, part)
            self.c[slot] = send(spot, spot, self.ahead if slot < 3 else self.behind)

        def start(self):
            self.send(0, self.me, 0)
            self.send(3, self.me, 1)
            self.send(1, self.me, 1)
            self.send(4, self.me, 0)

        def mid(self):
            self.c[0].wait_recv()
            self.send(2, (self.me + 3) % 4, 0)
            self.c[3].wait_recv()
            self.send(5, (self.me + 1) % 4, 1)

        def finish(self):
            for slot in (1, 4, 2, 5):
                self.c[slot].wait_recv()

    def quarter(half, part):
        return pl.ds(half * 32 + part * 16, 16)

    def along_x(ref, half):
        return lambda at, part: ref.at[at, :, quarter(half, part), :]

    def along_y(ref, half):
        return lambda at, part: ref.at[:, at, quarter(half, part), :]

    def in_x(ref, half):
        return lambda at, part: ref.at[at, y, quarter(half, part), :]

    def in_y(ref, half):
        return lambda at, part: ref.at[x, at, quarter(half, part), :]

    class Both:
        def __init__(self, *rings):
            self.rings = rings

        def start(self):
            for ring in self.rings:
                ring.start()

        def mid(self):
            for ring in self.rings:
                ring.mid()

        def finish(self):
            for ring in self.rings:
                ring.finish()

    def scatter(v):
        ref = du.at[v]
        return (
            Both(Scatter4(along_x(ref, 0), x, x_next, x_prev, rs_buf.at[v, 0]),
                 Scatter4(along_y(ref, 1), y, y_next, y_prev, rs_buf.at[v, 1])),
            Both(Scatter4(in_y(ref, 0), y, y_next, y_prev, rs_small.at[v, 0]),
                 Scatter4(in_x(ref, 1), x, x_next, x_prev, rs_small.at[v, 1])))

    def gather(ref):
        return (
            Both(Gather4(in_y(ref, 0), y, y_next, y_prev),
                 Gather4(in_x(ref, 1), x, x_next, x_prev)),
            Both(Gather4(along_x(ref, 0), x, x_next, x_prev),
                 Gather4(along_y(ref, 1), y, y_next, y_prev)))

    hops = (4, 3, 3, 2, 2, 1, 1)
    split = 2
    units = len(hops) * split
    back = 2 * split

    class ScatterZ:
        def __init__(self):
            self.c = {}

        def view(self, dest, way, i):
            part = i // split % 2 ^ way
            return dc_half.at[dest, pl.ds(part * 128 + i % split * (128 // split), 128 // split), :]

        def step(self, i):
            for way in (0, 1):
                hop = hops[i // split]
                spot = self.view((me_z + (n_z - hop if way else hop)) % n_z, way, i)
                if i >= back:
                    self.c[way, i - back].wait_recv()
                    add_to(spot, z_buf[way, i - back])
                self.c[way, i] = send(spot, z_buf.at[way, i], z_prev if way else z_next)

        def finish(self):
            for i in range(units - back, units):
                for way in (0, 1):
                    self.c[way, i].wait_recv()
                    add_to(self.view(me_z, way, i), z_buf[way, i])

    class GatherZ:
        def __init__(self):
            self.c = {}
            self.p = []

        def view(self, owner, way, i):
            part = i // split % 2 ^ way
            return agw.at[core * n_z + owner, pl.ds(part * 64 + i % split * (64 // split), 64 // split), :]

        def relay(self, way, i):
            self.c[way, i].wait_recv()
            far = i // split // 2 + 1
            spot = self.view((me_z + (far if way else n_z - far)) % n_z, way, i)
            return spot

        def step(self, i):
            for way in (0, 1):
                if i >= back:
                    spot = self.relay(way, i - back)
                else:
                    spot = self.view(me_z, way, i)
                self.c[way, i] = send(spot, spot, z_prev if way else z_next)
                if i >= back:
                    self.p.append(send(spot, spot, partner))

        def own(self):
            spot = agw.at[core * n_z + me_z]
            self.p.append(send(spot, spot, partner))

        def finish(self):
            for i in range(units - back, units):
                for way in (0, 1):
                    spot = self.relay(way, i)
                    self.p.append(send(spot, spot, partner))

    rings = [scatter(0), scatter(1)]

    step_m, step_w = 256, 512

    def first_pass(v):
        def step(i, cols):
            at = pl.ds(pl.multiple_of(i * step_m, step_m), step_m)
            glob = pl.ds(pl.multiple_of(v * clips + i * step_m, step_m), step_m)
            unit, _ = normalized(embeds[v][at, :].astype(F32))
            ub = unit.astype(BF16)
            unit_b[glob, :] = ub
            den = jnp.zeros((step_m, 128), F32)
            cols = list(cols)
            for k in range(protos // step_w):
                score = lax.dot_general(
                    ub, proto_b[k * step_w:(k + 1) * step_w, :],
                    (((1,), (1,)), ((), ())), preferred_element_type=F32)
                soft = jnp.exp(score * 10.0)
                code = soft * soft
                table[glob, k * step_w:(k + 1) * step_w] = code
                for j in range(step_w // 128):
                    den = den + soft[:, chunk(j)]
                    c = k * (step_w // 128) + j
                    cols[c] = cols[c] + fold8(code[:, chunk(j)])
            for j in range(step_m // 128):
                den_recv[me_p, pl.ds(v * view_blocks + i * (step_m // 128) + j, 1), :] = lane_sums(den[chunk(j), :])
            return tuple(cols)

        return lax.fori_loop(0, clips // step_m, step, (zero,) * lane_chunks)

    def cols_pass(v):
        def step(i, cols):
            at = pl.ds(pl.multiple_of(v * clips + i * 64, 64), 64)
            s = clip_b[at, :]
            return tuple(cols[c] + fold8(table[at, chunk(c)] * s) for c in range(lane_chunks))

        return lax.fori_loop(0, clips // 64, step, (zero,) * lane_chunks)

    def rows_pass(it, v):
        def step(i, carry):
            for j in range(2):
                block = 2 * i + j
                at = pl.ds(pl.multiple_of(v * clips + block * 128, 128), 128)
                acc = jnp.zeros((128, 128), F32)
                for c in range(lane_chunks):
                    acc = acc + table[at, chunk(c)] * scale[v, c:c + 1, :]
                row_recv[it, v, me_p, pl.ds(block, 1), :] = lane_sums(acc)
            return carry

        lax.fori_loop(0, view_blocks // 2, step, 0)
        return start_all(row_recv.at[it, v], me_p, n_p, p_id, row_send.at[it, v], row_sem.at[it, v])

    def wait_all(copies):
        for copy in copies:
            copy.wait_recv()
        sends.extend(copies)

    def pair_start(it, v, copies):
        wait_all(copies)
        pair = col_pair.at[it, v]
        pair[core] = total_of(col_z.at[it, v], n_z)
        copy = remote(pair.at[core], pair.at[core], colp_send.at[it, v], colp_sem.at[it, v], partner)
        copy.start()
        return copy

    sends = []
    z_copies = [None, None]
    row_copies = [None, None]
    z_cols = first_pass(0)
    pl.semaphore_wait(barrier, n_p - 1 + 2 * n_z - 1)
    z_copies[0] = put_cols(0, 0, z_cols)
    z_copies[1] = put_cols(0, 1, first_pass(1))
    den_copies = start_all(den_recv, me_p, n_p, p_id, den_send, den_sem)

    def transpose_unit(i, carry):
        at = pl.ds(pl.multiple_of(i * 128, 128), 128)
        unit_t[:, at] = unit_b[at, :].astype(F32).T.astype(BF16)
        return carry

    lax.fori_loop(0, row_blocks, transpose_unit, 0)

    def grad_pass(v):
        w = 1 - v

        def step(i, carry):
            mine = pl.ds(pl.multiple_of(v * clips + i * 64, 64), 64)
            other = pl.ds(pl.multiple_of(w * clips + i * 64, 64), 64)
            soft_scale = soft_b[mine, :]
            code_scale = code_b[other, :]
            for c in range(lane_chunks):
                e = table[mine, chunk(c)]
                code = table[other, chunk(c)] * scale[w, c:c + 1, :] * code_scale
                grads[mine, chunk(c)] = (e * lax.rsqrt(e) * soft_scale - code).astype(BF16)
            return carry

        lax.fori_loop(0, clips // 64, step, 0)

    def du_dot(v):
        def step(i, carry):
            at = pl.ds(pl.multiple_of(v * clips + i * 512, 512), 512)
            out = jnp.dot(grads[at, :], proto_b[...], preferred_element_type=F32)
            du[v, pl.ds(2 * i, 2)] = out.reshape(2, 4, 64, width)
            return carry

        lax.fori_loop(0, clips // 512, step, 0)

    for it in range(ITERS):
        pairs = [pair_start(it, v, z_copies[v]) for v in range(2)]
        for v in range(2):
            wait_all([pairs[v]])
            scale[v] = 1.0 / (protos_all * (col_pair[it, v, 0] + col_pair[it, v, 1]))
            row_copies[v] = rows_pass(it, v)
        if it == 0:
            wait_all(den_copies)
            soft = 10.0 / total_of(den_recv, n_p)
            for v in range(2):
                spread(soft[v * view_blocks:(v + 1) * view_blocks], v, soft_b)
        for v in range(2):
            wait_all(row_copies[v])
            row_sum = total_of(row_recv.at[it, v], n_p)
            if it < ITERS - 1:
                spread(1.0 / (clips_all * row_sum), v, clip_b)
                z_copies[v] = put_cols(it + 1, v, cols_pass(v))
            else:
                spread(10.0 / row_sum, v, code_b)
                grad_pass(1 - v)
                if v == 0:
                    du_dot(1)
                    rings[1][0].start()

    def project(grad, raw):
        unit, inverse = normalized(raw)
        along = jnp.sum(unit * grad, axis=-1, keepdims=True)
        return (grad - unit * along) * inverse

    def lanes_square(block):
        sq = block * block
        return jnp.sum(sq[:, :128] + sq[:, 128:], axis=0, keepdims=True)

    theirs = (1 - core) * n_z

    def pair_piece(i):
        return remote(
            dct.at[pl.ds(theirs + 2 * i, 2)], dc_pair.at[pl.ds(2 * i, 2)],
            pair_out.at[i], pair_in.at[i], partner)

    def dc_dot(first_chunk, sending):
        def step(i, carry):
            c = first_chunk + 2 * i
            at = pl.ds(pl.multiple_of(c * 128, 256), 256)
            out = jnp.dot(unit_t[...], grads[:, at], preferred_element_type=F32)
            dct[c] = out[:, :128]
            dct[c + 1] = out[:, 128:]
            if sending:
                pair_piece(i).start()
            return carry

        lax.fori_loop(0, n_z // 2, step, 0)

    outs = (slow_out, fast_out)
    gathers = [gather(out) for out in outs]
    zs, zg = ScatterZ(), GatherZ()

    def own_rows(v):
        raw = embeds[v][pl.ds(pl.multiple_of(me_p * 64, 64), 64), :].astype(F32)
        own = project(du[v, x, y], raw)
        outs[v][x, y] = own
        gathers[v][0].start()
        return lanes_square(own)

    rings[1][0].mid()
    dc_dot(theirs, True)
    dc_dot(core * n_z, False)
    for i in range(n_z // 2):
        pair_piece(i).wait_recv()
        for j in (2 * i, 2 * i + 1):
            dc_half[j] = dct[core * n_z + j] + dc_pair[j]
    for i in range(back):
        zs.step(i)
    du_dot(0)
    rings[0][0].start()
    rings[1][0].finish()
    rings[1][1].start()
    zs.step(4)
    zs.step(5)
    rings[1][1].mid()
    zs.step(6)
    rings[0][0].mid()
    zs.step(7)
    rings[1][1].finish()
    square_x = own_rows(1)
    zs.step(8)
    zs.step(9)
    gathers[1][0].mid()
    rings[0][0].finish()
    rings[0][1].start()
    zs.step(10)
    zs.step(11)
    gathers[1][0].finish()
    gathers[1][1].start()
    rings[0][1].mid()
    zs.step(12)
    zs.step(13)
    zs.finish()
    mine = core * n_z + me_z
    dw_own = project(dc_half[me_z].T, proto_ref[pl.ds(pl.multiple_of(mine * 128, 128), 128), :])
    agw[mine] = dw_own
    for i in range(back):
        zg.step(i)
    zg.own()
    rings[0][1].finish()
    square_x = square_x + own_rows(0)
    sq_p[me_p, 0:1, :] = lanes_square(dw_own)
    sq_p[me_p, 1:2, :] = square_x
    sq_p[me_p, 2:8, :] = jnp.zeros((6, 128), F32)
    sq_copies = start_all(sq_p, me_p, n_p, p_id, send_sem, sqp_sem)
    gathers[1][1].mid()
    zg.step(4)
    zg.step(5)
    gathers[0][0].mid()
    zg.step(6)
    zg.step(7)
    gathers[0][0].finish()
    gathers[0][1].start()
    zg.step(8)
    zg.step(9)
    zg.step(10)
    gathers[0][1].mid()
    zg.step(11)
    wait_all(sq_copies)
    sq_z[batch_me] = total_of(sq_p, n_p)
    sq_copies = start_all(sq_z, batch_me, 2 * n_z, b_id, sqz_send, sqz_sem)
    zg.step(12)
    zg.step(13)
    gathers[1][1].finish()
    gathers[0][1].finish()
    zg.finish()
    wait_all(sq_copies)
    square = jnp.sum(total_of(sq_z, 2 * n_z), axis=1, keepdims=True)
    entries = float(protos_all * width), float(2 * clips_all * width)
    for i, out in enumerate((wf_ref, xf_ref)):
        out[...] = jnp.broadcast_to(
            lax.rsqrt(square[i:i + 1, :] / entries[i] + NORM_EPS), (8, width))
    for copy in zg.p:
        copy.wait_recv()
    for i in range(n_z // 2):
        pair_piece(i).wait_send()
    for copy in pending + sends:
        copy.wait_send()


def body(slow_embed, fast_embed, prototypes):
    clips, width = slow_embed.shape
    protos = prototypes.shape[0]
    n_b = lax.axis_size("batch")
    n_p = lax.axis_size("proto")
    n_z = n_b // 2
    rows = 2 * clips
    DMA = pltpu.SemaphoreType.DMA
    vmem = pltpu.VMEM
    lane_chunks = protos // 128
    row_blocks = rows // 128
    scratch = [
        vmem((rows, protos), F32),
        vmem((rows, protos), BF16),
        vmem((rows, width), BF16),
        vmem((width, rows), BF16),
        vmem((protos, width), BF16),
        vmem((2, lane_chunks, 128), F32),
        vmem((rows, 128), F32),
        vmem((rows, 128), F32),
        vmem((rows, 128), F32),
        vmem((2, 4, 4, 64, width), F32),
        vmem((lane_chunks, width, 128), F32),
        vmem((n_z, width, 128), F32),
        vmem((n_z, width, 128), F32),
        vmem((2, 2, 6, 4, 16, width), F32),
        vmem((2, 2, 6, 16, width), F32),
        vmem((2, 14, 64, 128), F32),
        vmem((ITERS, 2, n_z, lane_chunks, 128), F32),
        vmem((ITERS, 2, 2, lane_chunks, 128), F32),
        vmem((ITERS, 2, n_p, row_blocks // 2, 128), F32),
        vmem((n_p, row_blocks, 128), F32),
        vmem((n_p, 8, 128), F32),
        vmem((n_b, 8, 128), F32),
        DMA((16,)), DMA((ITERS, 2, n_z)), DMA((ITERS, 2, n_z)), DMA((ITERS, 2)), DMA((ITERS, 2)),
        DMA((ITERS, 2, n_p)), DMA((ITERS, 2, n_p)),
        DMA((n_p,)), DMA((n_p,)),
        DMA((n_p,)), DMA((n_b,)), DMA((n_b,)), DMA((n_z // 2,)), DMA((n_z // 2,)),
        DMA((COPIES,)), DMA((COPIES,)),
    ]
    whole = pl.BlockSpec(memory_space=pltpu.VMEM)
    dw, slow, fast, dw_factor, dx_factor = pl.pallas_call(
        functools.partial(kernel, (clips, protos, width, n_z, n_p)),
        out_shape=(
            vmem((lane_chunks, 128, width), F32),
            vmem((4, 4, 64, width), F32),
            vmem((4, 4, 64, width), F32),
            vmem((8, width), F32),
            vmem((8, width), F32),
        ),
        in_specs=[whole] * 3,
        out_specs=(whole,) * 5,
        scratch_shapes=scratch,
        compiler_params=pltpu.CompilerParams(
            collective_id=0, has_side_effects=True, vmem_limit_bytes=56 * 2**20),
        name="swav",
    )(slow_embed, fast_embed, prototypes)

    def scaled(array, factor, rows):
        return (array.reshape(rows // 8, 8, width) * factor).reshape(rows, width)

    return (
        scaled(dw, dw_factor, protos),
        scaled(slow, dx_factor, clips),
        scaled(fast, dx_factor, clips),
    )


def solution(mesh):
    placed = (P("batch", None), P("batch", None), P("proto", None))
    return jax.shard_map(
        body,
        mesh=mesh,
        in_specs=placed,
        out_specs=(P("proto", None), P("batch", None), P("batch", None)),
        check_vma=False,
    )
```

```python
import functools

import jax
import jax.numpy as jnp
from jax import lax
from jax.experimental import pallas as pl
from jax.experimental.pallas import tpu as pltpu
from jax.sharding import PartitionSpec as P

ITERS = 3
COPIES = 192
NORM_EPS = 1e-06
MESH = pl.DeviceIdType.MESH
F32 = jnp.float32
BF16 = jnp.bfloat16


def normalized(rows):
    total = jnp.sum(rows * rows, axis=-1, keepdims=True) + 1e-12
    inverse = 1.0 / jnp.sqrt(total)
    return rows * inverse, inverse


def fold8(block):
    rows, lanes = block.shape
    return jnp.sum(block.reshape(rows // 8, 8, lanes), axis=0)


def kernel(
    dims,
    slow_ref, fast_ref, proto_ref,
    agw, agx, wf_ref, xf_ref,
    table, grads, unit_b, unit_t, proto_b, scale, clip_b, soft_b, code_b,
    du, dct, dc_pair, dc_half, rs_buf, rs_small, z_buf,
    col_z, col_pair, row_recv, den_recv, sq_p, sq_z,
    send_sem, col_send, col_sem, colp_send, colp_sem, row_send, row_sem, den_sem, den_send,
    sqp_sem, sqz_sem, sqz_send, pair_out, pair_in, out_sem, in_sem,
):
    clips, protos, width, n_z, n_p = dims
    batch_me = lax.axis_index("batch")
    me_p = lax.axis_index("proto")
    me_z = batch_me // 2
    core = batch_me % 2
    clips_all = clips * 2 * n_z
    protos_all = protos * n_p
    rows = 2 * clips
    lane_chunks = protos // 128
    row_blocks = rows // 128
    view_blocks = clips // 128
    embeds = (slow_ref, fast_ref)

    def p_id(d):
        return {"proto": (me_p + d) % n_p}

    def z_id(d):
        return {"batch": ((me_z + d) % n_z) * 2 + core}

    def b_id(d):
        return {"batch": (batch_me + d) % (2 * n_z)}

    partner = {"batch": me_z * 2 + 1 - core}

    def remote(src, dst, send, recv, device):
        return pltpu.make_async_remote_copy(
            src_ref=src, dst_ref=dst, send_sem=send, recv_sem=recv,
            device_id=device, device_id_type=MESH,
        )

    barrier = pltpu.get_barrier_semaphore()
    for d in range(1, n_p):
        pl.semaphore_signal(barrier, inc=1, device_id=p_id(d), device_id_type=MESH)
    for d in range(1, 2 * n_z):
        pl.semaphore_signal(barrier, inc=1, device_id=b_id(d), device_id_type=MESH)

    def proto_norm(i, carry):
        at = pl.ds(pl.multiple_of(i * 128, 128), 128)
        unit, _ = normalized(proto_ref[at, :])
        proto_b[at, :] = unit.astype(BF16)
        return carry

    lax.fori_loop(0, protos // 128, proto_norm, 0)

    def chunk(c):
        return slice(c * 128, (c + 1) * 128)

    def total_of(ref, count):
        acc = ref[0]
        for i in range(1, count):
            acc = acc + ref[i]
        return acc

    def start_all(ref, me, count, ids, send, recv):
        copies = []
        for d in range(1, count):
            copy = remote(ref.at[me], ref.at[me], send.at[d], recv.at[d], ids(d))
            copy.start()
            copies.append(copy)
        return copies

    zero = jnp.zeros((8, 128), F32)

    def put_cols(it, v, cols):
        for c in range(lane_chunks):
            col_z[it, v, me_z, c:c + 1, :] = jnp.sum(cols[c], axis=0, keepdims=True)
        return start_all(col_z.at[it, v], me_z, n_z, z_id, col_send.at[it, v], col_sem.at[it, v])

    def lane_sums(block):
        return jnp.sum(block.T, axis=0, keepdims=True)

    def spread(values, v, target):
        for i in range(view_blocks):
            at = slice(v * clips + i * 128, v * clips + (i + 1) * 128)
            target[at, :] = jnp.broadcast_to(values[i:i + 1, :], (128, 128)).T

    pending = []
    counter = [0]

    def send(src, dst, device):
        n = counter[0]
        counter[0] += 1
        copy = remote(src, dst, out_sem.at[n], in_sem.at[n], device)
        copy.start()
        pending.append(copy)
        return copy

    def add_to(ref, value):
        ref[...] = ref[...] + value

    x, y = me_p // 4, me_p % 4
    x_next = {"proto": (x + 1) % 4 * 4 + y}
    x_prev = {"proto": (x + 3) % 4 * 4 + y}
    y_next = {"proto": x * 4 + (y + 1) % 4}
    y_prev = {"proto": x * 4 + (y + 3) % 4}
    z_next, z_prev = z_id(1), z_id(n_z - 1)

    class Scatter4:
        def __init__(self, view, me, ahead, behind, buf):
            self.view, self.me, self.ahead, self.behind, self.buf = view, me, ahead, behind, buf
            self.c = {}

        def send(self, slot, dest, part):
            device = self.ahead if slot < 3 else self.behind
            self.c[slot] = send(self.view(dest, part), self.buf.at[slot], device)

        def start(self):
            m = self.me
            self.send(0, (m + 2) % 4, 0)
            self.send(3, (m + 2) % 4, 1)
            self.send(1, (m + 1) % 4, 1)
            self.send(4, (m + 3) % 4, 0)

        def mid(self):
            m = self.me
            self.c[0].wait_recv()
            add_to(self.view((m + 1) % 4, 0), self.buf[0])
            self.send(2, (m + 1) % 4, 0)
            self.c[3].wait_recv()
            add_to(self.view((m + 3) % 4, 1), self.buf[3])
            self.send(5, (m + 3) % 4, 1)

        def finish(self):
            for slot in (1, 4, 2, 5):
                self.c[slot].wait_recv()
            add_to(self.view(self.me, 0), self.buf[2] + self.buf[4])
            add_to(self.view(self.me, 1), self.buf[1] + self.buf[5])

    class Gather4:
        def __init__(self, view, me, ahead, behind):
            self.view, self.me, self.ahead, self.behind = view, me, ahead, behind
            self.c = {}

        def send(self, slot, owner, part):
            spot = self.view(owner, part)
            self.c[slot] = send(spot, spot, self.ahead if slot < 3 else self.behind)

        def start(self):
            self.send(0, self.me, 0)
            self.send(3, self.me, 1)
            self.send(1, self.me, 1)
            self.send(4, self.me, 0)

        def mid(self):
            self.c[0].wait_recv()
            self.send(2, (self.me + 3) % 4, 0)
            self.c[3].wait_recv()
            self.send(5, (self.me + 1) % 4, 1)

        def finish(self):
            for slot in (1, 4, 2, 5):
                self.c[slot].wait_recv()

    def quarter(half, part):
        return pl.ds(half * 64 + part * 32, 32)

    def along_x(ref, half):
        return lambda at, part: ref.at[at, :, quarter(half, part), :]

    def along_y(ref, half):
        return lambda at, part: ref.at[:, at, quarter(half, part), :]

    def in_x(ref, half):
        return lambda at, part: ref.at[at, y, quarter(half, part), :]

    def in_y(ref, half):
        return lambda at, part: ref.at[x, at, quarter(half, part), :]

    class Both:
        def __init__(self, *rings):
            self.rings = rings

        def start(self):
            for ring in self.rings:
                ring.start()

        def mid(self):
            for ring in self.rings:
                ring.mid()

        def finish(self):
            for ring in self.rings:
                ring.finish()

    def scatter(ref):
        return (
            Both(Scatter4(along_x(ref, 0), x, x_next, x_prev, rs_buf.at[0]),
                 Scatter4(along_y(ref, 1), y, y_next, y_prev, rs_buf.at[1])),
            Both(Scatter4(in_y(ref, 0), y, y_next, y_prev, rs_small.at[0]),
                 Scatter4(in_x(ref, 1), x, x_next, x_prev, rs_small.at[1])))

    def gather(ref):
        return (
            Both(Gather4(in_y(ref, 0), y, y_next, y_prev),
                 Gather4(in_x(ref, 1), x, x_next, x_prev)),
            Both(Gather4(along_x(ref, 0), x, x_next, x_prev),
                 Gather4(along_y(ref, 1), y, y_next, y_prev)))

    hops = (4, 3, 3, 2, 2, 1, 1)
    split = 1
    units = len(hops) * split
    back = 2 * split

    class ScatterZ:
        def __init__(self):
            self.c = {}

        def view(self, dest, way, i):
            part = i // split % 2 ^ way
            return dc_half.at[dest, pl.ds(part * 128 + i % split * (128 // split), 128 // split), :]

        def step(self, i):
            for way in (0, 1):
                hop = hops[i // split]
                spot = self.view((me_z + (n_z - hop if way else hop)) % n_z, way, i)
                if i >= back:
                    self.c[way, i - back].wait_recv()
                    add_to(spot, z_buf[way, i - back])
                self.c[way, i] = send(spot, z_buf.at[way, i], z_prev if way else z_next)

        def finish(self):
            for i in range(units - back, units):
                for way in (0, 1):
                    self.c[way, i].wait_recv()
                    add_to(self.view(me_z, way, i), z_buf[way, i])

    class GatherZ:
        def __init__(self):
            self.c = {}
            self.p = []

        def view(self, owner, way, i):
            part = i // split % 2 ^ way
            return agw.at[core * n_z + owner, pl.ds(part * 64 + i % split * (64 // split), 64 // split), :]

        def relay(self, way, i):
            self.c[way, i].wait_recv()
            far = i // split // 2 + 1
            spot = self.view((me_z + (far if way else n_z - far)) % n_z, way, i)
            return spot

        def step(self, i):
            for way in (0, 1):
                if i >= back:
                    spot = self.relay(way, i - back)
                else:
                    spot = self.view(me_z, way, i)
                self.c[way, i] = send(spot, spot, z_prev if way else z_next)
                if i >= back:
                    self.p.append(send(spot, spot, partner))

        def own(self):
            spot = agw.at[core * n_z + me_z]
            self.p.append(send(spot, spot, partner))

        def finish(self):
            for i in range(units - back, units):
                for way in (0, 1):
                    spot = self.relay(way, i)
                    self.p.append(send(spot, spot, partner))


    step_m, step_w = 256, 512

    def first_pass(v):
        def step(i, cols):
            at = pl.ds(pl.multiple_of(i * step_m, step_m), step_m)
            glob = pl.ds(pl.multiple_of(v * clips + i * step_m, step_m), step_m)
            unit, _ = normalized(embeds[v][at, :].astype(F32))
            ub = unit.astype(BF16)
            unit_b[glob, :] = ub
            den = jnp.zeros((step_m, 128), F32)
            cols = list(cols)
            for k in range(protos // step_w):
                score = lax.dot_general(
                    ub, proto_b[k * step_w:(k + 1) * step_w, :],
                    (((1,), (1,)), ((), ())), preferred_element_type=F32)
                soft = jnp.exp(score * 10.0)
                code = soft * soft
                table[glob, k * step_w:(k + 1) * step_w] = code
                for j in range(step_w // 128):
                    den = den + soft[:, chunk(j)]
                    c = k * (step_w // 128) + j
                    cols[c] = cols[c] + fold8(code[:, chunk(j)])
            for j in range(step_m // 128):
                den_recv[me_p, pl.ds(v * view_blocks + i * (step_m // 128) + j, 1), :] = lane_sums(den[chunk(j), :])
            return tuple(cols)

        return lax.fori_loop(0, clips // step_m, step, (zero,) * lane_chunks)

    def cols_pass(v):
        def step(i, cols):
            at = pl.ds(pl.multiple_of(v * clips + i * 64, 64), 64)
            s = clip_b[at, :]
            return tuple(cols[c] + fold8(table[at, chunk(c)] * s) for c in range(lane_chunks))

        return lax.fori_loop(0, clips // 64, step, (zero,) * lane_chunks)

    def rows_pass(it, v):
        def step(i, carry):
            for j in range(2):
                block = 2 * i + j
                at = pl.ds(pl.multiple_of(v * clips + block * 128, 128), 128)
                acc = jnp.zeros((128, 128), F32)
                for c in range(lane_chunks):
                    acc = acc + table[at, chunk(c)] * scale[v, c:c + 1, :]
                row_recv[it, v, me_p, pl.ds(block, 1), :] = lane_sums(acc)
            return carry

        lax.fori_loop(0, view_blocks // 2, step, 0)
        return start_all(row_recv.at[it, v], me_p, n_p, p_id, row_send.at[it, v], row_sem.at[it, v])

    def wait_all(copies):
        for copy in copies:
            copy.wait_recv()
        sends.extend(copies)

    def pair_start(it, v, copies):
        wait_all(copies)
        pair = col_pair.at[it, v]
        pair[core] = total_of(col_z.at[it, v], n_z)
        copy = remote(pair.at[core], pair.at[core], colp_send.at[it, v], colp_sem.at[it, v], partner)
        copy.start()
        return copy

    sends = []
    z_copies = [None, None]
    row_copies = [None, None]
    z_cols = first_pass(0)
    pl.semaphore_wait(barrier, n_p - 1 + 2 * n_z - 1)
    z_copies[0] = put_cols(0, 0, z_cols)
    z_copies[1] = put_cols(0, 1, first_pass(1))
    den_copies = start_all(den_recv, me_p, n_p, p_id, den_send, den_sem)

    def transpose_unit(i, carry):
        at = pl.ds(pl.multiple_of(i * 128, 128), 128)
        unit_t[:, at] = unit_b[at, :].astype(F32).T.astype(BF16)
        return carry

    lax.fori_loop(0, row_blocks, transpose_unit, 0)

    def grad_rows(v, first, count):
        w = 1 - v
        mine = pl.ds(pl.multiple_of(v * clips + first, count), count)
        other = pl.ds(pl.multiple_of(w * clips + first, count), count)
        soft_scale = soft_b[mine, :]
        code_scale = code_b[other, :]
        for c in range(lane_chunks):
            e = table[mine, chunk(c)]
            code = table[other, chunk(c)] * scale[w, c:c + 1, :] * code_scale
            grads[mine, chunk(c)] = (e * lax.rsqrt(e) * soft_scale - code).astype(BF16)

    def du_rows(v, i):
        at = pl.ds(pl.multiple_of(v * clips + i * 256, 256), 256)
        out = jnp.dot(grads[at, :], proto_b[...], preferred_element_type=F32)
        owner = v * (n_p // 2) + 2 * i
        du[owner // 4, pl.ds(owner % 4, 2)] = out.reshape(2, 128, width)

    def grad_pass(v, dots=None):
        def step(i, carry):
            if dots is not None:
                du_rows(dots, i)
            for j in range(4):
                grad_rows(v, i * 256 + j * 64, 64)
            return carry

        lax.fori_loop(0, clips // 256, step, 0)

    def du_dot(v):
        def step(i, carry):
            du_rows(v, i)
            return carry

        lax.fori_loop(0, clips // 256, step, 0)

    for it in range(ITERS):
        pairs = [pair_start(it, v, z_copies[v]) for v in range(2)]
        for v in range(2):
            wait_all([pairs[v]])
            scale[v] = 1.0 / (protos_all * (col_pair[it, v, 0] + col_pair[it, v, 1]))
            row_copies[v] = rows_pass(it, v)
        if it == 0:
            wait_all(den_copies)
            soft = 10.0 / total_of(den_recv, n_p)
            for v in range(2):
                spread(soft[v * view_blocks:(v + 1) * view_blocks], v, soft_b)
        for v in range(2):
            wait_all(row_copies[v])
            row_sum = total_of(row_recv.at[it, v], n_p)
            if it < ITERS - 1:
                spread(1.0 / (clips_all * row_sum), v, clip_b)
                z_copies[v] = put_cols(it + 1, v, cols_pass(v))
            else:
                spread(10.0 / row_sum, v, code_b)
                grad_pass(1 - v, 1 if v == 1 else None)

    def project(grad, raw):
        unit, inverse = normalized(raw)
        along = jnp.sum(unit * grad, axis=-1, keepdims=True)
        return (grad - unit * along) * inverse

    def lanes_square(block):
        sq = block * block
        return jnp.sum(sq[:, :128] + sq[:, 128:], axis=0, keepdims=True)

    theirs = (1 - core) * n_z

    def pair_piece(i):
        return remote(
            dct.at[pl.ds(theirs + 2 * i, 2)], dc_pair.at[pl.ds(2 * i, 2)],
            pair_out.at[i], pair_in.at[i], partner)

    def dc_dot(first_chunk, sending):
        def step(i, carry):
            c = first_chunk + 2 * i
            at = pl.ds(pl.multiple_of(c * 128, 256), 256)
            out = jnp.dot(unit_t[...], grads[:, at], preferred_element_type=F32)
            dct[c] = out[:, :128]
            dct[c + 1] = out[:, 128:]
            if sending:
                pair_piece(i).start()
            return carry

        lax.fori_loop(0, n_z // 2, step, 0)

    r1, r2 = scatter(du)
    g1, g2 = gather(agx)
    zs, zg = ScatterZ(), GatherZ()
    du_dot(0)
    r1.start()
    dc_dot(theirs, True)
    dc_dot(core * n_z, False)
    for i in range(n_z // 2):
        pair_piece(i).wait_recv()
        for j in (2 * i, 2 * i + 1):
            dc_half[j] = dct[core * n_z + j] + dc_pair[j]
    zs.step(0)
    zs.step(1)
    r1.mid()
    zs.step(2)
    zs.step(3)
    zs.step(4)
    r1.finish()
    r2.start()
    zs.step(5)
    zs.step(6)
    r2.mid()
    r2.finish()
    at = pl.ds(pl.multiple_of((me_p % view_blocks) * 128, 128), 128)
    raw = jnp.where(me_p < view_blocks, slow_ref[at, :].astype(F32), fast_ref[at, :].astype(F32))
    dx_own = project(du[x, y], raw)
    agx[x, y] = dx_own
    g1.start()
    zs.finish()
    mine = core * n_z + me_z
    dw_own = project(dc_half[me_z].T, proto_ref[pl.ds(pl.multiple_of(mine * 128, 128), 128), :])
    agw[mine] = dw_own
    zg.step(0)
    zg.step(1)
    zg.own()
    sq_p[me_p, 0:1, :] = lanes_square(dw_own)
    sq_p[me_p, 1:2, :] = lanes_square(dx_own)
    sq_p[me_p, 2:8, :] = jnp.zeros((6, 128), F32)
    sq_copies = start_all(sq_p, me_p, n_p, p_id, send_sem, sqp_sem)
    g1.mid()
    zg.step(2)
    g1.finish()
    g2.start()
    zg.step(3)
    zg.step(4)
    wait_all(sq_copies)
    sq_z[batch_me] = total_of(sq_p, n_p)
    sq_copies = start_all(sq_z, batch_me, 2 * n_z, b_id, sqz_send, sqz_sem)
    zg.step(5)
    g2.mid()
    zg.step(6)
    zg.finish()
    wait_all(sq_copies)
    square = jnp.sum(total_of(sq_z, 2 * n_z), axis=1, keepdims=True)
    entries = float(protos_all * width), float(2 * clips_all * width)
    for i, out in enumerate((wf_ref, xf_ref)):
        out[...] = jnp.broadcast_to(
            lax.rsqrt(square[i:i + 1, :] / entries[i] + NORM_EPS), (8, width))
    g2.finish()
    for copy in zg.p:
        copy.wait_recv()
    for i in range(n_z // 2):
        pair_piece(i).wait_send()
    for copy in pending + sends:
        copy.wait_send()


def body(slow_embed, fast_embed, prototypes):
    clips, width = slow_embed.shape
    protos = prototypes.shape[0]
    n_b = lax.axis_size("batch")
    n_p = lax.axis_size("proto")
    n_z = n_b // 2
    rows = 2 * clips
    DMA = pltpu.SemaphoreType.DMA
    vmem = pltpu.VMEM
    lane_chunks = protos // 128
    row_blocks = rows // 128
    scratch = [
        vmem((rows, protos), F32),
        vmem((rows, protos), BF16),
        vmem((rows, width), BF16),
        vmem((width, rows), BF16),
        vmem((protos, width), BF16),
        vmem((2, lane_chunks, 128), F32),
        vmem((rows, 128), F32),
        vmem((rows, 128), F32),
        vmem((rows, 128), F32),
        vmem((4, 4, 128, width), F32),
        vmem((lane_chunks, width, 128), F32),
        vmem((n_z, width, 128), F32),
        vmem((n_z, width, 128), F32),
        vmem((2, 6, 4, 32, width), F32),
        vmem((2, 6, 32, width), F32),
        vmem((2, 7, 128, 128), F32),
        vmem((ITERS, 2, n_z, lane_chunks, 128), F32),
        vmem((ITERS, 2, 2, lane_chunks, 128), F32),
        vmem((ITERS, 2, n_p, row_blocks // 2, 128), F32),
        vmem((n_p, row_blocks, 128), F32),
        vmem((n_p, 8, 128), F32),
        vmem((n_b, 8, 128), F32),
        DMA((16,)), DMA((ITERS, 2, n_z)), DMA((ITERS, 2, n_z)), DMA((ITERS, 2)), DMA((ITERS, 2)),
        DMA((ITERS, 2, n_p)), DMA((ITERS, 2, n_p)),
        DMA((n_p,)), DMA((n_p,)),
        DMA((n_p,)), DMA((n_b,)), DMA((n_b,)), DMA((n_z // 2,)), DMA((n_z // 2,)),
        DMA((COPIES,)), DMA((COPIES,)),
    ]
    whole = pl.BlockSpec(memory_space=pltpu.VMEM)
    dw, dx, dw_factor, dx_factor = pl.pallas_call(
        functools.partial(kernel, (clips, protos, width, n_z, n_p)),
        out_shape=(
            vmem((lane_chunks, 128, width), F32),
            vmem((4, 4, 128, width), F32),
            vmem((8, width), F32),
            vmem((8, width), F32),
        ),
        in_specs=[whole] * 3,
        out_specs=(whole,) * 4,
        scratch_shapes=scratch,
        compiler_params=pltpu.CompilerParams(
            collective_id=0, has_side_effects=True, vmem_limit_bytes=56 * 2**20),
        name="swav",
    )(slow_embed, fast_embed, prototypes)

    def scaled(array, factor, rows):
        return (array.reshape(rows // 8, 8, width) * factor).reshape(rows, width)

    return (
        scaled(dw, dw_factor, protos),
        scaled(dx[:2], dx_factor, clips),
        scaled(dx[2:], dx_factor, clips),
    )


def solution(mesh):
    placed = (P("batch", None), P("batch", None), P("proto", None))
    return jax.shard_map(
        body,
        mesh=mesh,
        in_specs=placed,
        out_specs=(P("proto", None), P("batch", None), P("batch", None)),
        check_vma=False,
    )
```

```python
import functools

import jax
import jax.numpy as jnp
from jax import lax
from jax.experimental import pallas as pl
from jax.experimental.pallas import tpu as pltpu
from jax.sharding import PartitionSpec as P

ITERS = 3
COPIES = 192
EXPONENT = 10.0 * 1.4426950408889634
NORM_EPS = 1e-06
MESH = pl.DeviceIdType.MESH
F32 = jnp.float32
BF16 = jnp.bfloat16


def normalized(rows):
    total = jnp.sum(rows * rows, axis=-1, keepdims=True) + 1e-12
    inverse = 1.0 / jnp.sqrt(total)
    return rows * inverse, inverse


def fold8(block):
    rows, lanes = block.shape
    return jnp.sum(block.reshape(rows // 8, 8, lanes), axis=0)


def kernel(
    dims,
    slow_ref, fast_ref, proto_ref,
    agw, agx, wf_ref, xf_ref,
    table, grads, unit_b, unit_t, proto_b, scale, clip_b, soft_b, code_b,
    du, dct, dc_pair, dc_half, rs_buf, rs_small, z_buf,
    col_z, col_pair, row_recv, den_recv, sq_p, sq_z,
    send_sem, col_send, col_sem, colp_send, colp_sem, row_send, row_sem, den_sem, den_send,
    sqp_sem, sqz_sem, sqz_send, pair_out, pair_in, out_sem, in_sem,
):
    clips, protos, width, n_z, n_p = dims
    batch_me = lax.axis_index("batch")
    me_p = lax.axis_index("proto")
    me_z = batch_me // 2
    core = batch_me % 2
    clips_all = clips * 2 * n_z
    protos_all = protos * n_p
    rows = 2 * clips
    lane_chunks = protos // 128
    row_blocks = rows // 128
    view_blocks = clips // 128
    embeds = (slow_ref, fast_ref)

    def p_id(d):
        return {"proto": (me_p + d) % n_p}

    def z_id(d):
        return {"batch": ((me_z + d) % n_z) * 2 + core}

    def b_id(d):
        return {"batch": (batch_me + d) % (2 * n_z)}

    partner = {"batch": me_z * 2 + 1 - core}

    def remote(src, dst, send, recv, device):
        return pltpu.make_async_remote_copy(
            src_ref=src, dst_ref=dst, send_sem=send, recv_sem=recv,
            device_id=device, device_id_type=MESH,
        )

    barrier = pltpu.get_barrier_semaphore()
    for d in range(1, n_p):
        pl.semaphore_signal(barrier, inc=1, device_id=p_id(d), device_id_type=MESH)
    for d in range(1, 2 * n_z):
        pl.semaphore_signal(barrier, inc=1, device_id=b_id(d), device_id_type=MESH)

    def proto_norm(i, carry):
        at = pl.ds(pl.multiple_of(i * 128, 128), 128)
        unit, _ = normalized(proto_ref[at, :])
        proto_b[at, :] = unit.astype(BF16)
        return carry

    lax.fori_loop(0, protos // 128, proto_norm, 0)

    def chunk(c):
        return slice(c * 128, (c + 1) * 128)

    def total_of(ref, count):
        acc = ref[0]
        for i in range(1, count):
            acc = acc + ref[i]
        return acc

    def start_all(ref, me, count, ids, send, recv):
        copies = []
        for d in range(1, count):
            copy = remote(ref.at[me], ref.at[me], send.at[d], recv.at[d], ids(d))
            copy.start()
            copies.append(copy)
        return copies

    zero = jnp.zeros((8, 128), F32)

    def put_cols(it, v, cols):
        for c in range(lane_chunks):
            col_z[it, v, me_z, c:c + 1, :] = jnp.sum(cols[c], axis=0, keepdims=True)
        return start_all(col_z.at[it, v], me_z, n_z, z_id, col_send.at[it, v], col_sem.at[it, v])

    def lane_sums(block):
        return jnp.sum(block.T, axis=0, keepdims=True)

    def spread(values, v, target):
        for i in range(view_blocks):
            at = slice(v * clips + i * 128, v * clips + (i + 1) * 128)
            target[at, :] = jnp.broadcast_to(values[i:i + 1, :], (128, 128)).T

    pending = []
    counter = [0]

    def send(src, dst, device):
        n = counter[0]
        counter[0] += 1
        copy = remote(src, dst, out_sem.at[n], in_sem.at[n], device)
        copy.start()
        pending.append(copy)
        return copy

    def add_to(ref, value):
        ref[...] = ref[...] + value

    x, y = me_p // 4, me_p % 4
    x_next = {"proto": (x + 1) % 4 * 4 + y}
    x_prev = {"proto": (x + 3) % 4 * 4 + y}
    y_next = {"proto": x * 4 + (y + 1) % 4}
    y_prev = {"proto": x * 4 + (y + 3) % 4}
    z_next, z_prev = z_id(1), z_id(n_z - 1)

    class Scatter4:
        def __init__(self, view, me, ahead, behind, buf):
            self.view, self.me, self.ahead, self.behind, self.buf = view, me, ahead, behind, buf
            self.c = {}

        def send(self, slot, dest, part):
            device = self.ahead if slot < 3 else self.behind
            self.c[slot] = send(self.view(dest, part), self.buf.at[slot], device)

        def start(self):
            m = self.me
            self.send(0, (m + 2) % 4, 0)
            self.send(3, (m + 2) % 4, 1)
            self.send(1, (m + 1) % 4, 1)
            self.send(4, (m + 3) % 4, 0)

        def mid(self):
            m = self.me
            self.c[0].wait_recv()
            add_to(self.view((m + 1) % 4, 0), self.buf[0])
            self.send(2, (m + 1) % 4, 0)
            self.c[3].wait_recv()
            add_to(self.view((m + 3) % 4, 1), self.buf[3])
            self.send(5, (m + 3) % 4, 1)

        def finish(self):
            for slot in (1, 4, 2, 5):
                self.c[slot].wait_recv()
            add_to(self.view(self.me, 0), self.buf[2] + self.buf[4])
            add_to(self.view(self.me, 1), self.buf[1] + self.buf[5])

    class Gather4:
        def __init__(self, view, me, ahead, behind):
            self.view, self.me, self.ahead, self.behind = view, me, ahead, behind
            self.c = {}

        def send(self, slot, owner, part):
            spot = self.view(owner, part)
            self.c[slot] = send(spot, spot, self.ahead if slot < 3 else self.behind)

        def start(self):
            self.send(0, self.me, 0)
            self.send(3, self.me, 1)
            self.send(1, self.me, 1)
            self.send(4, self.me, 0)

        def mid(self):
            self.c[0].wait_recv()
            self.send(2, (self.me + 3) % 4, 0)
            self.c[3].wait_recv()
            self.send(5, (self.me + 1) % 4, 1)

        def finish(self):
            for slot in (1, 4, 2, 5):
                self.c[slot].wait_recv()

    def quarter(half, part):
        return pl.ds(half * 64 + part * 32, 32)

    def along_x(ref, half):
        return lambda at, part: ref.at[at, :, quarter(half, part), :]

    def along_y(ref, half):
        return lambda at, part: ref.at[:, at, quarter(half, part), :]

    def in_x(ref, half):
        return lambda at, part: ref.at[at, y, quarter(half, part), :]

    def in_y(ref, half):
        return lambda at, part: ref.at[x, at, quarter(half, part), :]

    class Both:
        def __init__(self, *rings):
            self.rings = rings

        def start(self):
            for ring in self.rings:
                ring.start()

        def mid(self):
            for ring in self.rings:
                ring.mid()

        def finish(self):
            for ring in self.rings:
                ring.finish()

    def scatter(ref):
        return (
            Both(Scatter4(along_x(ref, 0), x, x_next, x_prev, rs_buf.at[0]),
                 Scatter4(along_y(ref, 1), y, y_next, y_prev, rs_buf.at[1])),
            Both(Scatter4(in_y(ref, 0), y, y_next, y_prev, rs_small.at[0]),
                 Scatter4(in_x(ref, 1), x, x_next, x_prev, rs_small.at[1])))

    def gather(ref):
        return (
            Both(Gather4(in_y(ref, 0), y, y_next, y_prev),
                 Gather4(in_x(ref, 1), x, x_next, x_prev)),
            Both(Gather4(along_x(ref, 0), x, x_next, x_prev),
                 Gather4(along_y(ref, 1), y, y_next, y_prev)))

    hops = (4, 3, 3, 2, 2, 1, 1)
    split = 1
    units = len(hops) * split
    back = 2 * split

    class ScatterZ:
        def __init__(self):
            self.c = {}

        def view(self, dest, way, i):
            part = i // split % 2 ^ way
            return dc_half.at[dest, pl.ds(part * 128 + i % split * (128 // split), 128 // split), :]

        def step(self, i):
            for way in (0, 1):
                hop = hops[i // split]
                spot = self.view((me_z + (n_z - hop if way else hop)) % n_z, way, i)
                if i >= back:
                    self.c[way, i - back].wait_recv()
                    add_to(spot, z_buf[way, i - back])
                self.c[way, i] = send(spot, z_buf.at[way, i], z_prev if way else z_next)

        def finish(self):
            for i in range(units - back, units):
                for way in (0, 1):
                    self.c[way, i].wait_recv()
                    add_to(self.view(me_z, way, i), z_buf[way, i])

    class GatherZ:
        def __init__(self):
            self.c = {}
            self.p = []

        def view(self, owner, way, i):
            part = i // split % 2 ^ way
            return agw.at[core * n_z + owner, pl.ds(part * 64 + i % split * (64 // split), 64 // split), :]

        def relay(self, way, i):
            self.c[way, i].wait_recv()
            far = i // split // 2 + 1
            spot = self.view((me_z + (far if way else n_z - far)) % n_z, way, i)
            return spot

        def step(self, i):
            for way in (0, 1):
                if i >= back:
                    spot = self.relay(way, i - back)
                else:
                    spot = self.view(me_z, way, i)
                self.c[way, i] = send(spot, spot, z_prev if way else z_next)
                if i >= back:
                    self.p.append(send(spot, spot, partner))

        def own(self):
            spot = agw.at[core * n_z + me_z]
            self.p.append(send(spot, spot, partner))

        def finish(self):
            for i in range(units - back, units):
                for way in (0, 1):
                    spot = self.relay(way, i)
                    self.p.append(send(spot, spot, partner))


    step_m, step_w = 512, 512

    def first_pass(v):
        def step(i, cols):
            at = pl.ds(pl.multiple_of(i * step_m, step_m), step_m)
            glob = pl.ds(pl.multiple_of(v * clips + i * step_m, step_m), step_m)
            unit, _ = normalized(embeds[v][at, :].astype(F32))
            ub = unit.astype(BF16)
            unit_b[glob, :] = ub
            cols = list(cols)
            for k in range(protos // step_w):
                score = lax.dot_general(
                    ub, proto_b[k * step_w:(k + 1) * step_w, :],
                    (((1,), (1,)), ((), ())), preferred_element_type=F32)
                soft = jnp.exp2(score * EXPONENT)
                code = soft * soft
                table[glob, k * step_w:(k + 1) * step_w] = code
                for j in range(step_w // 128):
                    c = k * (step_w // 128) + j
                    cols[c] = cols[c] + fold8(code[:, chunk(j)])
            return tuple(cols)

        return lax.fori_loop(0, clips // step_m, step, (zero,) * lane_chunks)

    def cols_pass(v):
        def step(i, cols):
            at = pl.ds(pl.multiple_of(v * clips + i * 64, 64), 64)
            s = clip_b[at, :]
            return tuple(cols[c] + fold8(table[at, chunk(c)] * s) for c in range(lane_chunks))

        return lax.fori_loop(0, clips // 64, step, (zero,) * lane_chunks)

    def rows_pass(it, v):
        def step(i, carry):
            for j in range(2):
                block = 2 * i + j
                at = pl.ds(pl.multiple_of(v * clips + block * 128, 128), 128)
                acc = jnp.zeros((128, 128), F32)
                for c in range(lane_chunks):
                    acc = acc + table[at, chunk(c)] * scale[v, c:c + 1, :]
                row_recv[it, v, me_p, pl.ds(block, 1), :] = lane_sums(acc)
            return carry

        lax.fori_loop(0, view_blocks // 2, step, 0)
        return start_all(row_recv.at[it, v], me_p, n_p, p_id, row_send.at[it, v], row_sem.at[it, v])

    def wait_all(copies):
        for copy in copies:
            copy.wait_recv()
        sends.extend(copies)

    def pair_start(it, v, copies):
        wait_all(copies)
        pair = col_pair.at[it, v]
        pair[core] = total_of(col_z.at[it, v], n_z)
        copy = remote(pair.at[core], pair.at[core], colp_send.at[it, v], colp_sem.at[it, v], partner)
        copy.start()
        return copy

    sends = []
    z_copies = [None, None]
    row_copies = [None, None]
    z_cols = first_pass(0)
    pl.semaphore_wait(barrier, n_p - 1 + 2 * n_z - 1)
    z_copies[0] = put_cols(0, 0, z_cols)
    z_copies[1] = put_cols(0, 1, first_pass(1))

    def soft_totals(i, carry):
        at = pl.ds(pl.multiple_of(i * 128, 128), 128)
        acc = jnp.zeros((128, 128), F32)
        for c in range(lane_chunks):
            e = table[at, chunk(c)]
            acc = acc + e * lax.rsqrt(e)
        den_recv[me_p, pl.ds(i, 1), :] = lane_sums(acc)
        return carry

    lax.fori_loop(0, row_blocks, soft_totals, 0)
    den_copies = start_all(den_recv, me_p, n_p, p_id, den_send, den_sem)

    def transpose_unit(i, carry):
        at = pl.ds(pl.multiple_of(i * 128, 128), 128)
        unit_t[i] = unit_b[at, :].astype(F32).T.astype(BF16)
        return carry


    def grad_rows(v, first, count):
        w = 1 - v
        mine = pl.ds(pl.multiple_of(v * clips + first, count), count)
        other = pl.ds(pl.multiple_of(w * clips + first, count), count)
        soft_scale = soft_b[mine, :]
        code_scale = code_b[other, :]
        for c in range(lane_chunks):
            e = table[mine, chunk(c)]
            code = table[other, chunk(c)] * scale[w, c:c + 1, :] * code_scale
            grads[c, mine, :] = (e * lax.rsqrt(e) * soft_scale - code).astype(BF16)

    def du_rows(v, i):
        at = pl.ds(pl.multiple_of(v * clips + i * 256, 256), 256)
        mine = jnp.concatenate([grads[c, at, :] for c in range(lane_chunks)], axis=1)
        out = jnp.dot(mine, proto_b[...], preferred_element_type=F32)
        owner = v * (n_p // 2) + 2 * i
        du[owner // 4, pl.ds(owner % 4, 2)] = out.reshape(2, 128, width)

    def grad_pass(v):
        def step(i, carry):
            for j in range(4):
                grad_rows(v, i * 256 + j * 64, 64)
            return carry

        lax.fori_loop(0, clips // 256, step, 0)

    def du_dot(v):
        def step(i, carry):
            du_rows(v, i)
            return carry

        lax.fori_loop(0, clips // 256, step, 0)

    for it in range(ITERS):
        pairs = [pair_start(it, v, z_copies[v]) for v in range(2)]
        for v in range(2):
            wait_all([pairs[v]])
            scale[v] = 1.0 / (protos_all * (col_pair[it, v, 0] + col_pair[it, v, 1]))
            row_copies[v] = rows_pass(it, v)
        if it == 0:
            lax.fori_loop(0, row_blocks, transpose_unit, 0)
        if it == 1:
            wait_all(den_copies)
            soft = 10.0 / total_of(den_recv, n_p)
            for v in range(2):
                spread(soft[v * view_blocks:(v + 1) * view_blocks], v, soft_b)
        for v in range(2):
            wait_all(row_copies[v])
            row_sum = total_of(row_recv.at[it, v], n_p)
            if it < ITERS - 1:
                spread(1.0 / (clips_all * row_sum), v, clip_b)
                z_copies[v] = put_cols(it + 1, v, cols_pass(v))
            else:
                spread(10.0 / row_sum, v, code_b)
                grad_pass(1 - v)
                if v == 0:
                    du_dot(1)

    def project(grad, raw):
        unit, inverse = normalized(raw)
        along = jnp.sum(unit * grad, axis=-1, keepdims=True)
        return (grad - unit * along) * inverse

    def lanes_square(block):
        sq = block * block
        return jnp.sum(sq[:, :128] + sq[:, 128:], axis=0, keepdims=True)

    theirs = (1 - core) * n_z

    def pair_piece(i):
        return remote(
            dct.at[pl.ds(theirs + 2 * i, 2)], dc_pair.at[pl.ds(2 * i, 2)],
            pair_out.at[i], pair_in.at[i], partner)

    def dc_dot(first_chunk, sending):
        def step(i, carry):
            c = first_chunk + 2 * i
            units_t = jnp.concatenate([unit_t[j] for j in range(row_blocks)], axis=1)
            pair = jnp.concatenate([grads[c], grads[c + 1]], axis=1)
            out = jnp.dot(units_t, pair, preferred_element_type=F32)
            dct[c] = out[:, :128]
            dct[c + 1] = out[:, 128:]
            if sending:
                pair_piece(i).start()
            return carry

        lax.fori_loop(0, n_z // 2, step, 0)

    r1, r2 = scatter(du)
    g1, g2 = gather(agx)
    zs, zg = ScatterZ(), GatherZ()
    du_dot(0)
    r1.start()
    dc_dot(theirs, True)
    dc_dot(core * n_z, False)
    for i in range(n_z // 2):
        pair_piece(i).wait_recv()
        for j in (2 * i, 2 * i + 1):
            dc_half[j] = dct[core * n_z + j] + dc_pair[j]
    zs.step(0)
    zs.step(1)
    r1.mid()
    zs.step(2)
    zs.step(3)
    zs.step(4)
    r1.finish()
    r2.start()
    zs.step(5)
    zs.step(6)
    r2.mid()
    r2.finish()
    at = pl.ds(pl.multiple_of((me_p % view_blocks) * 128, 128), 128)
    raw = jnp.where(me_p < view_blocks, slow_ref[at, :].astype(F32), fast_ref[at, :].astype(F32))
    dx_own = project(du[x, y], raw)
    agx[x, y] = dx_own
    g1.start()
    zs.finish()
    mine = core * n_z + me_z
    dw_own = project(dc_half[me_z].T, proto_ref[pl.ds(pl.multiple_of(mine * 128, 128), 128), :])
    agw[mine] = dw_own
    zg.step(0)
    zg.step(1)
    zg.own()
    sq_p[me_p, 0:1, :] = lanes_square(dw_own)
    sq_p[me_p, 1:2, :] = lanes_square(dx_own)
    sq_p[me_p, 2:8, :] = jnp.zeros((6, 128), F32)
    sq_copies = start_all(sq_p, me_p, n_p, p_id, send_sem, sqp_sem)
    g1.mid()
    zg.step(2)
    g1.finish()
    g2.start()
    zg.step(3)
    zg.step(4)
    wait_all(sq_copies)
    sq_z[batch_me] = total_of(sq_p, n_p)
    sq_copies = start_all(sq_z, batch_me, 2 * n_z, b_id, sqz_send, sqz_sem)
    zg.step(5)
    g2.mid()
    zg.step(6)
    zg.finish()
    wait_all(sq_copies)
    square = jnp.sum(total_of(sq_z, 2 * n_z), axis=1, keepdims=True)
    entries = float(protos_all * width), float(2 * clips_all * width)
    for i, out in enumerate((wf_ref, xf_ref)):
        out[...] = jnp.broadcast_to(
            lax.rsqrt(square[i:i + 1, :] / entries[i] + NORM_EPS), (8, width))
    g2.finish()
    for copy in zg.p:
        copy.wait_recv()
    for i in range(n_z // 2):
        pair_piece(i).wait_send()
    for copy in pending + sends:
        copy.wait_send()


def body(slow_embed, fast_embed, prototypes):
    clips, width = slow_embed.shape
    protos = prototypes.shape[0]
    n_b = lax.axis_size("batch")
    n_p = lax.axis_size("proto")
    n_z = n_b // 2
    rows = 2 * clips
    DMA = pltpu.SemaphoreType.DMA
    vmem = pltpu.VMEM
    lane_chunks = protos // 128
    row_blocks = rows // 128
    scratch = [
        vmem((rows, protos), F32),
        vmem((lane_chunks, rows, 128), BF16),
        vmem((rows, width), BF16),
        vmem((row_blocks, width, 128), BF16),
        vmem((protos, width), BF16),
        vmem((2, lane_chunks, 128), F32),
        vmem((rows, 128), F32),
        vmem((rows, 128), F32),
        vmem((rows, 128), F32),
        vmem((4, 4, 128, width), F32),
        vmem((lane_chunks, width, 128), F32),
        vmem((n_z, width, 128), F32),
        vmem((n_z, width, 128), F32),
        vmem((2, 6, 4, 32, width), F32),
        vmem((2, 6, 32, width), F32),
        vmem((2, 7, 128, 128), F32),
        vmem((ITERS, 2, n_z, lane_chunks, 128), F32),
        vmem((ITERS, 2, 2, lane_chunks, 128), F32),
        vmem((ITERS, 2, n_p, row_blocks // 2, 128), F32),
        vmem((n_p, row_blocks, 128), F32),
        vmem((n_p, 8, 128), F32),
        vmem((n_b, 8, 128), F32),
        DMA((16,)), DMA((ITERS, 2, n_z)), DMA((ITERS, 2, n_z)), DMA((ITERS, 2)), DMA((ITERS, 2)),
        DMA((ITERS, 2, n_p)), DMA((ITERS, 2, n_p)),
        DMA((n_p,)), DMA((n_p,)),
        DMA((n_p,)), DMA((n_b,)), DMA((n_b,)), DMA((n_z // 2,)), DMA((n_z // 2,)),
        DMA((COPIES,)), DMA((COPIES,)),
    ]
    whole = pl.BlockSpec(memory_space=pltpu.VMEM)
    dw, dx, dw_factor, dx_factor = pl.pallas_call(
        functools.partial(kernel, (clips, protos, width, n_z, n_p)),
        out_shape=(
            vmem((lane_chunks, 128, width), F32),
            vmem((4, 4, 128, width), F32),
            vmem((8, width), F32),
            vmem((8, width), F32),
        ),
        in_specs=[whole] * 3,
        out_specs=(whole,) * 4,
        scratch_shapes=scratch,
        compiler_params=pltpu.CompilerParams(
            collective_id=0, has_side_effects=True, vmem_limit_bytes=56 * 2**20),
        name="swav",
    )(slow_embed, fast_embed, prototypes)

    def scaled(array, factor, rows):
        return (array.reshape(rows // 8, 8, width) * factor).reshape(rows, width)

    return (
        scaled(dw, dw_factor, protos),
        scaled(dx[:2], dx_factor, clips),
        scaled(dx[2:], dx_factor, clips),
    )


def solution(mesh):
    placed = (P("batch", None), P("batch", None), P("proto", None))
    return jax.shard_map(
        body,
        mesh=mesh,
        in_specs=placed,
        out_specs=(P("proto", None), P("batch", None), P("batch", None)),
        check_vma=False,
    )
```

```python
import functools

import jax
import jax.numpy as jnp
from jax import lax
from jax.experimental import pallas as pl
from jax.experimental.pallas import tpu as pltpu
from jax.sharding import PartitionSpec as P

ITERS = 3
COPIES = 51
EXPONENT = 10.0 * 1.4426950408889634
NORM_EPS = 1e-06
MESH = pl.DeviceIdType.MESH
F32 = jnp.float32
BF16 = jnp.bfloat16


def normalized(rows):
    total = jnp.sum(rows * rows, axis=-1, keepdims=True) + 1e-12
    inverse = 1.0 / jnp.sqrt(total)
    return rows * inverse, inverse


def fold8(block):
    rows, lanes = block.shape
    return jnp.sum(block.reshape(rows // 8, 8, lanes), axis=0)


def kernel(
    dims,
    slow_ref, fast_ref, proto_ref,
    agw, agx, wf_ref, xf_ref,
    table, grads, unit_b, unit_t, proto_b, scale, clip_b, soft_b, code_b,
    du, dct, dc_pair, dc_half, rs_buf, rs_small, z_buf,
    col_z, col_pair, row_recv, den_recv, sq_p, sq_z,
    col_send, col_sem, colp_send, colp_sem, row_send, row_sem, small_send, small_sem,
    out_sem, in_sem,
):
    clips, protos, width, n_z, n_p = dims
    batch_me = lax.axis_index("batch")
    me_p = lax.axis_index("proto")
    me_z = batch_me // 2
    core = batch_me % 2
    clips_all = clips * 2 * n_z
    protos_all = protos * n_p
    rows = 2 * clips
    lane_chunks = protos // 128
    row_blocks = rows // 128
    view_blocks = clips // 128
    embeds = (slow_ref, fast_ref)

    def p_id(d):
        return {"proto": (me_p + d) % n_p}

    def z_id(d):
        return {"batch": ((me_z + d) % n_z) * 2 + core}

    def b_id(d):
        return {"batch": (batch_me + d) % (2 * n_z)}

    partner = {"batch": me_z * 2 + 1 - core}

    def remote(src, dst, send, recv, device):
        return pltpu.make_async_remote_copy(
            src_ref=src, dst_ref=dst, send_sem=send, recv_sem=recv,
            device_id=device, device_id_type=MESH,
        )

    barrier = pltpu.get_barrier_semaphore()
    for d in range(1, n_p):
        pl.semaphore_signal(barrier, inc=1, device_id=p_id(d), device_id_type=MESH)
    for d in range(1, 2 * n_z):
        pl.semaphore_signal(barrier, inc=1, device_id=b_id(d), device_id_type=MESH)

    def proto_norm(i, carry):
        at = pl.ds(pl.multiple_of(i * 128, 128), 128)
        unit, _ = normalized(proto_ref[at, :])
        proto_b[at, :] = unit.astype(BF16)
        return carry

    lax.fori_loop(0, protos // 128, proto_norm, 0)

    def chunk(c):
        return slice(c * 128, (c + 1) * 128)

    def total_of(ref, count):
        acc = ref[0]
        for i in range(1, count):
            acc = acc + ref[i]
        return acc

    def start_all(ref, me, count, ids, send, recv):
        for d in range(1, count):
            remote(ref.at[me], ref.at[me], send, recv, ids(d)).start()
        others = ref.at[pl.ds(0, count - 1)]
        return remote(others, others, send, recv, ids(1))

    zero = jnp.zeros((8, 128), F32)

    def put_cols(it, v, cols):
        for c in range(lane_chunks):
            col_z[it, v, me_z, c:c + 1, :] = jnp.sum(cols[c], axis=0, keepdims=True)
        return start_all(col_z.at[it, v], me_z, n_z, z_id, col_send, col_sem.at[it, v])

    def lane_sums(block):
        return jnp.sum(block.T, axis=0, keepdims=True)

    def spread(values, v, target):
        for i in range(view_blocks):
            at = slice(v * clips + i * 128, v * clips + (i + 1) * 128)
            target[at, :] = jnp.broadcast_to(values[i:i + 1, :], (128, 128)).T

    counter = [0]

    def slots(n):
        counter[0] += n
        return counter[0] - n

    def send(src, dst, device, group, slot):
        copy = remote(src, dst, out_sem.at[group], in_sem.at[slot], device)
        copy.start()
        return copy

    def bytes_of(ref, group, slot):
        return remote(ref, ref, out_sem.at[group], in_sem.at[slot], partner)

    def add_to(ref, value):
        ref[...] = ref[...] + value

    x, y = me_p // 4, me_p % 4
    x_next = {"proto": (x + 1) % 4 * 4 + y}
    x_prev = {"proto": (x + 3) % 4 * 4 + y}
    y_next = {"proto": x * 4 + (y + 1) % 4}
    y_prev = {"proto": x * 4 + (y + 3) % 4}
    z_next, z_prev = z_id(1), z_id(n_z - 1)

    class Scatter4:
        def __init__(self, view, me, ahead, behind, buf, group):
            self.view, self.me, self.ahead, self.behind, self.buf = view, me, ahead, behind, buf
            self.group, self.first = group, slots(3)
            self.c = {}

        def send(self, slot, dest, part):
            device = self.ahead if slot < 3 else self.behind
            self.c[slot] = send(
                self.view(dest, part), self.buf.at[slot], device, self.group,
                self.first + {0: 0, 3: 1}.get(slot, 2))

        def start(self):
            m = self.me
            self.send(0, (m + 2) % 4, 0)
            self.send(3, (m + 2) % 4, 1)
            self.send(1, (m + 1) % 4, 1)
            self.send(4, (m + 3) % 4, 0)

        def mid(self):
            m = self.me
            self.c[0].wait_recv()
            add_to(self.view((m + 1) % 4, 0), self.buf[0])
            self.send(2, (m + 1) % 4, 0)
            self.c[3].wait_recv()
            add_to(self.view((m + 3) % 4, 1), self.buf[3])
            self.send(5, (m + 3) % 4, 1)

        def finish(self):
            bytes_of(self.buf.at[pl.ds(0, 4)], self.group, self.first + 2).wait_recv()
            add_to(self.view(self.me, 0), self.buf[2] + self.buf[4])
            add_to(self.view(self.me, 1), self.buf[1] + self.buf[5])

    class Gather4:
        def __init__(self, view, me, ahead, behind, like, group):
            self.view, self.me, self.ahead, self.behind, self.like = view, me, ahead, behind, like
            self.group, self.first = group, slots(3)
            self.c = {}

        def send(self, slot, owner, part):
            spot = self.view(owner, part)
            self.c[slot] = send(
                spot, spot, self.ahead if slot < 3 else self.behind, self.group,
                self.first + {0: 0, 3: 1}.get(slot, 2))

        def start(self):
            self.send(0, self.me, 0)
            self.send(3, self.me, 1)
            self.send(1, self.me, 1)
            self.send(4, self.me, 0)

        def mid(self):
            self.c[0].wait_recv()
            self.send(2, (self.me + 3) % 4, 0)
            self.c[3].wait_recv()
            self.send(5, (self.me + 1) % 4, 1)

        def finish(self):
            bytes_of(self.like.at[pl.ds(0, 4)], self.group, self.first + 2).wait_recv()

    def quarter(half, part):
        return pl.ds(half * 64 + part * 32, 32)

    def along_x(ref, half):
        return lambda at, part: ref.at[at, :, quarter(half, part), :]

    def along_y(ref, half):
        return lambda at, part: ref.at[:, at, quarter(half, part), :]

    def in_x(ref, half):
        return lambda at, part: ref.at[at, y, quarter(half, part), :]

    def in_y(ref, half):
        return lambda at, part: ref.at[x, at, quarter(half, part), :]

    class Both:
        def __init__(self, *rings):
            self.rings = rings

        def start(self):
            for ring in self.rings:
                ring.start()

        def mid(self):
            for ring in self.rings:
                ring.mid()

        def finish(self):
            for ring in self.rings:
                ring.finish()

    def scatter(ref):
        return (
            Both(Scatter4(along_x(ref, 0), x, x_next, x_prev, rs_buf.at[0], 0),
                 Scatter4(along_y(ref, 1), y, y_next, y_prev, rs_buf.at[1], 0)),
            Both(Scatter4(in_y(ref, 0), y, y_next, y_prev, rs_small.at[0], 1),
                 Scatter4(in_x(ref, 1), x, x_next, x_prev, rs_small.at[1], 1)))

    def gather(ref):
        return (
            Both(Gather4(in_y(ref, 0), y, y_next, y_prev, rs_small.at[0], 2),
                 Gather4(in_x(ref, 1), x, x_next, x_prev, rs_small.at[1], 2)),
            Both(Gather4(along_x(ref, 0), x, x_next, x_prev, rs_buf.at[0], 3),
                 Gather4(along_y(ref, 1), y, y_next, y_prev, rs_buf.at[1], 3)))

    hops = (4, 3, 3, 2, 2, 1, 1)
    split = 1
    units = len(hops) * split
    back = 2 * split

    class ScatterZ:
        def __init__(self):
            self.first = slots(2 * (units - back) + 1)
            self.c = {}

        def view(self, dest, way, i):
            part = i // split % 2 ^ way
            return dc_half.at[dest, pl.ds(part * 128 + i % split * (128 // split), 128 // split), :]

        def step(self, i):
            for way in (0, 1):
                hop = hops[i // split]
                spot = self.view((me_z + (n_z - hop if way else hop)) % n_z, way, i)
                if i >= back:
                    self.c[way, i - back].wait_recv()
                    add_to(spot, z_buf[way, i - back])
                slot = self.first + min(2 * i + way, 2 * (units - back))
                self.c[way, i] = send(spot, z_buf.at[way, i], z_prev if way else z_next, 4, slot)

        def finish(self):
            last = z_buf.at[:, pl.ds(units - back, back)]
            bytes_of(last, 4, self.first + 2 * (units - back)).wait_recv()
            for i in range(units - back, units):
                for way in (0, 1):
                    add_to(self.view(me_z, way, i), z_buf[way, i])

    class GatherZ:
        def __init__(self):
            self.c = {}
            self.first, self.last = slots(2 * units), slots(1)

        def pass_on(self, spot):
            send(spot, spot, partner, 6, self.last)

        def view(self, owner, way, i):
            part = i // split % 2 ^ way
            return agw.at[core * n_z + owner, pl.ds(part * 64 + i % split * (64 // split), 64 // split), :]

        def relay(self, way, i):
            self.c[way, i].wait_recv()
            far = i // split // 2 + 1
            spot = self.view((me_z + (far if way else n_z - far)) % n_z, way, i)
            return spot

        def step(self, i):
            for way in (0, 1):
                if i >= back:
                    spot = self.relay(way, i - back)
                else:
                    spot = self.view(me_z, way, i)
                self.c[way, i] = send(
                    spot, spot, z_prev if way else z_next, 5, self.first + 2 * i + way)
                if i >= back:
                    self.pass_on(spot)

        def own(self):
            self.pass_on(agw.at[core * n_z + me_z])

        def finish(self):
            for i in range(units - back, units):
                for way in (0, 1):
                    self.pass_on(self.relay(way, i))


    step_m, step_w = 512, 512

    def first_pass(v):
        def step(i, cols):
            at = pl.ds(pl.multiple_of(i * step_m, step_m), step_m)
            glob = pl.ds(pl.multiple_of(v * clips + i * step_m, step_m), step_m)
            unit, _ = normalized(embeds[v][at, :].astype(F32))
            ub = unit.astype(BF16)
            unit_b[glob, :] = ub
            cols = list(cols)
            for k in range(protos // step_w):
                score = lax.dot_general(
                    ub, proto_b[k * step_w:(k + 1) * step_w, :],
                    (((1,), (1,)), ((), ())), preferred_element_type=F32)
                soft = jnp.exp2(score * EXPONENT)
                code = soft * soft
                table[glob, k * step_w:(k + 1) * step_w] = code
                for j in range(step_w // 128):
                    c = k * (step_w // 128) + j
                    cols[c] = cols[c] + fold8(code[:, chunk(j)])
            return tuple(cols)

        return lax.fori_loop(0, clips // step_m, step, (zero,) * lane_chunks)

    def cols_pass(v):
        def step(i, cols):
            at = pl.ds(pl.multiple_of(v * clips + i * 64, 64), 64)
            s = clip_b[at, :]
            return tuple(cols[c] + fold8(table[at, chunk(c)] * s) for c in range(lane_chunks))

        return lax.fori_loop(0, clips // 64, step, (zero,) * lane_chunks)

    def rows_pass(it, v):
        def step(i, carry):
            for j in range(2):
                block = 2 * i + j
                at = pl.ds(pl.multiple_of(v * clips + block * 128, 128), 128)
                acc = jnp.zeros((128, 128), F32)
                for c in range(lane_chunks):
                    acc = acc + table[at, chunk(c)] * scale[v, c:c + 1, :]
                row_recv[it, v, me_p, pl.ds(block, 1), :] = lane_sums(acc)
            return carry

        lax.fori_loop(0, view_blocks // 2, step, 0)
        return start_all(row_recv.at[it, v], me_p, n_p, p_id, row_send, row_sem.at[it, v])

    def wait_all(copies):
        copies.wait_recv()

    def pair_start(it, v, copies):
        wait_all(copies)
        pair = col_pair.at[it, v]
        pair[core] = total_of(col_z.at[it, v], n_z)
        copy = remote(pair.at[core], pair.at[core], colp_send, colp_sem.at[it, v], partner)
        copy.start()
        return copy

    z_copies = [None, None]
    row_copies = [None, None]
    z_cols = first_pass(0)
    pl.semaphore_wait(barrier, n_p - 1 + 2 * n_z - 1)
    z_copies[0] = put_cols(0, 0, z_cols)
    z_copies[1] = put_cols(0, 1, first_pass(1))

    def soft_totals(i, carry):
        at = pl.ds(pl.multiple_of(i * 128, 128), 128)
        acc = jnp.zeros((128, 128), F32)
        for c in range(lane_chunks):
            e = table[at, chunk(c)]
            acc = acc + e * lax.rsqrt(e)
        den_recv[me_p, pl.ds(i, 1), :] = lane_sums(acc)
        return carry

    lax.fori_loop(0, row_blocks, soft_totals, 0)
    den_copies = start_all(den_recv, me_p, n_p, p_id, small_send.at[0], small_sem.at[0])

    def transpose_unit(i, carry):
        at = pl.ds(pl.multiple_of(i * 128, 128), 128)
        unit_t[i] = unit_b[at, :].astype(F32).T.astype(BF16)
        return carry


    def grad_rows(v, first, count):
        w = 1 - v
        mine = pl.ds(pl.multiple_of(v * clips + first, count), count)
        other = pl.ds(pl.multiple_of(w * clips + first, count), count)
        soft_scale = soft_b[mine, :]
        code_scale = code_b[other, :]
        for c in range(lane_chunks):
            e = table[mine, chunk(c)]
            code = table[other, chunk(c)] * scale[w, c:c + 1, :] * code_scale
            grads[c, mine, :] = (e * lax.rsqrt(e) * soft_scale - code).astype(BF16)

    def du_rows(v, i):
        at = pl.ds(pl.multiple_of(v * clips + i * 256, 256), 256)
        mine = jnp.concatenate([grads[c, at, :] for c in range(lane_chunks)], axis=1)
        out = jnp.dot(mine, proto_b[...], preferred_element_type=F32)
        owner = v * (n_p // 2) + 2 * i
        du[owner // 4, pl.ds(owner % 4, 2)] = out.reshape(2, 128, width)

    def grad_pass(v):
        def step(i, carry):
            for j in range(4):
                grad_rows(v, i * 256 + j * 64, 64)
            return carry

        lax.fori_loop(0, clips // 256, step, 0)

    def du_dot(v):
        def step(i, carry):
            du_rows(v, i)
            return carry

        lax.fori_loop(0, clips // 256, step, 0)

    for it in range(ITERS):
        pairs = [pair_start(it, v, z_copies[v]) for v in range(2)]
        for v in range(2):
            wait_all(pairs[v])
            scale[v] = 1.0 / (protos_all * (col_pair[it, v, 0] + col_pair[it, v, 1]))
            row_copies[v] = rows_pass(it, v)
        if it == 0:
            lax.fori_loop(0, row_blocks, transpose_unit, 0)
        if it == 1:
            wait_all(den_copies)
            soft = 10.0 / total_of(den_recv, n_p)
            for v in range(2):
                spread(soft[v * view_blocks:(v + 1) * view_blocks], v, soft_b)
        for v in range(2):
            wait_all(row_copies[v])
            row_sum = total_of(row_recv.at[it, v], n_p)
            if it < ITERS - 1:
                spread(1.0 / (clips_all * row_sum), v, clip_b)
                z_copies[v] = put_cols(it + 1, v, cols_pass(v))
            else:
                spread(10.0 / row_sum, v, code_b)
                grad_pass(1 - v)
                if v == 0:
                    du_dot(1)

    def project(grad, raw):
        unit, inverse = normalized(raw)
        along = jnp.sum(unit * grad, axis=-1, keepdims=True)
        return (grad - unit * along) * inverse

    def lanes_square(block):
        sq = block * block
        return jnp.sum(sq[:, :128] + sq[:, 128:], axis=0, keepdims=True)

    theirs = (1 - core) * n_z
    pair_slot = slots(1)

    def pair_piece(i):
        return remote(
            dct.at[pl.ds(theirs + 2 * i, 2)], dc_pair.at[pl.ds(2 * i, 2)],
            out_sem.at[7], in_sem.at[pair_slot], partner)

    def dc_dot(first_chunk, sending):
        def step(i, carry):
            c = first_chunk + 2 * i
            units_t = jnp.concatenate([unit_t[j] for j in range(row_blocks)], axis=1)
            pair = jnp.concatenate([grads[c], grads[c + 1]], axis=1)
            out = jnp.dot(units_t, pair, preferred_element_type=F32)
            dct[c] = out[:, :128]
            dct[c + 1] = out[:, 128:]
            if sending:
                pair_piece(i).start()
            return carry

        lax.fori_loop(0, n_z // 2, step, 0)

    r1, r2 = scatter(du)
    g1, g2 = gather(agx)
    zs, zg = ScatterZ(), GatherZ()
    du_dot(0)
    r1.start()
    dc_dot(theirs, True)
    dc_dot(core * n_z, False)
    bytes_of(dc_pair, 7, pair_slot).wait_recv()
    for j in range(n_z):
        dc_half[j] = dct[core * n_z + j] + dc_pair[j]
    zs.step(0)
    zs.step(1)
    r1.mid()
    zs.step(2)
    zs.step(3)
    zs.step(4)
    r1.finish()
    r2.start()
    zs.step(5)
    zs.step(6)
    r2.mid()
    r2.finish()
    at = pl.ds(pl.multiple_of((me_p % view_blocks) * 128, 128), 128)
    raw = jnp.where(me_p < view_blocks, slow_ref[at, :].astype(F32), fast_ref[at, :].astype(F32))
    dx_own = project(du[x, y], raw)
    agx[x, y] = dx_own
    g1.start()
    zs.finish()
    mine = core * n_z + me_z
    dw_own = project(dc_half[me_z].T, proto_ref[pl.ds(pl.multiple_of(mine * 128, 128), 128), :])
    agw[mine] = dw_own
    zg.step(0)
    zg.step(1)
    zg.own()
    sq_p[me_p, 0:1, :] = lanes_square(dw_own)
    sq_p[me_p, 1:2, :] = lanes_square(dx_own)
    sq_p[me_p, 2:8, :] = jnp.zeros((6, 128), F32)
    sq_copies = start_all(sq_p, me_p, n_p, p_id, small_send.at[1], small_sem.at[1])
    g1.mid()
    zg.step(2)
    g1.finish()
    g2.start()
    zg.step(3)
    zg.step(4)
    wait_all(sq_copies)
    sqp_copies = sq_copies
    sq_z[batch_me] = total_of(sq_p, n_p)
    sq_copies = start_all(sq_z, batch_me, 2 * n_z, b_id, small_send.at[2], small_sem.at[2])
    zg.step(5)
    g2.mid()
    zg.step(6)
    zg.finish()
    wait_all(sq_copies)
    square = jnp.sum(total_of(sq_z, 2 * n_z), axis=1, keepdims=True)
    entries = float(protos_all * width), float(2 * clips_all * width)
    for i, out in enumerate((wf_ref, xf_ref)):
        out[...] = jnp.broadcast_to(
            lax.rsqrt(square[i:i + 1, :] / entries[i] + NORM_EPS), (8, width))
    g2.finish()
    bytes_of(dc_pair, 6, zg.last).wait_recv()
    for group, ref in enumerate((rs_buf, rs_small, rs_small, rs_buf, z_buf, z_buf, dc_pair, dc_pair)):
        bytes_of(ref, group, 0).wait_send()
    for ref, sem in (
        (col_z.at[:, :, pl.ds(0, n_z - 1)], col_send),
        (col_pair.at[:, :, 0], colp_send),
        (row_recv.at[:, :, pl.ds(0, n_p - 1)], row_send),
    ):
        remote(ref, ref, sem, in_sem.at[0], partner).wait_send()
    for copies in (den_copies, sqp_copies, sq_copies):
        copies.wait_send()


def body(slow_embed, fast_embed, prototypes):
    clips, width = slow_embed.shape
    protos = prototypes.shape[0]
    n_b = lax.axis_size("batch")
    n_p = lax.axis_size("proto")
    n_z = n_b // 2
    rows = 2 * clips
    DMA = pltpu.SemaphoreType.DMA
    vmem = pltpu.VMEM
    lane_chunks = protos // 128
    row_blocks = rows // 128
    scratch = [
        vmem((rows, protos), F32),
        vmem((lane_chunks, rows, 128), BF16),
        vmem((rows, width), BF16),
        vmem((row_blocks, width, 128), BF16),
        vmem((protos, width), BF16),
        vmem((2, lane_chunks, 128), F32),
        vmem((rows, 128), F32),
        vmem((rows, 128), F32),
        vmem((rows, 128), F32),
        vmem((4, 4, 128, width), F32),
        vmem((lane_chunks, width, 128), F32),
        vmem((n_z, width, 128), F32),
        vmem((n_z, width, 128), F32),
        vmem((2, 6, 4, 32, width), F32),
        vmem((2, 6, 32, width), F32),
        vmem((2, 7, 128, 128), F32),
        vmem((ITERS, 2, n_z, lane_chunks, 128), F32),
        vmem((ITERS, 2, 2, lane_chunks, 128), F32),
        vmem((ITERS, 2, n_p, row_blocks // 2, 128), F32),
        vmem((n_p, row_blocks, 128), F32),
        vmem((n_p, 8, 128), F32),
        vmem((n_b, 8, 128), F32),
        DMA(()), DMA((ITERS, 2)), DMA(()), DMA((ITERS, 2)), DMA(()), DMA((ITERS, 2)),
        DMA((3,)), DMA((3,)), DMA((8,)), DMA((COPIES,)),
    ]
    whole = pl.BlockSpec(memory_space=pltpu.VMEM)
    dw, dx, dw_factor, dx_factor = pl.pallas_call(
        functools.partial(kernel, (clips, protos, width, n_z, n_p)),
        out_shape=(
            vmem((lane_chunks, 128, width), F32),
            vmem((4, 4, 128, width), F32),
            vmem((8, width), F32),
            vmem((8, width), F32),
        ),
        in_specs=[whole] * 3,
        out_specs=(whole,) * 4,
        scratch_shapes=scratch,
        compiler_params=pltpu.CompilerParams(
            collective_id=0, has_side_effects=True, vmem_limit_bytes=56 * 2**20),
        name="swav",
    )(slow_embed, fast_embed, prototypes)

    def scaled(array, factor, rows):
        return (array.reshape(rows // 8, 8, width) * factor).reshape(rows, width)

    return (
        scaled(dw, dw_factor, protos),
        scaled(dx[:2], dx_factor, clips),
        scaled(dx[2:], dx_factor, clips),
    )


def solution(mesh):
    placed = (P("batch", None), P("batch", None), P("proto", None))
    return jax.shard_map(
        body,
        mesh=mesh,
        in_specs=placed,
        out_specs=(P("proto", None), P("batch", None), P("batch", None)),
        check_vma=False,
    )
```

```python
import functools

import jax
import jax.numpy as jnp
from jax import lax
from jax.experimental import pallas as pl
from jax.experimental.pallas import tpu as pltpu
from jax.sharding import PartitionSpec as P

ITERS = 3
COPIES = 51
EXPONENT = 10.0 * 1.4426950408889634
NORM_EPS = 1e-06
MESH = pl.DeviceIdType.MESH
F32 = jnp.float32
BF16 = jnp.bfloat16


def normalized(rows):
    total = jnp.sum(rows * rows, axis=-1, keepdims=True) + 1e-12
    inverse = 1.0 / jnp.sqrt(total)
    return rows * inverse, inverse


def fold8(block):
    rows, lanes = block.shape
    return jnp.sum(block.reshape(rows // 8, 8, lanes), axis=0)


def kernel(
    dims,
    slow_ref, fast_ref, proto_ref,
    agw, agx, wf_ref, xf_ref,
    table, grads, unit_b, unit_t, proto_b, scale, clip_b, soft_b, code_b,
    du, dct, dc_pair, dc_half, rs_buf, rs_small, z_buf,
    col_z, col_pair, row_recv, den_recv, sq_p, sq_z,
    col_send, col_sem, colp_send, colp_sem, row_send, row_sem, small_send, small_sem,
    out_sem, in_sem,
):
    clips, protos, width, n_z, n_p = dims
    batch_me = lax.axis_index("batch")
    me_p = lax.axis_index("proto")
    me_z = batch_me // 2
    core = batch_me % 2
    clips_all = clips * 2 * n_z
    protos_all = protos * n_p
    rows = 2 * clips
    lane_chunks = protos // 128
    row_blocks = rows // 128
    view_blocks = clips // 128
    embeds = (slow_ref, fast_ref)

    def p_id(d):
        return {"proto": (me_p // 4 + d // 4) % 4 * 4 + (me_p + d) % 4}

    def p_hops(d):
        return min(d // 4, 4 - d // 4) + min(d % 4, 4 - d % 4)

    def z_hops(d):
        return min(d, n_z - d)

    def z_id(d):
        return {"batch": ((me_z + d) % n_z) * 2 + core}

    def b_id(d):
        return {"batch": (batch_me + d) % (2 * n_z)}

    partner = {"batch": me_z * 2 + 1 - core}

    def remote(src, dst, send, recv, device):
        return pltpu.make_async_remote_copy(
            src_ref=src, dst_ref=dst, send_sem=send, recv_sem=recv,
            device_id=device, device_id_type=MESH,
        )

    barrier = pltpu.get_barrier_semaphore()
    for d in range(1, n_p):
        pl.semaphore_signal(barrier, inc=1, device_id=p_id(d), device_id_type=MESH)
    for d in range(1, 2 * n_z):
        pl.semaphore_signal(barrier, inc=1, device_id=b_id(d), device_id_type=MESH)

    def proto_norm(i, carry):
        at = pl.ds(pl.multiple_of(i * 128, 128), 128)
        unit, _ = normalized(proto_ref[at, :])
        proto_b[at, :] = unit.astype(BF16)
        return carry

    lax.fori_loop(0, protos // 128, proto_norm, 0)

    def chunk(c):
        return slice(c * 128, (c + 1) * 128)

    def total_of(ref, count):
        acc = ref[0]
        for i in range(1, count):
            acc = acc + ref[i]
        return acc

    def start_all(ref, me, count, ids, send, recv):
        hops_to = {p_id: p_hops, z_id: z_hops}.get(ids, lambda d: z_hops(d // 2))
        for d in sorted(range(1, count), key=hops_to, reverse=True):
            remote(ref.at[me], ref.at[me], send, recv, ids(d)).start()
        others = ref.at[pl.ds(0, count - 1)]
        return remote(others, others, send, recv, ids(1))

    zero = jnp.zeros((8, 128), F32)

    def put_cols(it, v, cols):
        for c in range(lane_chunks):
            col_z[it, v, me_z, c:c + 1, :] = jnp.sum(cols[c], axis=0, keepdims=True)
        return start_all(col_z.at[it, v], me_z, n_z, z_id, col_send, col_sem.at[it, v])

    def lane_sums(block):
        return jnp.sum(block.T, axis=0, keepdims=True)

    def spread(values, v, target):
        for i in range(view_blocks):
            at = slice(v * clips + i * 128, v * clips + (i + 1) * 128)
            target[at, :] = jnp.broadcast_to(values[i:i + 1, :], (128, 128)).T

    counter = [0]

    def slots(n):
        counter[0] += n
        return counter[0] - n

    def send(src, dst, device, group, slot):
        copy = remote(src, dst, out_sem.at[group], in_sem.at[slot], device)
        copy.start()
        return copy

    def bytes_of(ref, group, slot):
        return remote(ref, ref, out_sem.at[group], in_sem.at[slot], partner)

    def add_to(ref, value):
        ref[...] = ref[...] + value

    x, y = me_p // 4, me_p % 4
    x_next = {"proto": (x + 1) % 4 * 4 + y}
    x_prev = {"proto": (x + 3) % 4 * 4 + y}
    y_next = {"proto": x * 4 + (y + 1) % 4}
    y_prev = {"proto": x * 4 + (y + 3) % 4}
    z_next, z_prev = z_id(1), z_id(n_z - 1)

    class Scatter4:
        def __init__(self, view, me, ahead, behind, buf, group):
            self.view, self.me, self.ahead, self.behind, self.buf = view, me, ahead, behind, buf
            self.group, self.first = group, slots(3)
            self.c = {}

        def send(self, slot, dest, part):
            device = self.ahead if slot < 3 else self.behind
            self.c[slot] = send(
                self.view(dest, part), self.buf.at[slot], device, self.group,
                self.first + {0: 0, 3: 1}.get(slot, 2))

        def start(self):
            m = self.me
            self.send(0, (m + 2) % 4, 0)
            self.send(3, (m + 2) % 4, 1)
            self.send(1, (m + 1) % 4, 1)
            self.send(4, (m + 3) % 4, 0)

        def mid(self):
            m = self.me
            self.c[0].wait_recv()
            add_to(self.view((m + 1) % 4, 0), self.buf[0])
            self.send(2, (m + 1) % 4, 0)
            self.c[3].wait_recv()
            add_to(self.view((m + 3) % 4, 1), self.buf[3])
            self.send(5, (m + 3) % 4, 1)

        def finish(self):
            bytes_of(self.buf.at[pl.ds(0, 4)], self.group, self.first + 2).wait_recv()
            add_to(self.view(self.me, 0), self.buf[2] + self.buf[4])
            add_to(self.view(self.me, 1), self.buf[1] + self.buf[5])

    class Gather4:
        def __init__(self, view, me, ahead, behind, like, group):
            self.view, self.me, self.ahead, self.behind, self.like = view, me, ahead, behind, like
            self.group, self.first = group, slots(3)
            self.c = {}

        def send(self, slot, owner, part):
            spot = self.view(owner, part)
            self.c[slot] = send(
                spot, spot, self.ahead if slot < 3 else self.behind, self.group,
                self.first + {0: 0, 3: 1}.get(slot, 2))

        def start(self):
            self.send(0, self.me, 0)
            self.send(3, self.me, 1)
            self.send(1, self.me, 1)
            self.send(4, self.me, 0)

        def mid(self):
            self.c[0].wait_recv()
            self.send(2, (self.me + 3) % 4, 0)
            self.c[3].wait_recv()
            self.send(5, (self.me + 1) % 4, 1)

        def finish(self):
            bytes_of(self.like.at[pl.ds(0, 4)], self.group, self.first + 2).wait_recv()

    def quarter(half, part):
        return pl.ds(half * 64 + part * 32, 32)

    def along_x(ref, half):
        return lambda at, part: ref.at[at, :, quarter(half, part), :]

    def along_y(ref, half):
        return lambda at, part: ref.at[:, at, quarter(half, part), :]

    def in_x(ref, half):
        return lambda at, part: ref.at[at, y, quarter(half, part), :]

    def in_y(ref, half):
        return lambda at, part: ref.at[x, at, quarter(half, part), :]

    class Both:
        def __init__(self, *rings):
            self.rings = rings

        def start(self):
            for ring in self.rings:
                ring.start()

        def mid(self):
            for ring in self.rings:
                ring.mid()

        def finish(self):
            for ring in self.rings:
                ring.finish()

    def scatter(ref):
        return (
            Both(Scatter4(along_x(ref, 0), x, x_next, x_prev, rs_buf.at[0], 0),
                 Scatter4(along_y(ref, 1), y, y_next, y_prev, rs_buf.at[1], 0)),
            Both(Scatter4(in_y(ref, 0), y, y_next, y_prev, rs_small.at[0], 1),
                 Scatter4(in_x(ref, 1), x, x_next, x_prev, rs_small.at[1], 1)))

    def gather(ref):
        return (
            Both(Gather4(in_y(ref, 0), y, y_next, y_prev, rs_small.at[0], 2),
                 Gather4(in_x(ref, 1), x, x_next, x_prev, rs_small.at[1], 2)),
            Both(Gather4(along_x(ref, 0), x, x_next, x_prev, rs_buf.at[0], 3),
                 Gather4(along_y(ref, 1), y, y_next, y_prev, rs_buf.at[1], 3)))

    hops = (4, 3, 3, 2, 2, 1, 1)
    split = 1
    units = len(hops) * split
    back = 2 * split

    class ScatterZ:
        def __init__(self):
            self.first = slots(2 * (units - back) + 1)
            self.c = {}

        def view(self, dest, way, i):
            part = i // split % 2 ^ way
            return dc_half.at[dest, pl.ds(part * 128 + i % split * (128 // split), 128 // split), :]

        def step(self, i):
            for way in (0, 1):
                hop = hops[i // split]
                spot = self.view((me_z + (n_z - hop if way else hop)) % n_z, way, i)
                if i >= back:
                    self.c[way, i - back].wait_recv()
                    add_to(spot, z_buf[way, i - back])
                slot = self.first + min(2 * i + way, 2 * (units - back))
                self.c[way, i] = send(spot, z_buf.at[way, i], z_prev if way else z_next, 4, slot)

        def finish(self):
            last = z_buf.at[:, pl.ds(units - back, back)]
            bytes_of(last, 4, self.first + 2 * (units - back)).wait_recv()
            for i in range(units - back, units):
                for way in (0, 1):
                    add_to(self.view(me_z, way, i), z_buf[way, i])

    class GatherZ:
        def __init__(self):
            self.c = {}
            self.first, self.last = slots(2 * units), slots(1)

        def pass_on(self, spot):
            send(spot, spot, partner, 6, self.last)

        def view(self, owner, way, i):
            part = i // split % 2 ^ way
            return agw.at[core * n_z + owner, pl.ds(part * 64 + i % split * (64 // split), 64 // split), :]

        def relay(self, way, i):
            self.c[way, i].wait_recv()
            far = i // split // 2 + 1
            spot = self.view((me_z + (far if way else n_z - far)) % n_z, way, i)
            return spot

        def step(self, i):
            for way in (0, 1):
                if i >= back:
                    spot = self.relay(way, i - back)
                else:
                    spot = self.view(me_z, way, i)
                self.c[way, i] = send(
                    spot, spot, z_prev if way else z_next, 5, self.first + 2 * i + way)
                if i >= back:
                    self.pass_on(spot)

        def own(self):
            self.pass_on(agw.at[core * n_z + me_z])

        def finish(self):
            for i in range(units - back, units):
                for way in (0, 1):
                    self.pass_on(self.relay(way, i))


    step_m, step_w = 512, 512

    def first_pass(v):
        def step(i, cols):
            at = pl.ds(pl.multiple_of(i * step_m, step_m), step_m)
            glob = pl.ds(pl.multiple_of(v * clips + i * step_m, step_m), step_m)
            unit, _ = normalized(embeds[v][at, :].astype(F32))
            ub = unit.astype(BF16)
            unit_b[glob, :] = ub
            cols = list(cols)
            for k in range(protos // step_w):
                score = lax.dot_general(
                    ub, proto_b[k * step_w:(k + 1) * step_w, :],
                    (((1,), (1,)), ((), ())), preferred_element_type=F32)
                soft = jnp.exp2(score * EXPONENT)
                code = soft * soft
                table[glob, k * step_w:(k + 1) * step_w] = code
                for j in range(step_w // 128):
                    c = k * (step_w // 128) + j
                    cols[c] = cols[c] + fold8(code[:, chunk(j)])
            return tuple(cols)

        return lax.fori_loop(0, clips // step_m, step, (zero,) * lane_chunks)

    def cols_pass(v):
        def step(i, cols):
            at = pl.ds(pl.multiple_of(v * clips + i * 64, 64), 64)
            s = clip_b[at, :]
            return tuple(cols[c] + fold8(table[at, chunk(c)] * s) for c in range(lane_chunks))

        return lax.fori_loop(0, clips // 64, step, (zero,) * lane_chunks)

    def rows_pass(it, v):
        def step(i, carry):
            for j in range(2):
                block = 2 * i + j
                at = pl.ds(pl.multiple_of(v * clips + block * 128, 128), 128)
                acc = jnp.zeros((128, 128), F32)
                for c in range(lane_chunks):
                    acc = acc + table[at, chunk(c)] * scale[v, c:c + 1, :]
                row_recv[it, v, me_p, pl.ds(block, 1), :] = lane_sums(acc)
            return carry

        lax.fori_loop(0, view_blocks // 2, step, 0)
        return start_all(row_recv.at[it, v], me_p, n_p, p_id, row_send, row_sem.at[it, v])

    def wait_all(copies):
        copies.wait_recv()

    def pair_start(it, v, copies):
        wait_all(copies)
        pair = col_pair.at[it, v]
        pair[core] = total_of(col_z.at[it, v], n_z)
        copy = remote(pair.at[core], pair.at[core], colp_send, colp_sem.at[it, v], partner)
        copy.start()
        return copy

    z_copies = [None, None]
    row_copies = [None, None]
    z_cols = first_pass(0)
    pl.semaphore_wait(barrier, n_p - 1 + 2 * n_z - 1)
    z_copies[0] = put_cols(0, 0, z_cols)
    z_copies[1] = put_cols(0, 1, first_pass(1))

    def soft_totals(i, carry):
        at = pl.ds(pl.multiple_of(i * 128, 128), 128)
        acc = jnp.zeros((128, 128), F32)
        for c in range(lane_chunks):
            e = table[at, chunk(c)]
            acc = acc + e * lax.rsqrt(e)
        den_recv[me_p, pl.ds(i, 1), :] = lane_sums(acc)
        return carry

    lax.fori_loop(0, row_blocks, soft_totals, 0)
    den_copies = start_all(den_recv, me_p, n_p, p_id, small_send.at[0], small_sem.at[0])

    def transpose_unit(i, carry):
        at = pl.ds(pl.multiple_of(i * 128, 128), 128)
        unit_t[i] = unit_b[at, :].astype(F32).T.astype(BF16)
        return carry


    def grad_rows(v, first, count):
        w = 1 - v
        mine = pl.ds(pl.multiple_of(v * clips + first, count), count)
        other = pl.ds(pl.multiple_of(w * clips + first, count), count)
        soft_scale = soft_b[mine, :]
        code_scale = code_b[other, :]
        for c in range(lane_chunks):
            e = table[mine, chunk(c)]
            code = table[other, chunk(c)] * scale[w, c:c + 1, :] * code_scale
            grads[c, mine, :] = (e * lax.rsqrt(e) * soft_scale - code).astype(BF16)

    def du_rows(v, i):
        at = pl.ds(pl.multiple_of(v * clips + i * 256, 256), 256)
        mine = jnp.concatenate([grads[c, at, :] for c in range(lane_chunks)], axis=1)
        out = jnp.dot(mine, proto_b[...], preferred_element_type=F32)
        owner = v * (n_p // 2) + 2 * i
        du[owner // 4, pl.ds(owner % 4, 2)] = out.reshape(2, 128, width)

    def grad_pass(v):
        def step(i, carry):
            for j in range(4):
                grad_rows(v, i * 256 + j * 64, 64)
            return carry

        lax.fori_loop(0, clips // 256, step, 0)

    def du_dot(v):
        def step(i, carry):
            du_rows(v, i)
            return carry

        lax.fori_loop(0, clips // 256, step, 0)

    for it in range(ITERS):
        pairs = [pair_start(it, v, z_copies[v]) for v in range(2)]
        for v in range(2):
            wait_all(pairs[v])
            scale[v] = 1.0 / (protos_all * (col_pair[it, v, 0] + col_pair[it, v, 1]))
            row_copies[v] = rows_pass(it, v)
        if it == 0:
            lax.fori_loop(0, row_blocks, transpose_unit, 0)
        if it == 1:
            wait_all(den_copies)
            soft = 10.0 / total_of(den_recv, n_p)
            for v in range(2):
                spread(soft[v * view_blocks:(v + 1) * view_blocks], v, soft_b)
        for v in range(2):
            wait_all(row_copies[v])
            row_sum = total_of(row_recv.at[it, v], n_p)
            if it < ITERS - 1:
                spread(1.0 / (clips_all * row_sum), v, clip_b)
                z_copies[v] = put_cols(it + 1, v, cols_pass(v))
            else:
                spread(10.0 / row_sum, v, code_b)
                grad_pass(1 - v)
                if v == 0:
                    du_dot(1)

    def project(grad, raw):
        unit, inverse = normalized(raw)
        along = jnp.sum(unit * grad, axis=-1, keepdims=True)
        return (grad - unit * along) * inverse

    def lanes_square(block):
        sq = block * block
        return jnp.sum(sq[:, :128] + sq[:, 128:], axis=0, keepdims=True)

    theirs = (1 - core) * n_z
    pair_slot = slots(1)

    def pair_piece(i):
        return remote(
            dct.at[pl.ds(theirs + 2 * i, 2)], dc_pair.at[pl.ds(2 * i, 2)],
            out_sem.at[7], in_sem.at[pair_slot], partner)

    def dc_dot(first_chunk, sending):
        def step(i, carry):
            c = first_chunk + 2 * i
            units_t = jnp.concatenate([unit_t[j] for j in range(row_blocks)], axis=1)
            pair = jnp.concatenate([grads[c], grads[c + 1]], axis=1)
            out = jnp.dot(units_t, pair, preferred_element_type=F32)
            dct[c] = out[:, :128]
            dct[c + 1] = out[:, 128:]
            if sending:
                pair_piece(i).start()
            return carry

        lax.fori_loop(0, n_z // 2, step, 0)

    r1, r2 = scatter(du)
    g1, g2 = gather(agx)
    zs, zg = ScatterZ(), GatherZ()
    du_dot(0)
    r1.start()
    dc_dot(theirs, True)
    dc_dot(core * n_z, False)
    bytes_of(dc_pair, 7, pair_slot).wait_recv()
    for j in range(n_z):
        dc_half[j] = dct[core * n_z + j] + dc_pair[j]
    zs.step(0)
    zs.step(1)
    r1.mid()
    zs.step(2)
    zs.step(3)
    zs.step(4)
    r1.finish()
    r2.start()
    zs.step(5)
    zs.step(6)
    r2.mid()
    r2.finish()
    at = pl.ds(pl.multiple_of((me_p % view_blocks) * 128, 128), 128)
    raw = jnp.where(me_p < view_blocks, slow_ref[at, :].astype(F32), fast_ref[at, :].astype(F32))
    dx_own = project(du[x, y], raw)
    agx[x, y] = dx_own
    g1.start()
    zs.finish()
    mine = core * n_z + me_z
    dw_own = project(dc_half[me_z].T, proto_ref[pl.ds(pl.multiple_of(mine * 128, 128), 128), :])
    agw[mine] = dw_own
    zg.step(0)
    zg.step(1)
    zg.own()
    sq_p[me_p, 0:1, :] = lanes_square(dw_own)
    sq_p[me_p, 1:2, :] = lanes_square(dx_own)
    sq_p[me_p, 2:8, :] = jnp.zeros((6, 128), F32)
    sq_copies = start_all(sq_p, me_p, n_p, p_id, small_send.at[1], small_sem.at[1])
    g1.mid()
    zg.step(2)
    g1.finish()
    g2.start()
    zg.step(3)
    zg.step(4)
    wait_all(sq_copies)
    sqp_copies = sq_copies
    sq_z[batch_me] = total_of(sq_p, n_p)
    sq_copies = start_all(sq_z, batch_me, 2 * n_z, b_id, small_send.at[2], small_sem.at[2])
    zg.step(5)
    g2.mid()
    zg.step(6)
    zg.finish()
    wait_all(sq_copies)
    square = jnp.sum(total_of(sq_z, 2 * n_z), axis=1, keepdims=True)
    entries = float(protos_all * width), float(2 * clips_all * width)
    for i, out in enumerate((wf_ref, xf_ref)):
        out[...] = jnp.broadcast_to(
            lax.rsqrt(square[i:i + 1, :] / entries[i] + NORM_EPS), (8, width))
    g2.finish()
    bytes_of(dc_pair, 6, zg.last).wait_recv()
    for group, ref in enumerate((rs_buf, rs_small, rs_small, rs_buf, z_buf, z_buf, dc_pair, dc_pair)):
        bytes_of(ref, group, 0).wait_send()
    for ref, sem in (
        (col_z.at[:, :, pl.ds(0, n_z - 1)], col_send),
        (col_pair.at[:, :, 0], colp_send),
        (row_recv.at[:, :, pl.ds(0, n_p - 1)], row_send),
    ):
        remote(ref, ref, sem, in_sem.at[0], partner).wait_send()
    for copies in (den_copies, sqp_copies, sq_copies):
        copies.wait_send()


def body(slow_embed, fast_embed, prototypes):
    clips, width = slow_embed.shape
    protos = prototypes.shape[0]
    n_b = lax.axis_size("batch")
    n_p = lax.axis_size("proto")
    n_z = n_b // 2
    rows = 2 * clips
    DMA = pltpu.SemaphoreType.DMA
    vmem = pltpu.VMEM
    lane_chunks = protos // 128
    row_blocks = rows // 128
    scratch = [
        vmem((rows, protos), F32),
        vmem((lane_chunks, rows, 128), BF16),
        vmem((rows, width), BF16),
        vmem((row_blocks, width, 128), BF16),
        vmem((protos, width), BF16),
        vmem((2, lane_chunks, 128), F32),
        vmem((rows, 128), F32),
        vmem((rows, 128), F32),
        vmem((rows, 128), F32),
        vmem((4, 4, 128, width), F32),
        vmem((lane_chunks, width, 128), F32),
        vmem((n_z, width, 128), F32),
        vmem((n_z, width, 128), F32),
        vmem((2, 6, 4, 32, width), F32),
        vmem((2, 6, 32, width), F32),
        vmem((2, 7, 128, 128), F32),
        vmem((ITERS, 2, n_z, lane_chunks, 128), F32),
        vmem((ITERS, 2, 2, lane_chunks, 128), F32),
        vmem((ITERS, 2, n_p, row_blocks // 2, 128), F32),
        vmem((n_p, row_blocks, 128), F32),
        vmem((n_p, 8, 128), F32),
        vmem((n_b, 8, 128), F32),
        DMA(()), DMA((ITERS, 2)), DMA(()), DMA((ITERS, 2)), DMA(()), DMA((ITERS, 2)),
        DMA((3,)), DMA((3,)), DMA((8,)), DMA((COPIES,)),
    ]
    whole = pl.BlockSpec(memory_space=pltpu.VMEM)
    dw, dx, dw_factor, dx_factor = pl.pallas_call(
        functools.partial(kernel, (clips, protos, width, n_z, n_p)),
        out_shape=(
            vmem((lane_chunks, 128, width), F32),
            vmem((4, 4, 128, width), F32),
            vmem((8, width), F32),
            vmem((8, width), F32),
        ),
        in_specs=[whole] * 3,
        out_specs=(whole,) * 4,
        scratch_shapes=scratch,
        compiler_params=pltpu.CompilerParams(
            collective_id=0, has_side_effects=True, vmem_limit_bytes=56 * 2**20),
        name="swav",
    )(slow_embed, fast_embed, prototypes)

    def scaled(array, factor, rows):
        return (array.reshape(rows // 8, 8, width) * factor).reshape(rows, width)

    return (
        scaled(dw, dw_factor, protos),
        scaled(dx[:2], dx_factor, clips),
        scaled(dx[2:], dx_factor, clips),
    )


def solution(mesh):
    placed = (P("batch", None), P("batch", None), P("proto", None))
    return jax.shard_map(
        body,
        mesh=mesh,
        in_specs=placed,
        out_specs=(P("proto", None), P("batch", None), P("batch", None)),
        check_vma=False,
    )
```

```python
import functools

import jax
import jax.numpy as jnp
from jax import lax
from jax.experimental import pallas as pl
from jax.experimental.pallas import tpu as pltpu
from jax.sharding import PartitionSpec as P

ITERS = 3
COPIES = 51
EXPONENT = 10.0 * 1.4426950408889634
NORM_EPS = 1e-06
MESH = pl.DeviceIdType.MESH
F32 = jnp.float32
BF16 = jnp.bfloat16


def normalized(rows):
    total = jnp.sum(rows * rows, axis=-1, keepdims=True) + 1e-12
    inverse = 1.0 / jnp.sqrt(total)
    return rows * inverse, inverse


def fold8(block):
    rows, lanes = block.shape
    return jnp.sum(block.reshape(rows // 8, 8, lanes), axis=0)


def kernel(
    dims,
    slow_ref, fast_ref, proto_ref,
    agw, agx, wf_ref, xf_ref,
    table, grads, unit_b, unit_t, proto_b, scale, clip_b, soft_b, code_b,
    du, dct, dc_pair, dc_half, rs_buf, rs_small, z_buf,
    col_z, col_pair, row_recv, den_recv, sq_p, sq_z,
    col_send, col_sem, colp_send, colp_sem, row_send, row_sem, small_send, small_sem,
    out_sem, in_sem,
):
    clips, protos, width, n_z, n_p = dims
    batch_me = lax.axis_index("batch")
    me_p = lax.axis_index("proto")
    me_z = batch_me // 2
    core = batch_me % 2
    clips_all = clips * 2 * n_z
    protos_all = protos * n_p
    rows = 2 * clips
    lane_chunks = protos // 128
    row_blocks = rows // 128
    view_blocks = clips // 128
    embeds = (slow_ref, fast_ref)

    def p_id(d):
        return {"proto": (me_p // 4 + d // 4) % 4 * 4 + (me_p + d) % 4}

    def p_hops(d):
        return min(d // 4, 4 - d // 4) + min(d % 4, 4 - d % 4)

    def z_hops(d):
        return min(d, n_z - d)

    def z_id(d):
        return {"batch": ((me_z + d) % n_z) * 2 + core}

    def b_id(d):
        return {"batch": (batch_me + d) % (2 * n_z)}

    partner = {"batch": me_z * 2 + 1 - core}

    def remote(src, dst, send, recv, device):
        return pltpu.make_async_remote_copy(
            src_ref=src, dst_ref=dst, send_sem=send, recv_sem=recv,
            device_id=device, device_id_type=MESH,
        )

    barrier = pltpu.get_barrier_semaphore()
    for d in range(1, n_p):
        pl.semaphore_signal(barrier, inc=1, device_id=p_id(d), device_id_type=MESH)
    for d in range(1, 2 * n_z):
        pl.semaphore_signal(barrier, inc=1, device_id=b_id(d), device_id_type=MESH)

    def proto_norm(i, carry):
        at = pl.ds(pl.multiple_of(i * 512, 512), 512)
        unit, _ = normalized(proto_ref[at, :])
        proto_b[at, :] = unit.astype(BF16)
        return carry

    lax.fori_loop(0, protos // 512, proto_norm, 0)

    def chunk(c):
        return slice(c * 128, (c + 1) * 128)

    def total_of(ref, count):
        acc = ref[0]
        for i in range(1, count):
            acc = acc + ref[i]
        return acc

    def start_all(ref, me, count, ids, send, recv):
        hops_to = {p_id: p_hops, z_id: z_hops}.get(ids, lambda d: z_hops(d // 2))
        for d in sorted(range(1, count), key=hops_to, reverse=True):
            remote(ref.at[me], ref.at[me], send, recv, ids(d)).start()
        others = ref.at[pl.ds(0, count - 1)]
        return remote(others, others, send, recv, ids(1))

    zero = jnp.zeros((8, 128), F32)

    def put_cols(it, v, cols):
        for c in range(lane_chunks):
            col_z[it, v, me_z, c:c + 1, :] = jnp.sum(cols[c], axis=0, keepdims=True)
        return start_all(col_z.at[it, v], me_z, n_z, z_id, col_send, col_sem.at[it, v])

    def lane_sums(block):
        return jnp.sum(block.T, axis=0, keepdims=True)

    def spread(values, v, target):
        for i in range(view_blocks):
            at = slice(v * clips + i * 128, v * clips + (i + 1) * 128)
            target[at, :] = jnp.broadcast_to(values[i:i + 1, :], (128, 128)).T

    counter = [0]

    def slots(n):
        counter[0] += n
        return counter[0] - n

    def send(src, dst, device, group, slot):
        copy = remote(src, dst, out_sem.at[group], in_sem.at[slot], device)
        copy.start()
        return copy

    def bytes_of(ref, group, slot):
        return remote(ref, ref, out_sem.at[group], in_sem.at[slot], partner)

    def add_to(ref, value):
        ref[...] = ref[...] + value

    x, y = me_p // 4, me_p % 4
    x_next = {"proto": (x + 1) % 4 * 4 + y}
    x_prev = {"proto": (x + 3) % 4 * 4 + y}
    y_next = {"proto": x * 4 + (y + 1) % 4}
    y_prev = {"proto": x * 4 + (y + 3) % 4}
    z_next, z_prev = z_id(1), z_id(n_z - 1)

    class Scatter4:
        def __init__(self, view, me, ahead, behind, buf, group):
            self.view, self.me, self.ahead, self.behind, self.buf = view, me, ahead, behind, buf
            self.group, self.first = group, slots(3)
            self.c = {}

        def send(self, slot, dest, part):
            device = self.ahead if slot < 3 else self.behind
            self.c[slot] = send(
                self.view(dest, part), self.buf.at[slot], device, self.group,
                self.first + {0: 0, 3: 1}.get(slot, 2))

        def start(self):
            m = self.me
            self.send(0, (m + 2) % 4, 0)
            self.send(3, (m + 2) % 4, 1)
            self.send(1, (m + 1) % 4, 1)
            self.send(4, (m + 3) % 4, 0)

        def mid(self):
            m = self.me
            self.c[0].wait_recv()
            add_to(self.view((m + 1) % 4, 0), self.buf[0])
            self.send(2, (m + 1) % 4, 0)
            self.c[3].wait_recv()
            add_to(self.view((m + 3) % 4, 1), self.buf[3])
            self.send(5, (m + 3) % 4, 1)

        def finish(self):
            bytes_of(self.buf.at[pl.ds(0, 4)], self.group, self.first + 2).wait_recv()
            add_to(self.view(self.me, 0), self.buf[2] + self.buf[4])
            add_to(self.view(self.me, 1), self.buf[1] + self.buf[5])

    class Gather4:
        def __init__(self, view, me, ahead, behind, like, group):
            self.view, self.me, self.ahead, self.behind, self.like = view, me, ahead, behind, like
            self.group, self.first = group, slots(3)
            self.c = {}

        def send(self, slot, owner, part):
            spot = self.view(owner, part)
            self.c[slot] = send(
                spot, spot, self.ahead if slot < 3 else self.behind, self.group,
                self.first + {0: 0, 3: 1}.get(slot, 2))

        def start(self):
            self.send(0, self.me, 0)
            self.send(3, self.me, 1)
            self.send(1, self.me, 1)
            self.send(4, self.me, 0)

        def mid(self):
            self.c[0].wait_recv()
            self.send(2, (self.me + 3) % 4, 0)
            self.c[3].wait_recv()
            self.send(5, (self.me + 1) % 4, 1)

        def finish(self):
            bytes_of(self.like.at[pl.ds(0, 4)], self.group, self.first + 2).wait_recv()

    def quarter(half, part):
        return pl.ds(half * 64 + part * 32, 32)

    def along_x(ref, half):
        return lambda at, part: ref.at[at, :, quarter(half, part), :]

    def along_y(ref, half):
        return lambda at, part: ref.at[:, at, quarter(half, part), :]

    def in_x(ref, half):
        return lambda at, part: ref.at[at, y, quarter(half, part), :]

    def in_y(ref, half):
        return lambda at, part: ref.at[x, at, quarter(half, part), :]

    class Both:
        def __init__(self, *rings):
            self.rings = rings

        def start(self):
            for ring in self.rings:
                ring.start()

        def mid(self):
            for ring in self.rings:
                ring.mid()

        def finish(self):
            for ring in self.rings:
                ring.finish()

    def scatter(ref):
        return (
            Both(Scatter4(along_x(ref, 0), x, x_next, x_prev, rs_buf.at[0], 0),
                 Scatter4(along_y(ref, 1), y, y_next, y_prev, rs_buf.at[1], 0)),
            Both(Scatter4(in_y(ref, 0), y, y_next, y_prev, rs_small.at[0], 1),
                 Scatter4(in_x(ref, 1), x, x_next, x_prev, rs_small.at[1], 1)))

    def gather(ref):
        return (
            Both(Gather4(in_y(ref, 0), y, y_next, y_prev, rs_small.at[0], 2),
                 Gather4(in_x(ref, 1), x, x_next, x_prev, rs_small.at[1], 2)),
            Both(Gather4(along_x(ref, 0), x, x_next, x_prev, rs_buf.at[0], 3),
                 Gather4(along_y(ref, 1), y, y_next, y_prev, rs_buf.at[1], 3)))

    hops = (4, 3, 3, 2, 2, 1, 1)
    split = 1
    units = len(hops) * split
    back = 2 * split

    class ScatterZ:
        def __init__(self):
            self.first = slots(2 * (units - back) + 1)
            self.c = {}

        def view(self, dest, way, i):
            part = i // split % 2 ^ way
            return dc_half.at[dest, pl.ds(part * 128 + i % split * (128 // split), 128 // split), :]

        def step(self, i):
            for way in (0, 1):
                hop = hops[i // split]
                spot = self.view((me_z + (n_z - hop if way else hop)) % n_z, way, i)
                if i >= back:
                    self.c[way, i - back].wait_recv()
                    add_to(spot, z_buf[way, i - back])
                slot = self.first + min(2 * i + way, 2 * (units - back))
                self.c[way, i] = send(spot, z_buf.at[way, i], z_prev if way else z_next, 4, slot)

        def finish(self):
            last = z_buf.at[:, pl.ds(units - back, back)]
            bytes_of(last, 4, self.first + 2 * (units - back)).wait_recv()
            for i in range(units - back, units):
                for way in (0, 1):
                    add_to(self.view(me_z, way, i), z_buf[way, i])

    class GatherZ:
        def __init__(self):
            self.c = {}
            self.first, self.last = slots(2 * units), slots(1)

        def pass_on(self, spot):
            send(spot, spot, partner, 6, self.last)

        def view(self, owner, way, i):
            part = i // split % 2 ^ way
            return agw.at[core * n_z + owner, pl.ds(part * 64 + i % split * (64 // split), 64 // split), :]

        def relay(self, way, i):
            self.c[way, i].wait_recv()
            far = i // split // 2 + 1
            spot = self.view((me_z + (far if way else n_z - far)) % n_z, way, i)
            return spot

        def step(self, i):
            for way in (0, 1):
                if i >= back:
                    spot = self.relay(way, i - back)
                else:
                    spot = self.view(me_z, way, i)
                self.c[way, i] = send(
                    spot, spot, z_prev if way else z_next, 5, self.first + 2 * i + way)
                if i >= back:
                    self.pass_on(spot)

        def own(self):
            self.pass_on(agw.at[core * n_z + me_z])

        def finish(self):
            for i in range(units - back, units):
                for way in (0, 1):
                    self.pass_on(self.relay(way, i))


    step_m, step_w = 512, 512

    def first_pass(v):
        def step(i, cols):
            at = pl.ds(pl.multiple_of(i * step_m, step_m), step_m)
            glob = pl.ds(pl.multiple_of(v * clips + i * step_m, step_m), step_m)
            unit, _ = normalized(embeds[v][at, :].astype(F32))
            ub = unit.astype(BF16)
            unit_b[glob, :] = ub
            cols = list(cols)
            for k in range(protos // step_w):
                score = lax.dot_general(
                    ub, proto_b[k * step_w:(k + 1) * step_w, :],
                    (((1,), (1,)), ((), ())), preferred_element_type=F32)
                soft = jnp.exp2(score * EXPONENT)
                code = soft * soft
                table[glob, k * step_w:(k + 1) * step_w] = code
                for j in range(step_w // 128):
                    c = k * (step_w // 128) + j
                    cols[c] = cols[c] + fold8(code[:, chunk(j)])
            return tuple(cols)

        return lax.fori_loop(0, clips // step_m, step, (zero,) * lane_chunks)

    def cols_pass(v):
        def step(i, cols):
            at = pl.ds(pl.multiple_of(v * clips + i * 64, 64), 64)
            s = clip_b[at, :]
            return tuple(cols[c] + fold8(table[at, chunk(c)] * s) for c in range(lane_chunks))

        return lax.fori_loop(0, clips // 64, step, (zero,) * lane_chunks)

    def rows_pass(it, v):
        def step(i, carry):
            for j in range(2):
                block = 2 * i + j
                at = pl.ds(pl.multiple_of(v * clips + block * 128, 128), 128)
                acc = jnp.zeros((128, 128), F32)
                for c in range(lane_chunks):
                    acc = acc + table[at, chunk(c)] * scale[v, c:c + 1, :]
                row_recv[it, v, me_p, pl.ds(block, 1), :] = lane_sums(acc)
            return carry

        lax.fori_loop(0, view_blocks // 2, step, 0)
        return start_all(row_recv.at[it, v], me_p, n_p, p_id, row_send, row_sem.at[it, v])

    def wait_all(copies):
        copies.wait_recv()

    def pair_start(it, v, copies):
        wait_all(copies)
        pair = col_pair.at[it, v]
        pair[core] = total_of(col_z.at[it, v], n_z)
        copy = remote(pair.at[core], pair.at[core], colp_send, colp_sem.at[it, v], partner)
        copy.start()
        return copy

    z_copies = [None, None]
    row_copies = [None, None]
    z_cols = first_pass(0)
    pl.semaphore_wait(barrier, n_p - 1 + 2 * n_z - 1)
    z_copies[0] = put_cols(0, 0, z_cols)
    z_copies[1] = put_cols(0, 1, first_pass(1))

    def soft_totals(i, carry):
        at = pl.ds(pl.multiple_of(i * 128, 128), 128)
        acc = jnp.zeros((128, 128), F32)
        for c in range(lane_chunks):
            e = table[at, chunk(c)]
            acc = acc + e * lax.rsqrt(e)
        den_recv[me_p, pl.ds(i, 1), :] = lane_sums(acc)
        return carry

    lax.fori_loop(0, row_blocks, soft_totals, 0)
    den_copies = start_all(den_recv, me_p, n_p, p_id, small_send.at[0], small_sem.at[0])

    def transpose_unit(i, carry):
        at = pl.ds(pl.multiple_of(i * 128, 128), 128)
        unit_t[i] = unit_b[at, :].astype(F32).T.astype(BF16)
        return carry


    def grad_rows(v, first, count):
        w = 1 - v
        mine = pl.ds(pl.multiple_of(v * clips + first, count), count)
        other = pl.ds(pl.multiple_of(w * clips + first, count), count)
        soft_scale = soft_b[mine, :]
        code_scale = code_b[other, :]
        for c in range(lane_chunks):
            e = table[mine, chunk(c)]
            code = table[other, chunk(c)] * scale[w, c:c + 1, :] * code_scale
            grads[c, mine, :] = (e * lax.rsqrt(e) * soft_scale - code).astype(BF16)

    def du_rows(v, i):
        at = pl.ds(pl.multiple_of(v * clips + i * 256, 256), 256)
        mine = jnp.concatenate([grads[c, at, :] for c in range(lane_chunks)], axis=1)
        out = jnp.dot(mine, proto_b[...], preferred_element_type=F32)
        owner = v * (n_p // 2) + 2 * i
        du[owner // 4, pl.ds(owner % 4, 2)] = out.reshape(2, 128, width)

    def grad_pass(v):
        def step(i, carry):
            for j in range(4):
                grad_rows(v, i * 256 + j * 64, 64)
            return carry

        lax.fori_loop(0, clips // 256, step, 0)

    def du_dot(v):
        def step(i, carry):
            du_rows(v, i)
            return carry

        lax.fori_loop(0, clips // 256, step, 0)

    for it in range(ITERS):
        pairs = [pair_start(it, v, z_copies[v]) for v in range(2)]
        for v in range(2):
            wait_all(pairs[v])
            scale[v] = 1.0 / (protos_all * (col_pair[it, v, 0] + col_pair[it, v, 1]))
            row_copies[v] = rows_pass(it, v)
        if it == 0:
            lax.fori_loop(0, row_blocks, transpose_unit, 0)
        if it == 1:
            wait_all(den_copies)
            soft = 10.0 / total_of(den_recv, n_p)
            for v in range(2):
                spread(soft[v * view_blocks:(v + 1) * view_blocks], v, soft_b)
        for v in range(2):
            wait_all(row_copies[v])
            row_sum = total_of(row_recv.at[it, v], n_p)
            if it < ITERS - 1:
                spread(1.0 / (clips_all * row_sum), v, clip_b)
                z_copies[v] = put_cols(it + 1, v, cols_pass(v))
            else:
                spread(10.0 / row_sum, v, code_b)
                grad_pass(1 - v)
                if v == 0:
                    du_dot(1)

    def project(grad, raw):
        unit, inverse = normalized(raw)
        along = jnp.sum(unit * grad, axis=-1, keepdims=True)
        return (grad - unit * along) * inverse

    def lanes_square(block):
        sq = block * block
        return jnp.sum(sq[:, :128] + sq[:, 128:], axis=0, keepdims=True)

    theirs = (1 - core) * n_z
    pair_slot = slots(1)

    def pair_piece(i):
        return remote(
            dct.at[pl.ds(theirs + 2 * i, 2)], dc_pair.at[pl.ds(2 * i, 2)],
            out_sem.at[7], in_sem.at[pair_slot], partner)

    def dc_dot(first_chunk, sending):
        def step(i, carry):
            c = first_chunk + 2 * i
            units_t = jnp.concatenate([unit_t[j] for j in range(row_blocks)], axis=1)
            pair = jnp.concatenate([grads[c], grads[c + 1]], axis=1)
            out = jnp.dot(units_t, pair, preferred_element_type=F32)
            dct[c] = out[:, :128]
            dct[c + 1] = out[:, 128:]
            if sending:
                pair_piece(i).start()
            return carry

        lax.fori_loop(0, n_z // 2, step, 0)

    r1, r2 = scatter(du)
    g1, g2 = gather(agx)
    zs, zg = ScatterZ(), GatherZ()
    du_dot(0)
    r1.start()
    dc_dot(theirs, True)
    dc_dot(core * n_z, False)
    bytes_of(dc_pair, 7, pair_slot).wait_recv()
    for j in range(n_z):
        dc_half[j] = dct[core * n_z + j] + dc_pair[j]
    zs.step(0)
    zs.step(1)
    r1.mid()
    zs.step(2)
    zs.step(3)
    zs.step(4)
    r1.finish()
    r2.start()
    zs.step(5)
    r2.mid()
    zs.step(6)
    r2.finish()
    at = pl.ds(pl.multiple_of((me_p % view_blocks) * 128, 128), 128)
    raw = jnp.where(me_p < view_blocks, slow_ref[at, :].astype(F32), fast_ref[at, :].astype(F32))
    dx_own = project(du[x, y], raw)
    agx[x, y] = dx_own
    g1.start()
    zs.finish()
    mine = core * n_z + me_z
    dw_own = project(dc_half[me_z].T, proto_ref[pl.ds(pl.multiple_of(mine * 128, 128), 128), :])
    agw[mine] = dw_own
    zg.step(0)
    zg.step(1)
    zg.own()
    sq_p[me_p, 0:1, :] = lanes_square(dw_own)
    sq_p[me_p, 1:2, :] = lanes_square(dx_own)
    sq_p[me_p, 2:8, :] = jnp.zeros((6, 128), F32)
    sq_copies = start_all(sq_p, me_p, n_p, p_id, small_send.at[1], small_sem.at[1])
    g1.mid()
    g1.finish()
    g2.start()
    zg.step(2)
    zg.step(3)
    zg.step(4)
    wait_all(sq_copies)
    sqp_copies = sq_copies
    sq_z[batch_me] = total_of(sq_p, n_p)
    sq_copies = start_all(sq_z, batch_me, 2 * n_z, b_id, small_send.at[2], small_sem.at[2])
    zg.step(5)
    g2.mid()
    zg.step(6)
    zg.finish()
    wait_all(sq_copies)
    square = jnp.sum(total_of(sq_z, 2 * n_z), axis=1, keepdims=True)
    entries = float(protos_all * width), float(2 * clips_all * width)
    for i, out in enumerate((wf_ref, xf_ref)):
        out[...] = jnp.broadcast_to(
            lax.rsqrt(square[i:i + 1, :] / entries[i] + NORM_EPS), (8, width))
    g2.finish()
    bytes_of(dc_pair, 6, zg.last).wait_recv()
    for group, ref in enumerate((rs_buf, rs_small, rs_small, rs_buf, z_buf, z_buf, dc_pair, dc_pair)):
        bytes_of(ref, group, 0).wait_send()
    for ref, sem in (
        (col_z.at[:, :, pl.ds(0, n_z - 1)], col_send),
        (col_pair.at[:, :, 0], colp_send),
        (row_recv.at[:, :, pl.ds(0, n_p - 1)], row_send),
    ):
        remote(ref, ref, sem, in_sem.at[0], partner).wait_send()
    for copies in (den_copies, sqp_copies, sq_copies):
        copies.wait_send()


def body(slow_embed, fast_embed, prototypes):
    clips, width = slow_embed.shape
    protos = prototypes.shape[0]
    n_b = lax.axis_size("batch")
    n_p = lax.axis_size("proto")
    n_z = n_b // 2
    rows = 2 * clips
    DMA = pltpu.SemaphoreType.DMA
    vmem = pltpu.VMEM
    lane_chunks = protos // 128
    row_blocks = rows // 128
    scratch = [
        vmem((rows, protos), F32),
        vmem((lane_chunks, rows, 128), BF16),
        vmem((rows, width), BF16),
        vmem((row_blocks, width, 128), BF16),
        vmem((protos, width), BF16),
        vmem((2, lane_chunks, 128), F32),
        vmem((rows, 128), F32),
        vmem((rows, 128), F32),
        vmem((rows, 128), F32),
        vmem((4, 4, 128, width), F32),
        vmem((lane_chunks, width, 128), F32),
        vmem((n_z, width, 128), F32),
        vmem((n_z, width, 128), F32),
        vmem((2, 6, 4, 32, width), F32),
        vmem((2, 6, 32, width), F32),
        vmem((2, 7, 128, 128), F32),
        vmem((ITERS, 2, n_z, lane_chunks, 128), F32),
        vmem((ITERS, 2, 2, lane_chunks, 128), F32),
        vmem((ITERS, 2, n_p, row_blocks // 2, 128), F32),
        vmem((n_p, row_blocks, 128), F32),
        vmem((n_p, 8, 128), F32),
        vmem((n_b, 8, 128), F32),
        DMA(()), DMA((ITERS, 2)), DMA(()), DMA((ITERS, 2)), DMA(()), DMA((ITERS, 2)),
        DMA((3,)), DMA((3,)), DMA((8,)), DMA((COPIES,)),
    ]
    whole = pl.BlockSpec(memory_space=pltpu.VMEM)
    dw, dx, dw_factor, dx_factor = pl.pallas_call(
        functools.partial(kernel, (clips, protos, width, n_z, n_p)),
        out_shape=(
            vmem((lane_chunks, 128, width), F32),
            vmem((4, 4, 128, width), F32),
            vmem((8, width), F32),
            vmem((8, width), F32),
        ),
        in_specs=[whole] * 3,
        out_specs=(whole,) * 4,
        scratch_shapes=scratch,
        compiler_params=pltpu.CompilerParams(
            collective_id=0, has_side_effects=True, vmem_limit_bytes=56 * 2**20),
        name="swav",
    )(slow_embed, fast_embed, prototypes)

    def scaled(array, factor, rows):
        return (array.reshape(rows // 8, 8, width) * factor).reshape(rows, width)

    return (
        scaled(dw, dw_factor, protos),
        scaled(dx[:2], dx_factor, clips),
        scaled(dx[2:], dx_factor, clips),
    )


def solution(mesh):
    placed = (P("batch", None), P("batch", None), P("proto", None))
    return jax.shard_map(
        body,
        mesh=mesh,
        in_specs=placed,
        out_specs=(P("proto", None), P("batch", None), P("batch", None)),
        check_vma=False,
    )
```

```python
import functools

import jax
import jax.numpy as jnp
from jax import lax
from jax.experimental import pallas as pl
from jax.experimental.pallas import tpu as pltpu
from jax.sharding import PartitionSpec as P

ITERS = 3
COPIES = 51
EXPONENT = 10.0 * 1.4426950408889634
NORM_EPS = 1e-06
MESH = pl.DeviceIdType.MESH
F32 = jnp.float32
BF16 = jnp.bfloat16


def normalized(rows):
    total = jnp.sum(rows * rows, axis=-1, keepdims=True) + 1e-12
    inverse = 1.0 / jnp.sqrt(total)
    return rows * inverse, inverse


def fold8(block):
    rows, lanes = block.shape
    return jnp.sum(block.reshape(rows // 8, 8, lanes), axis=0)


def kernel(
    dims,
    slow_ref, fast_ref, proto_ref,
    agw, agx, wf_ref, xf_ref,
    table, grads, unit_b, unit_t, proto_b, scale, clip_b, soft_b, code_b,
    du, dct, dc_pair, dc_half, rs_buf, rs_small, z_buf,
    col_z, col_pair, row_recv, den_recv, sq_p, sq_z,
    col_send, col_sem, colp_send, colp_sem, row_send, row_sem, small_send, small_sem,
    out_sem, in_sem,
):
    clips, protos, width, n_z, n_p = dims
    batch_me = lax.axis_index("batch")
    me_p = lax.axis_index("proto")
    me_z = batch_me // 2
    core = batch_me % 2
    clips_all = clips * 2 * n_z
    protos_all = protos * n_p
    rows = 2 * clips
    lane_chunks = protos // 128
    row_blocks = rows // 128
    view_blocks = clips // 128
    embeds = (slow_ref, fast_ref)

    def p_id(d):
        return {"proto": (me_p // 4 + d // 4) % 4 * 4 + (me_p + d) % 4}

    def p_hops(d):
        return min(d // 4, 4 - d // 4) + min(d % 4, 4 - d % 4)

    def z_hops(d):
        return min(d, n_z - d)

    def z_id(d):
        return {"batch": ((me_z + d) % n_z) * 2 + core}

    def b_id(d):
        return {"batch": (batch_me + d) % (2 * n_z)}

    partner = {"batch": me_z * 2 + 1 - core}

    def remote(src, dst, send, recv, device):
        return pltpu.make_async_remote_copy(
            src_ref=src, dst_ref=dst, send_sem=send, recv_sem=recv,
            device_id=device, device_id_type=MESH,
        )

    barrier = pltpu.get_barrier_semaphore()
    for d in range(1, n_p):
        pl.semaphore_signal(barrier, inc=1, device_id=p_id(d), device_id_type=MESH)
    for d in range(1, 2 * n_z):
        pl.semaphore_signal(barrier, inc=1, device_id=b_id(d), device_id_type=MESH)

    def proto_norm(i, carry):
        at = pl.ds(pl.multiple_of(i * 512, 512), 512)
        unit, _ = normalized(proto_ref[at, :])
        proto_b[at, :] = unit.astype(BF16)
        return carry

    lax.fori_loop(0, protos // 512, proto_norm, 0)

    def chunk(c):
        return slice(c * 128, (c + 1) * 128)

    def total_of(ref, count):
        acc = ref[0]
        for i in range(1, count):
            acc = acc + ref[i]
        return acc

    def start_all(ref, me, count, ids, send, recv):
        hops_to = {p_id: p_hops, z_id: z_hops}.get(ids, lambda d: z_hops(d // 2))
        for d in sorted(range(1, count), key=hops_to, reverse=True):
            remote(ref.at[me], ref.at[me], send, recv, ids(d)).start()
        others = ref.at[pl.ds(0, count - 1)]
        return remote(others, others, send, recv, ids(1))

    zero = jnp.zeros((8, 128), F32)

    def put_cols(it, v, cols):
        for c in range(lane_chunks):
            col_z[it, v, me_z, c:c + 1, :] = jnp.sum(cols[c], axis=0, keepdims=True)
        return start_all(col_z.at[it, v], me_z, n_z, z_id, col_send, col_sem.at[it, v])

    def lane_sums(block):
        return jnp.sum(block.T, axis=0, keepdims=True)

    def spread(values, v, target):
        for i in range(view_blocks):
            at = slice(v * clips + i * 128, v * clips + (i + 1) * 128)
            target[at, :] = jnp.broadcast_to(values[i:i + 1, :], (128, 128)).T

    counter = [0]

    def slots(n):
        counter[0] += n
        return counter[0] - n

    def send(src, dst, device, group, slot):
        copy = remote(src, dst, out_sem.at[group], in_sem.at[slot], device)
        copy.start()
        return copy

    def bytes_of(ref, group, slot):
        return remote(ref, ref, out_sem.at[group], in_sem.at[slot], partner)

    def add_to(ref, value):
        ref[...] = ref[...] + value

    x, y = me_p // 4, me_p % 4
    x_next = {"proto": (x + 1) % 4 * 4 + y}
    x_prev = {"proto": (x + 3) % 4 * 4 + y}
    y_next = {"proto": x * 4 + (y + 1) % 4}
    y_prev = {"proto": x * 4 + (y + 3) % 4}
    z_next, z_prev = z_id(1), z_id(n_z - 1)

    class Scatter4:
        def __init__(self, view, me, ahead, behind, buf, group):
            self.view, self.me, self.ahead, self.behind, self.buf = view, me, ahead, behind, buf
            self.group, self.first = group, slots(3)
            self.c = {}

        def send(self, slot, dest, part):
            device = self.ahead if slot < 3 else self.behind
            self.c[slot] = send(
                self.view(dest, part), self.buf.at[slot], device, self.group,
                self.first + {0: 0, 3: 1}.get(slot, 2))

        def start(self):
            m = self.me
            self.send(0, (m + 2) % 4, 0)
            self.send(3, (m + 2) % 4, 1)
            self.send(1, (m + 1) % 4, 1)
            self.send(4, (m + 3) % 4, 0)

        def mid(self):
            m = self.me
            self.c[0].wait_recv()
            add_to(self.view((m + 1) % 4, 0), self.buf[0])
            self.send(2, (m + 1) % 4, 0)
            self.c[3].wait_recv()
            add_to(self.view((m + 3) % 4, 1), self.buf[3])
            self.send(5, (m + 3) % 4, 1)

        def finish(self):
            bytes_of(self.buf.at[pl.ds(0, 4)], self.group, self.first + 2).wait_recv()
            add_to(self.view(self.me, 0), self.buf[2] + self.buf[4])
            add_to(self.view(self.me, 1), self.buf[1] + self.buf[5])

    class Gather4:
        def __init__(self, view, me, ahead, behind, like, group):
            self.view, self.me, self.ahead, self.behind, self.like = view, me, ahead, behind, like
            self.group, self.first = group, slots(3)
            self.c = {}

        def send(self, slot, owner, part):
            spot = self.view(owner, part)
            self.c[slot] = send(
                spot, spot, self.ahead if slot < 3 else self.behind, self.group,
                self.first + {0: 0, 3: 1}.get(slot, 2))

        def start(self):
            self.send(0, self.me, 0)
            self.send(3, self.me, 1)
            self.send(1, self.me, 1)
            self.send(4, self.me, 0)

        def mid(self):
            self.c[0].wait_recv()
            self.send(2, (self.me + 3) % 4, 0)
            self.c[3].wait_recv()
            self.send(5, (self.me + 1) % 4, 1)

        def finish(self):
            bytes_of(self.like.at[pl.ds(0, 4)], self.group, self.first + 2).wait_recv()

    def quarter(half, part):
        return pl.ds(half * 64 + part * 32, 32)

    def along_x(ref, half):
        return lambda at, part: ref.at[at, :, quarter(half, part), :]

    def along_y(ref, half):
        return lambda at, part: ref.at[:, at, quarter(half, part), :]

    def in_x(ref, half):
        return lambda at, part: ref.at[at, y, quarter(half, part), :]

    def in_y(ref, half):
        return lambda at, part: ref.at[x, at, quarter(half, part), :]

    class Both:
        def __init__(self, *rings):
            self.rings = rings

        def start(self):
            for ring in self.rings:
                ring.start()

        def mid(self):
            for ring in self.rings:
                ring.mid()

        def finish(self):
            for ring in self.rings:
                ring.finish()

    def scatter(ref):
        return (
            Both(Scatter4(along_x(ref, 0), x, x_next, x_prev, rs_buf.at[0], 0),
                 Scatter4(along_y(ref, 1), y, y_next, y_prev, rs_buf.at[1], 0)),
            Both(Scatter4(in_y(ref, 0), y, y_next, y_prev, rs_small.at[0], 1),
                 Scatter4(in_x(ref, 1), x, x_next, x_prev, rs_small.at[1], 1)))

    def gather(ref):
        return (
            Both(Gather4(in_y(ref, 0), y, y_next, y_prev, rs_small.at[0], 2),
                 Gather4(in_x(ref, 1), x, x_next, x_prev, rs_small.at[1], 2)),
            Both(Gather4(along_x(ref, 0), x, x_next, x_prev, rs_buf.at[0], 3),
                 Gather4(along_y(ref, 1), y, y_next, y_prev, rs_buf.at[1], 3)))

    hops = (4, 3, 3, 2, 2, 1, 1)
    split = 1
    units = len(hops) * split
    back = 2 * split

    class ScatterZ:
        def __init__(self):
            self.first = slots(2 * (units - back) + 1)
            self.c = {}

        def view(self, dest, way, i):
            part = i // split % 2 ^ way
            return dc_half.at[dest, pl.ds(part * 128 + i % split * (128 // split), 128 // split), :]

        def step(self, i):
            for way in (0, 1):
                hop = hops[i // split]
                spot = self.view((me_z + (n_z - hop if way else hop)) % n_z, way, i)
                if i >= back:
                    self.c[way, i - back].wait_recv()
                    add_to(spot, z_buf[way, i - back])
                slot = self.first + min(2 * i + way, 2 * (units - back))
                self.c[way, i] = send(spot, z_buf.at[way, i], z_prev if way else z_next, 4, slot)

        def finish(self):
            last = z_buf.at[:, pl.ds(units - back, back)]
            bytes_of(last, 4, self.first + 2 * (units - back)).wait_recv()
            for i in range(units - back, units):
                for way in (0, 1):
                    add_to(self.view(me_z, way, i), z_buf[way, i])

    class GatherZ:
        def __init__(self):
            self.c = {}
            self.first, self.last = slots(2 * units), slots(1)

        def pass_on(self, spot):
            send(spot, spot, partner, 6, self.last)

        def view(self, owner, way, i):
            part = i // split % 2 ^ way
            return agw.at[core * n_z + owner, pl.ds(part * 64 + i % split * (64 // split), 64 // split), :]

        def relay(self, way, i):
            self.c[way, i].wait_recv()
            far = i // split // 2 + 1
            spot = self.view((me_z + (far if way else n_z - far)) % n_z, way, i)
            return spot

        def step(self, i):
            for way in (0, 1):
                if i >= back:
                    spot = self.relay(way, i - back)
                else:
                    spot = self.view(me_z, way, i)
                self.c[way, i] = send(
                    spot, spot, z_prev if way else z_next, 5, self.first + 2 * i + way)
                if i >= back:
                    self.pass_on(spot)

        def own(self):
            self.pass_on(agw.at[core * n_z + me_z])

        def finish(self):
            for i in range(units - back, units):
                for way in (0, 1):
                    self.pass_on(self.relay(way, i))


    step_m, step_w = 512, 512

    def first_pass(v):
        def step(i, cols):
            at = pl.ds(pl.multiple_of(i * step_m, step_m), step_m)
            glob = pl.ds(pl.multiple_of(v * clips + i * step_m, step_m), step_m)
            unit, _ = normalized(embeds[v][at, :].astype(F32))
            ub = unit.astype(BF16)
            unit_b[glob, :] = ub
            cols = list(cols)
            for k in range(protos // step_w):
                score = lax.dot_general(
                    ub, proto_b[k * step_w:(k + 1) * step_w, :],
                    (((1,), (1,)), ((), ())), preferred_element_type=F32)
                soft = jnp.exp2(score * EXPONENT)
                code = soft * soft
                table[glob, k * step_w:(k + 1) * step_w] = code
                for j in range(step_w // 128):
                    c = k * (step_w // 128) + j
                    cols[c] = cols[c] + fold8(code[:, chunk(j)])
            return tuple(cols)

        return lax.fori_loop(0, clips // step_m, step, (zero,) * lane_chunks)

    def cols_pass(v):
        def step(i, cols):
            at = pl.ds(pl.multiple_of(v * clips + i * 64, 64), 64)
            s = clip_b[at, :]
            return tuple(cols[c] + fold8(table[at, chunk(c)] * s) for c in range(lane_chunks))

        return lax.fori_loop(0, clips // 64, step, (zero,) * lane_chunks)

    def rows_pass(it, v):
        def step(i, carry):
            for j in range(2):
                block = 2 * i + j
                at = pl.ds(pl.multiple_of(v * clips + block * 128, 128), 128)
                acc = jnp.zeros((128, 128), F32)
                for c in range(lane_chunks):
                    acc = acc + table[at, chunk(c)] * scale[v, c:c + 1, :]
                row_recv[it, v, me_p, pl.ds(block, 1), :] = lane_sums(acc)
            return carry

        lax.fori_loop(0, view_blocks // 2, step, 0)
        return start_all(row_recv.at[it, v], me_p, n_p, p_id, row_send, row_sem.at[it, v])

    def wait_all(copies):
        copies.wait_recv()

    def pair_start(it, v, copies):
        wait_all(copies)
        pair = col_pair.at[it, v]
        pair[core] = total_of(col_z.at[it, v], n_z)
        copy = remote(pair.at[core], pair.at[core], colp_send, colp_sem.at[it, v], partner)
        copy.start()
        return copy

    z_copies = [None, None]
    row_copies = [None, None]
    z_cols = first_pass(0)
    pl.semaphore_wait(barrier, n_p - 1 + 2 * n_z - 1)
    z_copies[0] = put_cols(0, 0, z_cols)
    z_copies[1] = put_cols(0, 1, first_pass(1))

    def soft_totals(i, carry):
        at = pl.ds(pl.multiple_of(i * 128, 128), 128)
        acc = jnp.zeros((128, 128), F32)
        for c in range(lane_chunks):
            e = table[at, chunk(c)]
            acc = acc + e * lax.rsqrt(e)
        den_recv[me_p, pl.ds(i, 1), :] = lane_sums(acc)
        return carry

    lax.fori_loop(0, row_blocks, soft_totals, 0)
    den_copies = start_all(den_recv, me_p, n_p, p_id, small_send.at[0], small_sem.at[0])

    def transpose_unit(i, carry):
        at = pl.ds(pl.multiple_of(i * 128, 128), 128)
        unit_t[i] = unit_b[at, :].astype(F32).T.astype(BF16)
        return carry


    def grad_rows(v, first, count):
        w = 1 - v
        mine = pl.ds(pl.multiple_of(v * clips + first, count), count)
        other = pl.ds(pl.multiple_of(w * clips + first, count), count)
        soft_scale = soft_b[mine, :]
        code_scale = code_b[other, :]
        for c in range(lane_chunks):
            e = table[mine, chunk(c)]
            code = table[other, chunk(c)] * scale[w, c:c + 1, :] * code_scale
            grads[c, mine, :] = (e * lax.rsqrt(e) * soft_scale - code).astype(BF16)

    def du_rows(v, i):
        at = pl.ds(pl.multiple_of(v * clips + i * 256, 256), 256)
        mine = jnp.concatenate([grads[c, at, :] for c in range(lane_chunks)], axis=1)
        out = jnp.dot(mine, proto_b[...], preferred_element_type=F32)
        owner = v * (n_p // 2) + 2 * i
        du[owner // 4, pl.ds(owner % 4, 2)] = out.reshape(2, 128, width)

    def grad_pass(v):
        def step(i, carry):
            for j in range(4):
                grad_rows(v, i * 256 + j * 64, 64)
            return carry

        lax.fori_loop(0, clips // 256, step, 0)

    def du_dot(v):
        def step(i, carry):
            du_rows(v, i)
            return carry

        lax.fori_loop(0, clips // 256, step, 0)

    for it in range(ITERS):
        pairs = [pair_start(it, v, z_copies[v]) for v in range(2)]
        for v in range(2):
            wait_all(pairs[v])
            scale[v] = 1.0 / (protos_all * (col_pair[it, v, 0] + col_pair[it, v, 1]))
            row_copies[v] = rows_pass(it, v)
        if it == 0:
            lax.fori_loop(0, row_blocks, transpose_unit, 0)
        if it == 1:
            wait_all(den_copies)
            soft = 10.0 / total_of(den_recv, n_p)
            for v in range(2):
                spread(soft[v * view_blocks:(v + 1) * view_blocks], v, soft_b)
        for v in range(2):
            wait_all(row_copies[v])
            row_sum = total_of(row_recv.at[it, v], n_p)
            if it < ITERS - 1:
                spread(1.0 / (clips_all * row_sum), v, clip_b)
                z_copies[v] = put_cols(it + 1, v, cols_pass(v))
            else:
                spread(10.0 / row_sum, v, code_b)
                grad_pass(1 - v)
                if v == 0:
                    du_dot(1)

    def project(grad, raw):
        unit, inverse = normalized(raw)
        along = jnp.sum(unit * grad, axis=-1, keepdims=True)
        return (grad - unit * along) * inverse

    def lanes_square(block):
        sq = block * block
        return jnp.sum(sq[:, :128] + sq[:, 128:], axis=0, keepdims=True)

    theirs = (1 - core) * n_z
    pair_slot = slots(1)

    def pair_piece(i):
        return remote(
            dct.at[pl.ds(theirs + 2 * i, 2)], dc_pair.at[pl.ds(2 * i, 2)],
            out_sem.at[7], in_sem.at[pair_slot], partner)

    def dc_dot(first_chunk, sending):
        def step(i, carry):
            c = first_chunk + 2 * i
            units_t = jnp.concatenate([unit_t[j] for j in range(row_blocks)], axis=1)
            pair = jnp.concatenate([grads[c], grads[c + 1]], axis=1)
            out = jnp.dot(units_t, pair, preferred_element_type=F32)
            dct[c] = out[:, :128]
            dct[c + 1] = out[:, 128:]
            if sending:
                pair_piece(i).start()
            return carry

        lax.fori_loop(0, n_z // 2, step, 0)

    r1, r2 = scatter(du)
    g1, g2 = gather(agx)
    zs, zg = ScatterZ(), GatherZ()
    du_dot(0)
    r1.start()
    dc_dot(theirs, True)
    dc_dot(core * n_z, False)
    bytes_of(dc_pair, 7, pair_slot).wait_recv()
    for j in range(n_z):
        dc_half[j] = dct[core * n_z + j] + dc_pair[j]
    zs.step(0)
    zs.step(1)
    r1.mid()
    zs.step(2)
    zs.step(3)
    zs.step(4)
    zs.step(5)
    r1.finish()
    r2.start()
    zs.step(6)
    r2.mid()
    r2.finish()
    at = pl.ds(pl.multiple_of((me_p % view_blocks) * 128, 128), 128)
    raw = jnp.where(me_p < view_blocks, slow_ref[at, :].astype(F32), fast_ref[at, :].astype(F32))
    dx_own = project(du[x, y], raw)
    agx[x, y] = dx_own
    g1.start()
    zs.finish()
    mine = core * n_z + me_z
    dw_own = project(dc_half[me_z].T, proto_ref[pl.ds(pl.multiple_of(mine * 128, 128), 128), :])
    agw[mine] = dw_own
    zg.step(0)
    zg.step(1)
    zg.own()
    sq_p[me_p, 0:1, :] = lanes_square(dw_own)
    sq_p[me_p, 1:2, :] = lanes_square(dx_own)
    sq_p[me_p, 2:8, :] = jnp.zeros((6, 128), F32)
    sq_copies = start_all(sq_p, me_p, n_p, p_id, small_send.at[1], small_sem.at[1])
    g1.mid()
    zg.step(2)
    g1.finish()
    g2.start()
    zg.step(3)
    zg.step(4)
    wait_all(sq_copies)
    sqp_copies = sq_copies
    sq_z[batch_me] = total_of(sq_p, n_p)
    sq_copies = start_all(sq_z, batch_me, 2 * n_z, b_id, small_send.at[2], small_sem.at[2])
    zg.step(5)
    g2.mid()
    zg.step(6)
    zg.finish()
    wait_all(sq_copies)
    square = jnp.sum(total_of(sq_z, 2 * n_z), axis=1, keepdims=True)
    entries = float(protos_all * width), float(2 * clips_all * width)
    for i, out in enumerate((wf_ref, xf_ref)):
        out[...] = jnp.broadcast_to(
            lax.rsqrt(square[i:i + 1, :] / entries[i] + NORM_EPS), (8, width))
    g2.finish()
    bytes_of(dc_pair, 6, zg.last).wait_recv()
    for group, ref in enumerate((rs_buf, rs_small, rs_small, rs_buf, z_buf, z_buf, dc_pair, dc_pair)):
        bytes_of(ref, group, 0).wait_send()
    for ref, sem in (
        (col_z.at[:, :, pl.ds(0, n_z - 1)], col_send),
        (col_pair.at[:, :, 0], colp_send),
        (row_recv.at[:, :, pl.ds(0, n_p - 1)], row_send),
    ):
        remote(ref, ref, sem, in_sem.at[0], partner).wait_send()
    for copies in (den_copies, sqp_copies, sq_copies):
        copies.wait_send()


def body(slow_embed, fast_embed, prototypes):
    clips, width = slow_embed.shape
    protos = prototypes.shape[0]
    n_b = lax.axis_size("batch")
    n_p = lax.axis_size("proto")
    n_z = n_b // 2
    rows = 2 * clips
    DMA = pltpu.SemaphoreType.DMA
    vmem = pltpu.VMEM
    lane_chunks = protos // 128
    row_blocks = rows // 128
    scratch = [
        vmem((rows, protos), F32),
        vmem((lane_chunks, rows, 128), BF16),
        vmem((rows, width), BF16),
        vmem((row_blocks, width, 128), BF16),
        vmem((protos, width), BF16),
        vmem((2, lane_chunks, 128), F32),
        vmem((rows, 128), F32),
        vmem((rows, 128), F32),
        vmem((rows, 128), F32),
        vmem((4, 4, 128, width), F32),
        vmem((lane_chunks, width, 128), F32),
        vmem((n_z, width, 128), F32),
        vmem((n_z, width, 128), F32),
        vmem((2, 6, 4, 32, width), F32),
        vmem((2, 6, 32, width), F32),
        vmem((2, 7, 128, 128), F32),
        vmem((ITERS, 2, n_z, lane_chunks, 128), F32),
        vmem((ITERS, 2, 2, lane_chunks, 128), F32),
        vmem((ITERS, 2, n_p, row_blocks // 2, 128), F32),
        vmem((n_p, row_blocks, 128), F32),
        vmem((n_p, 8, 128), F32),
        vmem((n_b, 8, 128), F32),
        DMA(()), DMA((ITERS, 2)), DMA(()), DMA((ITERS, 2)), DMA(()), DMA((ITERS, 2)),
        DMA((3,)), DMA((3,)), DMA((8,)), DMA((COPIES,)),
    ]
    whole = pl.BlockSpec(memory_space=pltpu.VMEM)
    dw, dx, dw_factor, dx_factor = pl.pallas_call(
        functools.partial(kernel, (clips, protos, width, n_z, n_p)),
        out_shape=(
            vmem((lane_chunks, 128, width), F32),
            vmem((4, 4, 128, width), F32),
            vmem((8, width), F32),
            vmem((8, width), F32),
        ),
        in_specs=[whole] * 3,
        out_specs=(whole,) * 4,
        scratch_shapes=scratch,
        compiler_params=pltpu.CompilerParams(
            collective_id=0, has_side_effects=True, vmem_limit_bytes=56 * 2**20),
        name="swav",
    )(slow_embed, fast_embed, prototypes)

    def scaled(array, factor, rows):
        return (array.reshape(rows // 8, 8, width) * factor).reshape(rows, width)

    return (
        scaled(dw, dw_factor, protos),
        scaled(dx[:2], dx_factor, clips),
        scaled(dx[2:], dx_factor, clips),
    )


def solution(mesh):
    placed = (P("batch", None), P("batch", None), P("proto", None))
    return jax.shard_map(
        body,
        mesh=mesh,
        in_specs=placed,
        out_specs=(P("proto", None), P("batch", None), P("batch", None)),
        check_vma=False,
    )
```
